128 devices in a mesh: group: 4 (over x), cluster: 32 (over z, y, core).
Axes of the slice: x: 4, y: 4, z: 4, core: 2. Of those that a mesh axis runs over, the one named last changes fastest.
Arguments:
- charges: float32 [1048576, 128], P(('group', 'cluster')), may hold values from -6 to 6
- leaf_size: int32 [4096], P(('group', 'cluster')), may hold values from 1 to 256, 786432 in all
- leaf_basis: float32 [4096, 64, 256], P(('group', 'cluster')), may hold values from -0.375 to 0.375
- leaf_transfer: float32 [4096, 64, 64], P(('group', 'cluster')), may hold values from -0.375 to 0.375
- mid_transfer: float32 [1024, 64, 64], P(('group', 'cluster')), may hold values from -0.25 to 0.25
- leaf_parent: int32 [4096], P(('group', 'cluster')), may hold values from 0 to 7, as said below
- send_leaf: int32 [32768], P(('group', 'cluster')), may hold values from 0 to 32, as said below
- pair_leaf: int32 [4096, 12], P(('group', 'cluster')), may hold values from 0 to 256, as said below
- leaf_coupling: float32 [4096, 64, 768], P(('group', 'cluster')), may hold values from -0.21875 to 0.21875
- send_mid: int32 [32768], P(('group', 'cluster')), may hold values from 0 to 8, as said below
- pair_mid: int32 [1024, 32], P(('group', 'cluster')), may hold values from 0 to 256, as said below
- mid_coupling: float32 [1024, 64, 2048], P(('group', 'cluster')), may hold values from -0.125 to 0.125
- top_pairs: int32 [128, 4], P('group'), may hold values from 0 to 128, as said below
- top_coupling: float32 [128, 64, 256], P('group'), may hold values from -0.375 to 0.375
Outputs:
- far_field: float32 [1048576, 128], P(('group', 'cluster'))
The draws below stay inside these ranges and needn't reach their ends.
Inputs may be any that keep to these rules, and one draw needn't show every extreme that they name: `send_leaf`: entry (d * 128 + r) * 2 + j is the leaf, local to device d, whose block d puts in slot j for device r, or 32 for an empty slot; the leaves in one sender's slots to one receiver are distinct; some receiver has every slot from every sender filled. `pair_leaf`: row t names leaf t's admissible partners as positions 2 * d + j among the slots its owner receives, filled slots only and distinct within a row, or 256 for no partner; every filled slot is named by some row of its receiver. `send_mid`: as send_leaf, for level-one clusters: local indices below 8, 8 for an empty slot; some receiver has every slot from every sender filled. `pair_mid`: as pair_leaf, for level-one clusters; every filled slot is named by some row of its receiver. `leaf_parent`: every level-one cluster of a device is the parent of at least one of its leaves. `top_pairs`: row o names coarse clusters other than o, distinct within a row, at least one a row, or 128 for no partner.
All inputs are finite; a program needn't handle non-finite values. No bound on the sum of `leaf_size` on one device may be relied on, other than what follows from the above.
Results may differ from the reference program's by a relative error of at most 0.000062.
Values sent between devices are 32-bit elements; how exact they have to be, the bound alone decides.
A program may use at most 128 MiB of HBM per device.

```python
import math
import jax
import jax.numpy as jnp
import numpy as np
from jax import lax

PORTS = 128
RANK = 64
LEAF = 256
SLOTS = 2
LIST_LEAF = 12
LIST_MID = 32
LIST_TOP = 4
LEAVES_DEV = 32
MIDS_DEV = 8
OWNERS = 128
LEAVES = 4096
MIDS = 1024
COARSE = 128
UNKNOWNS = 1048576


def distinct_order(key, row_count, width):
    scores = jax.random.randint(key, (row_count, width), 0, 1 << 20) * width + jnp.arange(width, dtype=jnp.int32)[None, :]
    return jnp.argsort(scores, axis=1).astype(jnp.int32)


def routing_plan(key, per_owner, listed):
    streams = jax.random.split(key, 6)
    heavy_row = jax.random.randint(streams[0], (OWNERS, 1), 0, 2)
    counts = jax.random.randint(streams[1], (OWNERS, OWNERS), 0, SLOTS // 2 + 1) + heavy_row * (SLOTS - SLOTS // 2)
    full_row = jax.random.randint(streams[2], (), 0, OWNERS)
    counts = jnp.where(jnp.arange(OWNERS, dtype=jnp.int32)[:, None] == full_row, SLOTS, counts)
    ordering = distinct_order(streams[3], OWNERS * OWNERS, per_owner).reshape(OWNERS, OWNERS, per_owner)
    chosen = ordering[:, :, :SLOTS]
    slot_ids = jnp.arange(SLOTS, dtype=jnp.int32)
    is_live = slot_ids[None, None, :] < counts[:, :, None]
    send_table = jnp.where(is_live, chosen, per_owner)
    send_table = jnp.transpose(send_table, (1, 0, 2)).reshape(-1).astype(jnp.int32)
    flat_live = is_live.reshape(OWNERS, OWNERS * SLOTS)
    position = jnp.arange(OWNERS * SLOTS, dtype=jnp.int32)
    sort_value = jnp.where(flat_live, 0, 1) * (OWNERS * SLOTS) + position[None, :]
    live_list = jnp.argsort(sort_value, axis=1).astype(jnp.int32)
    live_total = jnp.sum(flat_live.astype(jnp.int32), axis=1)
    need_each = (live_total + per_owner - 1) // per_owner
    low_fill = jnp.minimum(need_each, listed)
    drawn_fill = jax.random.randint(streams[4], (OWNERS, per_owner), 0, listed + 1)
    filled = jnp.minimum(jnp.maximum(drawn_fill, low_fill[:, None]), jnp.minimum(live_total, listed)[:, None])
    first_spot = jnp.cumsum(filled, axis=1) - filled
    rotation = jax.random.randint(streams[5], (OWNERS, 1, 1), 0, OWNERS * SLOTS)
    column = jnp.arange(listed, dtype=jnp.int32)
    spot_index = first_spot[:, :, None] + column[None, None, :] + rotation
    safe_total = jnp.maximum(live_total, 1)
    wrapped = (spot_index % safe_total[:, None, None]).reshape(OWNERS, per_owner * listed)
    picked = jnp.take_along_axis(live_list, wrapped, axis=1).reshape(OWNERS, per_owner, listed)
    pair_table = jnp.where(column[None, None, :] < filled[:, :, None], picked, OWNERS * SLOTS)
    return (send_table, pair_table.reshape(OWNERS * per_owner, listed).astype(jnp.int32))


def draw_send_leaf(key, part):
    return routing_plan(jax.random.fold_in(key, 11), LEAVES_DEV, LIST_LEAF)[0]


def draw_pair_leaf(key, part):
    return routing_plan(jax.random.fold_in(key, 11), LEAVES_DEV, LIST_LEAF)[1]


def draw_send_mid(key, part):
    return routing_plan(jax.random.fold_in(key, 12), MIDS_DEV, LIST_MID)[0]


def draw_pair_mid(key, part):
    return routing_plan(jax.random.fold_in(key, 12), MIDS_DEV, LIST_MID)[1]


def draw_leaf_parent(key, part):
    streams = jax.random.split(jax.random.fold_in(key, 13), 2)
    local_index = jnp.arange(LEAVES_DEV, dtype=jnp.int32)
    spare_parent = jax.random.randint(streams[0], (OWNERS, LEAVES_DEV), 0, MIDS_DEV)
    base_parent = jnp.where(local_index[None, :] < MIDS_DEV, local_index[None, :], spare_parent)
    ordering = distinct_order(streams[1], OWNERS, LEAVES_DEV)
    return jnp.take_along_axis(base_parent, ordering, axis=1).reshape(-1).astype(jnp.int32)


def draw_top_pairs(key, part):
    streams = jax.random.split(jax.random.fold_in(key, 14), 3)
    ordering = distinct_order(streams[0], COARSE, COARSE - 1)[:, :LIST_TOP]
    target = jnp.arange(COARSE, dtype=jnp.int32)[:, None]
    sources = (target + 1 + ordering) % COARSE
    filled = jax.random.randint(streams[1], (COARSE, 1), 1, LIST_TOP + 1)
    full_row = jax.random.randint(streams[2], (), 0, COARSE)
    filled = jnp.where(target == full_row, LIST_TOP, filled)
    column = jnp.arange(LIST_TOP, dtype=jnp.int32)[None, :]
    return jnp.where(column < filled, sources, COARSE).astype(jnp.int32)


def level_of(key, extent, cuts, smallest, top_value):
    def one(dim, shards_of):
        draws = jax.random.uniform(jax.random.fold_in(jax.random.fold_in(key, 6), dim), (shards_of,), jnp.float32, smallest / len(cuts), top_value / len(cuts))
        return jnp.repeat(jnp.exp(draws), extent[dim] // shards_of).reshape((-1,) + (1,) * (len(extent) - dim - 1))

    gain = one(*cuts[0])
    for cut in cuts[1:]:
        gain = gain * one(*cut)
    return gain


def split_up(amount, total, bound, skew):
    loads = [(1 << 20) // math.isqrt(standing ** skew) + 1 for standing in range(2, amount + 1)]
    surplus, holding = total - bound - (amount - 1), [1] * (amount - 1)
    while surplus > 0:
        free = [i for i in range(amount - 1) if holding[i] < bound]
        pool, left = sum([loads[i] for i in free]), surplus
        for i in free:
            extra = min(bound - holding[i], max(1, left * loads[i] // pool), surplus)
            holding[i] = holding[i] + extra
            surplus = surplus - extra
    return np.array([bound] + holding)


def uneven_parts(own_key, number_of, total, limit, skew):
    if number_of == 2:
        one = jax.random.randint(own_key, (), max(1, total - limit), min(limit, total - 1) + 1)
        return jnp.stack([one, total - one])
    tallies = jnp.asarray(split_up(number_of, total, limit, skew), jnp.int32)
    twos = (number_of - 1) // 2
    giver, taker = tallies[1:1 + 2 * twos:2], tallies[2:2 + 2 * twos:2]
    margin = jnp.minimum(giver - 1, limit - taker)
    moved = jax.random.randint(jax.random.fold_in(own_key, 1), (twos,), 0, 1 << 20) % (margin + 1)
    tallies = tallies.at[1:1 + 2 * twos:2].set(giver - moved).at[2:2 + 2 * twos:2].set(taker + moved)
    return tallies[jax.random.permutation(jax.random.fold_in(own_key, 2), number_of)]


def bell_draw(own_key, dims, deviation, limit, shards=(), kind=jnp.bfloat16):
    values = deviation * jax.random.normal(own_key, dims, jnp.float32)
    if shards:
        values = values * level_of(own_key, dims, shards, -0.22, 0.18)
    return jnp.clip(values, -limit, limit).astype(kind)


def setup_inputs(seed: int = 0) -> dict:
    keys = jax.random.split(jax.random.key(seed), 15)
    charges = bell_draw(keys[0], (UNKNOWNS, PORTS), 1.0, 6.0, ((0, 128),), jnp.float32)
    leaf_size = uneven_parts(keys[1], LEAVES, LEAVES * (LEAF * 3 // 4), LEAF, 1).astype(jnp.int32)
    leaf_basis = bell_draw(keys[2], (LEAVES, RANK, LEAF), LEAF ** -0.5, 0.375, ((0, 128),), jnp.float32)
    leaf_transfer = bell_draw(keys[3], (LEAVES, RANK, RANK), (4 * RANK) ** -0.5, 0.375, ((0, 128),), jnp.float32)
    mid_transfer = bell_draw(keys[4], (MIDS, RANK, RANK), (MIDS_DEV * RANK) ** -0.5, 0.25, ((0, 128),), jnp.float32)
    leaf_parent = draw_leaf_parent(jax.random.fold_in(keys[14], 71), 0)
    send_leaf = draw_send_leaf(jax.random.fold_in(keys[14], 71), 0)
    pair_leaf = draw_pair_leaf(jax.random.fold_in(keys[14], 71), 0)
    leaf_coupling = bell_draw(keys[8], (LEAVES, RANK, LIST_LEAF * RANK), (LIST_LEAF * RANK) ** -0.5, 0.21875, ((0, 128),), jnp.float32)
    send_mid = draw_send_mid(jax.random.fold_in(keys[14], 71), 0)
    pair_mid = draw_pair_mid(jax.random.fold_in(keys[14], 71), 0)
    mid_coupling = bell_draw(keys[11], (MIDS, RANK, LIST_MID * RANK), (LIST_MID * RANK) ** -0.5, 0.125, ((0, 128),), jnp.float32)
    top_pairs = draw_top_pairs(jax.random.fold_in(keys[14], 71), 0)
    top_coupling = bell_draw(keys[13], (COARSE, RANK, LIST_TOP * RANK), (LIST_TOP * RANK) ** -0.5, 0.375, ((0, 4),), jnp.float32)
    return dict(charges=charges, leaf_size=leaf_size, leaf_basis=leaf_basis, leaf_transfer=leaf_transfer, mid_transfer=mid_transfer, leaf_parent=leaf_parent, send_leaf=send_leaf, pair_leaf=pair_leaf, leaf_coupling=leaf_coupling, send_mid=send_mid, pair_mid=pair_mid, mid_coupling=mid_coupling, top_pairs=top_pairs, top_coupling=top_coupling)


exact_mode = lax.Precision.HIGHEST


def couple(coupling, coef, index):
    stacked = jnp.take(coef, index, axis=0, mode="fill", fill_value=0.0)
    stacked = stacked.reshape(index.shape[0], index.shape[1] * coef.shape[1], coef.shape[2])
    return jnp.einsum("nkq,nqp->nkp", coupling, stacked, precision=exact_mode)


def couple_blocks(coupling, coef, index):
    per_owner = coupling.shape[0] // OWNERS

    def apply_block(pieces):
        return couple(pieces[0], coef, pieces[1])

    coupled = lax.map(apply_block, (coupling.reshape(OWNERS, per_owner, coupling.shape[1], coupling.shape[2]), index.reshape(OWNERS, per_owner, index.shape[1])))
    return coupled.reshape(coupling.shape[0], coef.shape[1], coef.shape[2])


def source_index(send_table, pair_table, per_owner):
    slot_table = send_table.reshape(OWNERS, OWNERS, SLOTS)
    receiver = (jnp.arange(pair_table.shape[0], dtype=jnp.int32) // per_owner)[:, None]
    is_live = pair_table < OWNERS * SLOTS
    sender = jnp.minimum(pair_table // SLOTS, OWNERS - 1).astype(jnp.int32)
    slot_index = (pair_table % SLOTS).astype(jnp.int32)
    local_index = slot_table[sender, receiver, slot_index]
    found = sender * per_owner + local_index
    return jnp.where(is_live & (local_index < per_owner), found, OWNERS * per_owner).astype(jnp.int32)


def reference(charges, leaf_size, leaf_basis, leaf_transfer, mid_transfer, leaf_parent, send_leaf, pair_leaf, leaf_coupling, send_mid, pair_mid, mid_coupling, top_pairs, top_coupling):
    point_mask = (jnp.arange(LEAF, dtype=jnp.int32)[None, :] < leaf_size[:, None]).astype(jnp.float32)
    blocks = charges.reshape(LEAVES, LEAF, PORTS) * point_mask[:, :, None]
    coef_leaf = jnp.einsum("lkm,lmp->lkp", leaf_basis, blocks, precision=exact_mode)
    parent_global = ((jnp.arange(LEAVES, dtype=jnp.int32) // LEAVES_DEV) * MIDS_DEV + leaf_parent).astype(jnp.int32)
    moved_up = jnp.einsum("ljk,lkp->ljp", leaf_transfer, coef_leaf, precision=exact_mode)
    coef_mid = jax.ops.segment_sum(moved_up, parent_global, num_segments=MIDS)
    moved_mid = jnp.einsum("mjk,mkp->mjp", mid_transfer, coef_mid, precision=exact_mode)
    coef_top = jnp.sum(moved_mid.reshape(OWNERS, MIDS_DEV, RANK, PORTS), axis=1)
    near_leaf = couple_blocks(leaf_coupling, coef_leaf, source_index(send_leaf, pair_leaf, LEAVES_DEV))
    near_mid = couple_blocks(mid_coupling, coef_mid, source_index(send_mid, pair_mid, MIDS_DEV))
    near_top = couple(top_coupling, coef_top, top_pairs)
    top_spread = jnp.repeat(near_top, MIDS_DEV, axis=0)
    down_mid = near_mid + jnp.einsum("mjk,mjp->mkp", mid_transfer, top_spread, precision=exact_mode)
    from_parent = jnp.take(down_mid, parent_global, axis=0)
    down_leaf = near_leaf + jnp.einsum("ljk,ljp->lkp", leaf_transfer, from_parent, precision=exact_mode)
    far_field = jnp.einsum("lkm,lkp->lmp", leaf_basis, down_leaf, precision=exact_mode) * point_mask[:, :, None]
    return far_field.reshape(UNKNOWNS, PORTS)
```

```python
import jax
import jax.numpy as jnp
from jax import lax
from jax.sharding import PartitionSpec as P

exact_mode = lax.Precision.HIGHEST


def couple(coupling, coef, index):
    stacked = jnp.take(coef, index, axis=0, mode="fill", fill_value=0.0)
    stacked = stacked.reshape(index.shape[0], index.shape[1] * coef.shape[1], coef.shape[2])
    return jnp.einsum("nkq,nqp->nkp", coupling, stacked, precision=exact_mode)


def body(
    charges,
    leaf_size,
    leaf_basis,
    leaf_transfer,
    mid_transfer,
    leaf_parent,
    send_leaf,
    pair_leaf,
    leaf_coupling,
    send_mid,
    pair_mid,
    mid_coupling,
    top_pairs,
    top_coupling,
):
    leaf_count, coef_rank, leaf_points = leaf_basis.shape
    port_count = charges.shape[1]
    mid_count = mid_transfer.shape[0]
    owners = send_leaf.shape[0] // 2
    slots = 2
    point_mask = (jnp.arange(leaf_points, dtype=jnp.int32)[None, :] < leaf_size[:, None]).astype(
        jnp.float32
    )
    blocks = charges.reshape(leaf_count, leaf_points, port_count) * point_mask[:, :, None]
    coef_leaf = jnp.einsum("lkm,lmp->lkp", leaf_basis, blocks, precision=exact_mode)
    moved_up = jnp.einsum("ljk,lkp->ljp", leaf_transfer, coef_leaf, precision=exact_mode)
    parent_map = (leaf_parent[None, :] == jnp.arange(mid_count, dtype=jnp.int32)[:, None]).astype(
        jnp.float32
    )
    coef_mid = jnp.einsum("ml,ljp->mjp", parent_map, moved_up, precision=exact_mode)
    coef_top = jnp.einsum("mjk,mkp->jp", mid_transfer, coef_mid, precision=exact_mode)

    outgoing_leaf = jnp.take(coef_leaf, send_leaf, axis=0, mode="fill", fill_value=0.0)
    outgoing_leaf = outgoing_leaf.reshape(owners, slots, coef_rank, port_count)
    top_rows = jnp.broadcast_to(coef_top[None, None], (owners, 1, coef_rank, port_count))
    outgoing = jnp.concatenate([outgoing_leaf, top_rows], axis=1).reshape(
        owners * (slots + 1), coef_rank, port_count
    )
    arrived = lax.all_to_all(outgoing, ("group", "cluster"), split_axis=0, concat_axis=0, tiled=True)

    outgoing_mid = jnp.take(coef_mid, send_mid, axis=0, mode="fill", fill_value=0.0)
    arrived_mid = lax.all_to_all(
        outgoing_mid, ("group", "cluster"), split_axis=0, concat_axis=0, tiled=True
    )

    total_rows = owners * (slots + 1)
    leaf_rows = jnp.where(
        pair_leaf < owners * slots, pair_leaf + pair_leaf // slots, total_rows
    )
    near_leaf = couple(leaf_coupling, arrived, leaf_rows)

    position = lax.axis_index("cluster")
    wanted = lax.dynamic_slice_in_dim(top_pairs, position, 1, 0)
    own_coupling = lax.dynamic_slice_in_dim(top_coupling, position, 1, 0)
    top_rows_idx = jnp.where(
        (wanted >= 0) & (wanted < owners), wanted * (slots + 1) + slots, total_rows
    )
    near_top = couple(own_coupling, arrived, top_rows_idx)[0]

    near_mid = couple(mid_coupling, arrived_mid, pair_mid)
    down_mid = near_mid + jnp.einsum("mjk,jp->mkp", mid_transfer, near_top, precision=exact_mode)
    from_parent = jnp.einsum("ml,mkp->lkp", parent_map, down_mid, precision=exact_mode)
    down_leaf = near_leaf + jnp.einsum(
        "ljk,ljp->lkp", leaf_transfer, from_parent, precision=exact_mode
    )
    far_field = (
        jnp.einsum("lkm,lkp->lmp", leaf_basis, down_leaf, precision=exact_mode)
        * point_mask[:, :, None]
    )
    return far_field.reshape(leaf_count * leaf_points, port_count)


def solution(mesh):
    in_specs = (
        P(("group", "cluster"), None),
        P(("group", "cluster")),
        P(("group", "cluster"), None, None),
        P(("group", "cluster"), None, None),
        P(("group", "cluster"), None, None),
        P(("group", "cluster")),
        P(("group", "cluster")),
        P(("group", "cluster"), None),
        P(("group", "cluster"), None, None),
        P(("group", "cluster")),
        P(("group", "cluster"), None),
        P(("group", "cluster"), None, None),
        P("group", None),
        P("group", None, None),
    )
    out_specs = P(("group", "cluster"), None)
    return jax.shard_map(body, mesh=mesh, in_specs=in_specs, out_specs=out_specs, check_vma=False)
```

```python
import jax
import jax.numpy as jnp
from jax import lax
from jax.sharding import PartitionSpec as P

exact_mode = lax.Precision.HIGHEST


def couple(coupling, coef, index):
    stacked = jnp.take(coef, index, axis=0, mode="fill", fill_value=0.0)
    stacked = stacked.reshape(index.shape[0], index.shape[1] * coef.shape[1], coef.shape[2])
    return jnp.einsum("nkq,nqp->nkp", coupling, stacked, precision=exact_mode)


def body(
    charges,
    leaf_size,
    leaf_basis,
    leaf_transfer,
    mid_transfer,
    leaf_parent,
    send_leaf,
    pair_leaf,
    leaf_coupling,
    send_mid,
    pair_mid,
    mid_coupling,
    top_pairs,
    top_coupling,
):
    leaf_count, coef_rank, leaf_points = leaf_basis.shape
    port_count = charges.shape[1]
    mid_count = mid_transfer.shape[0]
    owners = send_leaf.shape[0] // 2
    slots = 2
    point_mask = (jnp.arange(leaf_points, dtype=jnp.int32)[None, :] < leaf_size[:, None]).astype(
        jnp.float32
    )
    blocks = charges.reshape(leaf_count, leaf_points, port_count) * point_mask[:, :, None]
    coef_leaf = jnp.einsum("lkm,lmp->lkp", leaf_basis, blocks, precision=exact_mode)
    moved_up = jnp.einsum("ljk,lkp->ljp", leaf_transfer, coef_leaf, precision=exact_mode)
    parent_map = (leaf_parent[None, :] == jnp.arange(mid_count, dtype=jnp.int32)[:, None]).astype(
        jnp.float32
    )
    coef_mid = jnp.einsum("ml,ljp->mjp", parent_map, moved_up, precision=exact_mode)
    coef_top = jnp.einsum("mjk,mkp->jp", mid_transfer, coef_mid, precision=exact_mode)

    outgoing_leaf = jnp.take(coef_leaf, send_leaf, axis=0, mode="fill", fill_value=0.0)
    outgoing_mid = jnp.take(coef_mid, send_mid, axis=0, mode="fill", fill_value=0.0)
    outgoing = jnp.concatenate(
        [
            outgoing_leaf.reshape(owners, slots, coef_rank, port_count),
            outgoing_mid.reshape(owners, slots, coef_rank, port_count),
        ],
        axis=1,
    ).reshape(owners * 2 * slots, coef_rank, port_count)
    arrived = lax.all_to_all(outgoing, ("group", "cluster"), split_axis=0, concat_axis=0, tiled=True)

    listed = top_pairs.shape[1]
    position = lax.axis_index("cluster")
    wanted = lax.dynamic_slice_in_dim(top_pairs, position, 1, 0)[0]
    own_coupling = lax.dynamic_slice_in_dim(top_coupling, position, 1, 0)[0]
    shard_rows = lax.all_gather(coef_top[None], ("group", "cluster"), axis=0, tiled=True)
    inside = (wanted >= 0) & (wanted < shard_rows.shape[0])
    taken_rows = jnp.take(shard_rows, jnp.clip(wanted, 0, shard_rows.shape[0] - 1), axis=0)
    picked = jnp.where(
        inside[:, None, None], taken_rows, jnp.zeros((listed, coef_rank, port_count), jnp.float32)
    )
    near_top = jnp.einsum(
        "kq,qp->kp",
        own_coupling,
        picked.reshape(listed * coef_rank, port_count),
        precision=exact_mode,
    )

    total_rows = owners * 2 * slots
    live_leaf = pair_leaf < owners * slots
    leaf_rows = jnp.where(live_leaf, pair_leaf + (pair_leaf // slots) * slots, total_rows)
    near_leaf = couple(leaf_coupling, arrived, leaf_rows)
    live_mid = pair_mid < owners * slots
    mid_rows = jnp.where(live_mid, pair_mid + (pair_mid // slots + 1) * slots, total_rows)
    near_mid = couple(mid_coupling, arrived, mid_rows)
    down_mid = near_mid + jnp.einsum("mjk,jp->mkp", mid_transfer, near_top, precision=exact_mode)
    from_parent = jnp.einsum("ml,mkp->lkp", parent_map, down_mid, precision=exact_mode)
    down_leaf = near_leaf + jnp.einsum(
        "ljk,ljp->lkp", leaf_transfer, from_parent, precision=exact_mode
    )
    far_field = (
        jnp.einsum("lkm,lkp->lmp", leaf_basis, down_leaf, precision=exact_mode)
        * point_mask[:, :, None]
    )
    return far_field.reshape(leaf_count * leaf_points, port_count)


def solution(mesh):
    in_specs = (
        P(("group", "cluster"), None),
        P(("group", "cluster")),
        P(("group", "cluster"), None, None),
        P(("group", "cluster"), None, None),
        P(("group", "cluster"), None, None),
        P(("group", "cluster")),
        P(("group", "cluster")),
        P(("group", "cluster"), None),
        P(("group", "cluster"), None, None),
        P(("group", "cluster")),
        P(("group", "cluster"), None),
        P(("group", "cluster"), None, None),
        P("group", None),
        P("group", None, None),
    )
    out_specs = P(("group", "cluster"), None)
    return jax.shard_map(body, mesh=mesh, in_specs=in_specs, out_specs=out_specs, check_vma=False)
```

```python
import functools

import jax
import jax.numpy as jnp
from jax import lax
from jax.experimental import pallas as pl
from jax.experimental.pallas import tpu as pltpu
from jax.sharding import PartitionSpec as P

exact_mode = lax.Precision.HIGHEST


def couple(coupling, coef, index):
    stacked = jnp.take(coef, index, axis=0, mode="fill", fill_value=0.0)
    stacked = stacked.reshape(index.shape[0], index.shape[1] * coef.shape[1], coef.shape[2])
    return jnp.einsum("nkq,nqp->nkp", coupling, stacked, precision=exact_mode)


def couple_kernel(nb, listed, total, idx_ref, arrived_ref, coupling_ref, out_ref):
    i = pl.program_id(0)
    rank = arrived_ref.shape[1]
    for t in range(nb):
        acc = jnp.zeros(out_ref.shape[1:], jnp.float32)
        for k in range(listed):
            r = idx_ref[(i * nb + t) * listed + k]
            valid = r < total
            blk = arrived_ref[jnp.minimum(r, total - 1)]
            c = coupling_ref[t, :, k * rank : (k + 1) * rank]
            prod = jnp.dot(c, blk, precision=exact_mode, preferred_element_type=jnp.float32)
            acc = acc + jnp.where(valid, prod, 0.0)
        out_ref[t] = acc


def couple_pallas(coupling, arrived, rows, nb):
    n, rank, width = coupling.shape
    listed = rows.shape[1]
    total, _, ports = arrived.shape
    grid_spec = pltpu.PrefetchScalarGridSpec(
        num_scalar_prefetch=1,
        grid=(n // nb,),
        in_specs=[
            pl.BlockSpec(
                (total, rank, ports), lambda i, idx: (0, 0, 0), pipeline_mode=pl.Buffered(1)
            ),
            pl.BlockSpec((nb, rank, width), lambda i, idx: (i, 0, 0)),
        ],
        out_specs=pl.BlockSpec((nb, rank, ports), lambda i, idx: (i, 0, 0)),
    )
    return pl.pallas_call(
        functools.partial(couple_kernel, nb, listed, total),
        grid_spec=grid_spec,
        out_shape=jax.ShapeDtypeStruct((n, rank, ports), jnp.float32),
        compiler_params=pltpu.CompilerParams(vmem_limit_bytes=60 * 1024 * 1024),
        cost_estimate=pl.CostEstimate(
            flops=2 * n * rank * width * ports,
            bytes_accessed=4 * (n * rank * width + total * rank * ports + n * rank * ports),
            transcendentals=0,
        ),
    )(rows.reshape(-1), arrived, coupling)


def body(
    charges,
    leaf_size,
    leaf_basis,
    leaf_transfer,
    mid_transfer,
    leaf_parent,
    send_leaf,
    pair_leaf,
    leaf_coupling,
    send_mid,
    pair_mid,
    mid_coupling,
    top_pairs,
    top_coupling,
):
    leaf_count, coef_rank, leaf_points = leaf_basis.shape
    port_count = charges.shape[1]
    mid_count = mid_transfer.shape[0]
    owners = send_leaf.shape[0] // 2
    slots = 2
    point_mask = (jnp.arange(leaf_points, dtype=jnp.int32)[None, :] < leaf_size[:, None]).astype(
        jnp.float32
    )
    blocks = charges.reshape(leaf_count, leaf_points, port_count) * point_mask[:, :, None]
    coef_leaf = jnp.einsum("lkm,lmp->lkp", leaf_basis, blocks, precision=exact_mode)
    moved_up = jnp.einsum("ljk,lkp->ljp", leaf_transfer, coef_leaf, precision=exact_mode)
    parent_map = (leaf_parent[None, :] == jnp.arange(mid_count, dtype=jnp.int32)[:, None]).astype(
        jnp.float32
    )
    coef_mid = jnp.einsum("ml,ljp->mjp", parent_map, moved_up, precision=exact_mode)
    coef_top = jnp.einsum("mjk,mkp->jp", mid_transfer, coef_mid, precision=exact_mode)

    outgoing_leaf = jnp.take(coef_leaf, send_leaf, axis=0, mode="fill", fill_value=0.0)
    outgoing_mid = jnp.take(coef_mid, send_mid, axis=0, mode="fill", fill_value=0.0)
    outgoing = jnp.concatenate(
        [
            outgoing_leaf.reshape(owners, slots, coef_rank, port_count),
            outgoing_mid.reshape(owners, slots, coef_rank, port_count),
        ],
        axis=1,
    ).reshape(owners * 2 * slots, coef_rank, port_count)
    arrived = lax.all_to_all(outgoing, ("group", "cluster"), split_axis=0, concat_axis=0, tiled=True)

    listed = top_pairs.shape[1]
    position = lax.axis_index("cluster")
    wanted = lax.dynamic_slice_in_dim(top_pairs, position, 1, 0)[0]
    own_coupling = lax.dynamic_slice_in_dim(top_coupling, position, 1, 0)[0]
    shard_rows = lax.all_gather(coef_top[None], ("group", "cluster"), axis=0, tiled=True)
    inside = (wanted >= 0) & (wanted < shard_rows.shape[0])
    taken_rows = jnp.take(shard_rows, jnp.clip(wanted, 0, shard_rows.shape[0] - 1), axis=0)
    picked = jnp.where(
        inside[:, None, None], taken_rows, jnp.zeros((listed, coef_rank, port_count), jnp.float32)
    )
    near_top = jnp.einsum(
        "kq,qp->kp",
        own_coupling,
        picked.reshape(listed * coef_rank, port_count),
        precision=exact_mode,
    )

    total_rows = owners * 2 * slots
    live_leaf = pair_leaf < owners * slots
    leaf_rows = jnp.where(live_leaf, pair_leaf + (pair_leaf // slots) * slots, total_rows)
    near_leaf = couple_pallas(leaf_coupling, arrived, leaf_rows, 4)
    live_mid = pair_mid < owners * slots
    mid_rows = jnp.where(live_mid, pair_mid + (pair_mid // slots + 1) * slots, total_rows)
    near_mid = couple_pallas(mid_coupling, arrived, mid_rows, 2)
    down_mid = near_mid + jnp.einsum("mjk,jp->mkp", mid_transfer, near_top, precision=exact_mode)
    from_parent = jnp.einsum("ml,mkp->lkp", parent_map, down_mid, precision=exact_mode)
    down_leaf = near_leaf + jnp.einsum(
        "ljk,ljp->lkp", leaf_transfer, from_parent, precision=exact_mode
    )
    far_field = (
        jnp.einsum("lkm,lkp->lmp", leaf_basis, down_leaf, precision=exact_mode)
        * point_mask[:, :, None]
    )
    return far_field.reshape(leaf_count * leaf_points, port_count)


def solution(mesh):
    in_specs = (
        P(("group", "cluster"), None),
        P(("group", "cluster")),
        P(("group", "cluster"), None, None),
        P(("group", "cluster"), None, None),
        P(("group", "cluster"), None, None),
        P(("group", "cluster")),
        P(("group", "cluster")),
        P(("group", "cluster"), None),
        P(("group", "cluster"), None, None),
        P(("group", "cluster")),
        P(("group", "cluster"), None),
        P(("group", "cluster"), None, None),
        P("group", None),
        P("group", None, None),
    )
    out_specs = P(("group", "cluster"), None)
    return jax.shard_map(body, mesh=mesh, in_specs=in_specs, out_specs=out_specs, check_vma=False)
```

```python
import functools

import jax
import jax.numpy as jnp
from jax import lax
from jax.experimental import pallas as pl
from jax.experimental.pallas import tpu as pltpu
from jax.sharding import PartitionSpec as P

exact_mode = lax.Precision.HIGHEST


def couple(coupling, coef, index):
    stacked = jnp.take(coef, index, axis=0, mode="fill", fill_value=0.0)
    stacked = stacked.reshape(index.shape[0], index.shape[1] * coef.shape[1], coef.shape[2])
    return jnp.einsum("nkq,nqp->nkp", coupling, stacked, precision=exact_mode)


def couple_kernel(nb, listed, total, idx_ref, arrived_ref, coupling_ref, out_ref):
    i = pl.program_id(0)
    rank = arrived_ref.shape[1]
    for t in range(nb):
        acc = jnp.zeros(out_ref.shape[1:], jnp.float32)
        for k in range(listed):
            r = idx_ref[(i * nb + t) * listed + k]
            valid = r < total
            blk = arrived_ref[jnp.minimum(r, total - 1)]
            c = coupling_ref[t, :, k * rank : (k + 1) * rank]
            prod = jnp.dot(c, blk, precision=exact_mode, preferred_element_type=jnp.float32)
            acc = acc + jnp.where(valid, prod, 0.0)
        out_ref[t] = acc


def couple_pallas(coupling, arrived, rows, nb):
    n, rank, width = coupling.shape
    listed = rows.shape[1]
    total, _, ports = arrived.shape
    grid_spec = pltpu.PrefetchScalarGridSpec(
        num_scalar_prefetch=1,
        grid=(n // nb,),
        in_specs=[
            pl.BlockSpec(
                (total, rank, ports), lambda i, idx: (0, 0, 0), pipeline_mode=pl.Buffered(1)
            ),
            pl.BlockSpec((nb, rank, width), lambda i, idx: (i, 0, 0)),
        ],
        out_specs=pl.BlockSpec((nb, rank, ports), lambda i, idx: (i, 0, 0)),
    )
    return pl.pallas_call(
        functools.partial(couple_kernel, nb, listed, total),
        grid_spec=grid_spec,
        out_shape=jax.ShapeDtypeStruct((n, rank, ports), jnp.float32),
        compiler_params=pltpu.CompilerParams(vmem_limit_bytes=60 * 1024 * 1024),
        cost_estimate=pl.CostEstimate(
            flops=2 * n * rank * width * ports,
            bytes_accessed=4 * (n * rank * width + total * rank * ports + n * rank * ports),
            transcendentals=0,
        ),
    )(rows.reshape(-1), arrived, coupling)


def top_kernel(listed, coarse, idx_ref, pos_ref, gathered_ref, coupling_ref, out_ref):
    rank = gathered_ref.shape[1]
    lanes = gathered_ref.shape[0]
    per_lane = coarse // lanes
    position = pos_ref[0]
    for o in range(coupling_ref.shape[0]):
        out_ref[o] = jnp.zeros(out_ref.shape[1:], jnp.float32)
        for k in range(listed):
            s = idx_ref[o * listed + k]

            @pl.when((s < coarse) & (s % per_lane == position))
            def _():
                blk = gathered_ref[jnp.minimum(s // per_lane, lanes - 1)]
                c = coupling_ref[o, :, k * rank : (k + 1) * rank]
                out_ref[o] += jnp.dot(
                    c, blk, precision=exact_mode, preferred_element_type=jnp.float32
                )


def top_partial(top_pairs, position, gathered, top_coupling, coarse):
    n, rank, width = top_coupling.shape
    listed = top_pairs.shape[1]
    ports = gathered.shape[2]
    grid_spec = pltpu.PrefetchScalarGridSpec(
        num_scalar_prefetch=2,
        grid=(1,),
        in_specs=[
            pl.BlockSpec(gathered.shape, lambda i, idx, pos: (0, 0, 0)),
            pl.BlockSpec(top_coupling.shape, lambda i, idx, pos: (0, 0, 0)),
        ],
        out_specs=pl.BlockSpec((n, rank, ports), lambda i, idx, pos: (0, 0, 0)),
    )
    return pl.pallas_call(
        functools.partial(top_kernel, listed, coarse),
        grid_spec=grid_spec,
        out_shape=jax.ShapeDtypeStruct((n, rank, ports), jnp.float32),
        cost_estimate=pl.CostEstimate(
            flops=2 * rank * width * ports,
            bytes_accessed=4 * (n * rank * width + n * rank * ports),
            transcendentals=0,
        ),
    )(top_pairs.reshape(-1), position, gathered, top_coupling)


def body(
    charges,
    leaf_size,
    leaf_basis,
    leaf_transfer,
    mid_transfer,
    leaf_parent,
    send_leaf,
    pair_leaf,
    leaf_coupling,
    send_mid,
    pair_mid,
    mid_coupling,
    top_pairs,
    top_coupling,
):
    leaf_count, coef_rank, leaf_points = leaf_basis.shape
    port_count = charges.shape[1]
    mid_count = mid_transfer.shape[0]
    owners = send_leaf.shape[0] // 2
    slots = 2
    point_mask = (jnp.arange(leaf_points, dtype=jnp.int32)[None, :] < leaf_size[:, None]).astype(
        jnp.float32
    )
    blocks = charges.reshape(leaf_count, leaf_points, port_count) * point_mask[:, :, None]
    coef_leaf = jnp.einsum("lkm,lmp->lkp", leaf_basis, blocks, precision=exact_mode)
    moved_up = jnp.einsum("ljk,lkp->ljp", leaf_transfer, coef_leaf, precision=exact_mode)
    parent_map = (leaf_parent[None, :] == jnp.arange(mid_count, dtype=jnp.int32)[:, None]).astype(
        jnp.float32
    )
    coef_mid = jnp.einsum("ml,ljp->mjp", parent_map, moved_up, precision=exact_mode)
    coef_top = jnp.einsum("mjk,mkp->jp", mid_transfer, coef_mid, precision=exact_mode)

    outgoing_leaf = jnp.take(coef_leaf, send_leaf, axis=0, mode="fill", fill_value=0.0)
    outgoing_mid = jnp.take(coef_mid, send_mid, axis=0, mode="fill", fill_value=0.0)
    outgoing = jnp.concatenate(
        [
            outgoing_leaf.reshape(owners, slots, coef_rank, port_count),
            outgoing_mid.reshape(owners, slots, coef_rank, port_count),
        ],
        axis=1,
    ).reshape(owners * 2 * slots, coef_rank, port_count)
    arrived = lax.all_to_all(outgoing, ("group", "cluster"), split_axis=0, concat_axis=0, tiled=True)

    lanes = lax.all_gather(coef_top[None], "group", axis=0, tiled=True)
    position = lax.axis_index("cluster").astype(jnp.int32).reshape(1)
    partial = top_partial(top_pairs, position, lanes, top_coupling, owners)
    near_top = lax.psum_scatter(partial, "cluster", scatter_dimension=0, tiled=True)[0]

    total_rows = owners * 2 * slots
    live_leaf = pair_leaf < owners * slots
    leaf_rows = jnp.where(live_leaf, pair_leaf + (pair_leaf // slots) * slots, total_rows)
    near_leaf = couple_pallas(leaf_coupling, arrived, leaf_rows, 4)
    live_mid = pair_mid < owners * slots
    mid_rows = jnp.where(live_mid, pair_mid + (pair_mid // slots + 1) * slots, total_rows)
    near_mid = couple_pallas(mid_coupling, arrived, mid_rows, 2)
    down_mid = near_mid + jnp.einsum("mjk,jp->mkp", mid_transfer, near_top, precision=exact_mode)
    from_parent = jnp.einsum("ml,mkp->lkp", parent_map, down_mid, precision=exact_mode)
    down_leaf = near_leaf + jnp.einsum(
        "ljk,ljp->lkp", leaf_transfer, from_parent, precision=exact_mode
    )
    far_field = (
        jnp.einsum("lkm,lkp->lmp", leaf_basis, down_leaf, precision=exact_mode)
        * point_mask[:, :, None]
    )
    return far_field.reshape(leaf_count * leaf_points, port_count)


def solution(mesh):
    in_specs = (
        P(("group", "cluster"), None),
        P(("group", "cluster")),
        P(("group", "cluster"), None, None),
        P(("group", "cluster"), None, None),
        P(("group", "cluster"), None, None),
        P(("group", "cluster")),
        P(("group", "cluster")),
        P(("group", "cluster"), None),
        P(("group", "cluster"), None, None),
        P(("group", "cluster")),
        P(("group", "cluster"), None),
        P(("group", "cluster"), None, None),
        P("group", None),
        P("group", None, None),
    )
    out_specs = P(("group", "cluster"), None)
    return jax.shard_map(body, mesh=mesh, in_specs=in_specs, out_specs=out_specs, check_vma=False)
```

```python
import functools

import jax
import jax.numpy as jnp
from jax import lax
from jax.experimental import pallas as pl
from jax.experimental.pallas import tpu as pltpu
from jax.sharding import PartitionSpec as P

exact_mode = lax.Precision.HIGHEST


def couple(coupling, coef, index):
    stacked = jnp.take(coef, index, axis=0, mode="fill", fill_value=0.0)
    stacked = stacked.reshape(index.shape[0], index.shape[1] * coef.shape[1], coef.shape[2])
    return jnp.einsum("nkq,nqp->nkp", coupling, stacked, precision=exact_mode)


def couple_kernel(nb, listed, total, idx_ref, arrived_ref, coupling_ref, out_ref):
    i = pl.program_id(0)
    rank = arrived_ref.shape[1]
    for t in range(nb):
        acc = jnp.zeros(out_ref.shape[1:], jnp.float32)
        for k in range(listed):
            r = idx_ref[(i * nb + t) * listed + k]
            valid = r < total
            blk = arrived_ref[jnp.minimum(r, total - 1)]
            c = coupling_ref[t, :, k * rank : (k + 1) * rank]
            prod = jnp.dot(c, blk, precision=exact_mode, preferred_element_type=jnp.float32)
            acc = acc + jnp.where(valid, prod, 0.0)
        out_ref[t] = acc


def couple_pallas(coupling, arrived, rows, nb):
    n, rank, width = coupling.shape
    listed = rows.shape[1]
    total, _, ports = arrived.shape
    grid_spec = pltpu.PrefetchScalarGridSpec(
        num_scalar_prefetch=1,
        grid=(n // nb,),
        in_specs=[
            pl.BlockSpec(
                (total, rank, ports), lambda i, idx: (0, 0, 0), pipeline_mode=pl.Buffered(1)
            ),
            pl.BlockSpec((nb, rank, width), lambda i, idx: (i, 0, 0)),
        ],
        out_specs=pl.BlockSpec((nb, rank, ports), lambda i, idx: (i, 0, 0)),
    )
    return pl.pallas_call(
        functools.partial(couple_kernel, nb, listed, total),
        grid_spec=grid_spec,
        out_shape=jax.ShapeDtypeStruct((n, rank, ports), jnp.float32),
        compiler_params=pltpu.CompilerParams(vmem_limit_bytes=60 * 1024 * 1024),
        cost_estimate=pl.CostEstimate(
            flops=2 * n * rank * width * ports,
            bytes_accessed=4 * (n * rank * width + total * rank * ports + n * rank * ports),
            transcendentals=0,
        ),
    )(rows.reshape(-1), arrived, coupling)


def payload_kernel(chunk, size_ref, parent_ref, send_leaf_ref, send_mid_ref, charges_ref, basis_ref,
                   transfer_ref, mid_transfer_ref, out_ref, top_ref, leaf_sc, mid_sc):
    i = pl.program_id(0)
    leaves, rank, points = basis_ref.shape
    mids = mid_transfer_ref.shape[0]

    @pl.when(i == 0)
    def _():
        mid_sc[...] = jnp.zeros(mid_sc.shape, jnp.float32)
        rows = lax.broadcasted_iota(jnp.int32, (points, 1), 0)
        for l in range(leaves):
            blk = charges_ref[l * points:(l + 1) * points, :]
            blk = jnp.where(rows < size_ref[l], blk, 0.0)
            coef = jnp.dot(basis_ref[l], blk, precision=exact_mode, preferred_element_type=jnp.float32)
            leaf_sc[l] = coef
            up = jnp.dot(transfer_ref[l], coef, precision=exact_mode, preferred_element_type=jnp.float32)
            p = parent_ref[l]
            mid_sc[p] = mid_sc[p] + up
        top = jnp.zeros(top_ref.shape, jnp.float32)
        for c in range(mids):
            top = top + jnp.dot(mid_transfer_ref[c], mid_sc[c], precision=exact_mode,
                                preferred_element_type=jnp.float32)
        top_ref[...] = top

    per = chunk // 4
    for q in range(per):
        r = i * per + q
        for j in range(2):
            a = send_leaf_ref[r * 2 + j]
            out_ref[q * 4 + j] = jnp.where(a < leaves, leaf_sc[jnp.minimum(a, leaves - 1)], 0.0)
            b = send_mid_ref[r * 2 + j]
            out_ref[q * 4 + 2 + j] = jnp.where(b < mids, mid_sc[jnp.minimum(b, mids - 1)], 0.0)

def build_payload(charges, leaf_size, leaf_parent, send_leaf, send_mid, leaf_basis, leaf_transfer, mid_transfer, steps=8):
    leaves, rank, points = leaf_basis.shape
    ports = charges.shape[1]
    mids = mid_transfer.shape[0]
    owners = send_leaf.shape[0] // 2
    total = owners * 4
    chunk = total // steps
    full = lambda shape: pl.BlockSpec(shape, lambda i, *_: (0,) * len(shape), pipeline_mode=pl.Buffered(1))
    grid_spec = pltpu.PrefetchScalarGridSpec(
        num_scalar_prefetch=4,
        grid=(steps,),
        in_specs=[full(charges.shape), full(leaf_basis.shape), full(leaf_transfer.shape), full(mid_transfer.shape)],
        out_specs=[pl.BlockSpec((chunk, rank, ports), lambda i, *_: (i, 0, 0)),
                   pl.BlockSpec((rank, ports), lambda i, *_: (0, 0))],
        scratch_shapes=[pltpu.VMEM((leaves, rank, ports), jnp.float32), pltpu.VMEM((mids, rank, ports), jnp.float32)],
    )
    return pl.pallas_call(
        functools.partial(payload_kernel, chunk),
        grid_spec=grid_spec,
        out_shape=[jax.ShapeDtypeStruct((total, rank, ports), jnp.float32), jax.ShapeDtypeStruct((rank, ports), jnp.float32)],
        compiler_params=pltpu.CompilerParams(vmem_limit_bytes=60 * 1024 * 1024, dimension_semantics=("arbitrary",)),
        cost_estimate=pl.CostEstimate(flops=2 * leaves * rank * points * ports, bytes_accessed=4 * (charges.size + leaf_basis.size + total * rank * ports), transcendentals=0),
    )(leaf_size, leaf_parent, send_leaf, send_mid, charges, leaf_basis, leaf_transfer, mid_transfer)

def far_kernel(nb, size_ref, parent_ref, near_ref, transfer_ref, basis_ref, down_mid_ref, out_ref):
    i = pl.program_id(0)
    rank = near_ref.shape[1]
    points = basis_ref.shape[2]
    rows = lax.broadcasted_iota(jnp.int32, (points, 1), 0)
    tdims = (((0,), (0,)), ((), ()))
    for t in range(nb):
        l = i * nb + t
        p = parent_ref[l]
        dm = down_mid_ref[p]
        dl = near_ref[t] + lax.dot_general(transfer_ref[t], dm, tdims, precision=exact_mode, preferred_element_type=jnp.float32)
        far = lax.dot_general(basis_ref[t], dl, tdims, precision=exact_mode, preferred_element_type=jnp.float32)
        out_ref[t * points:(t + 1) * points, :] = jnp.where(rows < size_ref[l], far, 0.0)

def far_field_pallas(near_leaf, leaf_transfer, leaf_basis, down_mid, leaf_size, leaf_parent, nb=8):
    leaves, rank, points = leaf_basis.shape
    ports = near_leaf.shape[2]
    grid_spec = pltpu.PrefetchScalarGridSpec(
        num_scalar_prefetch=2,
        grid=(leaves // nb,),
        in_specs=[pl.BlockSpec((nb, rank, ports), lambda i, *_: (i, 0, 0)),
                  pl.BlockSpec((nb, rank, rank), lambda i, *_: (i, 0, 0)),
                  pl.BlockSpec((nb, rank, points), lambda i, *_: (i, 0, 0)),
                  pl.BlockSpec(down_mid.shape, lambda i, *_: (0, 0, 0))],
        out_specs=pl.BlockSpec((nb * points, ports), lambda i, *_: (i, 0)),
    )
    return pl.pallas_call(
        functools.partial(far_kernel, nb),
        grid_spec=grid_spec,
        out_shape=jax.ShapeDtypeStruct((leaves * points, ports), jnp.float32),
        compiler_params=pltpu.CompilerParams(vmem_limit_bytes=60 * 1024 * 1024),
        cost_estimate=pl.CostEstimate(flops=2 * leaves * rank * points * ports, bytes_accessed=4 * (leaf_basis.size + 2 * leaves * points * ports), transcendentals=0),
    )(leaf_size, leaf_parent, near_leaf, leaf_transfer, leaf_basis, down_mid)


def body(
    charges,
    leaf_size,
    leaf_basis,
    leaf_transfer,
    mid_transfer,
    leaf_parent,
    send_leaf,
    pair_leaf,
    leaf_coupling,
    send_mid,
    pair_mid,
    mid_coupling,
    top_pairs,
    top_coupling,
):
    leaf_count, coef_rank, leaf_points = leaf_basis.shape
    port_count = charges.shape[1]
    mid_count = mid_transfer.shape[0]
    owners = send_leaf.shape[0] // 2
    slots = 2
    arrived_rows, coef_top = build_payload(
        charges, leaf_size, leaf_parent, send_leaf, send_mid, leaf_basis, leaf_transfer, mid_transfer
    )
    arrived = lax.all_to_all(
        arrived_rows, ("group", "cluster"), split_axis=0, concat_axis=0, tiled=True
    )

    listed = top_pairs.shape[1]
    position = lax.axis_index("cluster")
    wanted = lax.dynamic_slice_in_dim(top_pairs, position, 1, 0)[0]
    own_coupling = lax.dynamic_slice_in_dim(top_coupling, position, 1, 0)[0]
    shard_rows = lax.all_gather(coef_top[None], ("group", "cluster"), axis=0, tiled=True)
    inside = (wanted >= 0) & (wanted < shard_rows.shape[0])
    taken_rows = jnp.take(shard_rows, jnp.clip(wanted, 0, shard_rows.shape[0] - 1), axis=0)
    picked = jnp.where(
        inside[:, None, None], taken_rows, jnp.zeros((listed, coef_rank, port_count), jnp.float32)
    )
    near_top = jnp.einsum(
        "kq,qp->kp",
        own_coupling,
        picked.reshape(listed * coef_rank, port_count),
        precision=exact_mode,
    )

    total_rows = owners * 2 * slots
    live_leaf = pair_leaf < owners * slots
    leaf_rows = jnp.where(live_leaf, pair_leaf + (pair_leaf // slots) * slots, total_rows)
    near_leaf = couple_pallas(leaf_coupling, arrived, leaf_rows, 4)
    live_mid = pair_mid < owners * slots
    mid_rows = jnp.where(live_mid, pair_mid + (pair_mid // slots + 1) * slots, total_rows)
    near_mid = couple_pallas(mid_coupling, arrived, mid_rows, 2)
    down_mid = near_mid + jnp.einsum("mjk,jp->mkp", mid_transfer, near_top, precision=exact_mode)
    return far_field_pallas(near_leaf, leaf_transfer, leaf_basis, down_mid, leaf_size, leaf_parent)


def solution(mesh):
    in_specs = (
        P(("group", "cluster"), None),
        P(("group", "cluster")),
        P(("group", "cluster"), None, None),
        P(("group", "cluster"), None, None),
        P(("group", "cluster"), None, None),
        P(("group", "cluster")),
        P(("group", "cluster")),
        P(("group", "cluster"), None),
        P(("group", "cluster"), None, None),
        P(("group", "cluster")),
        P(("group", "cluster"), None),
        P(("group", "cluster"), None, None),
        P("group", None),
        P("group", None, None),
    )
    out_specs = P(("group", "cluster"), None)
    return jax.shard_map(body, mesh=mesh, in_specs=in_specs, out_specs=out_specs, check_vma=False)
```

```python
import functools

import jax
import jax.numpy as jnp
from jax import lax
from jax.experimental import pallas as pl
from jax.experimental.pallas import tpu as pltpu
from jax.sharding import PartitionSpec as P

exact_mode = lax.Precision.HIGHEST


def couple(coupling, coef, index):
    stacked = jnp.take(coef, index, axis=0, mode="fill", fill_value=0.0)
    stacked = stacked.reshape(index.shape[0], index.shape[1] * coef.shape[1], coef.shape[2])
    return jnp.einsum("nkq,nqp->nkp", coupling, stacked, precision=exact_mode)


def couple_kernel(nb, listed, total, idx_ref, arrived_ref, coupling_ref, out_ref):
    i = pl.program_id(0)
    rank = arrived_ref.shape[1]
    for t in range(nb):
        acc = jnp.zeros(out_ref.shape[1:], jnp.float32)
        for k in range(listed):
            r = idx_ref[(i * nb + t) * listed + k]
            valid = r < total
            blk = arrived_ref[jnp.minimum(r, total - 1)]
            c = coupling_ref[t, :, k * rank : (k + 1) * rank]
            prod = jnp.dot(c, blk, precision=exact_mode, preferred_element_type=jnp.float32)
            acc = acc + jnp.where(valid, prod, 0.0)
        out_ref[t] = acc


def couple_pallas(coupling, arrived, rows, nb):
    n, rank, width = coupling.shape
    listed = rows.shape[1]
    total, _, ports = arrived.shape
    grid_spec = pltpu.PrefetchScalarGridSpec(
        num_scalar_prefetch=1,
        grid=(n // nb,),
        in_specs=[
            pl.BlockSpec(
                (total, rank, ports), lambda i, idx: (0, 0, 0), pipeline_mode=pl.Buffered(1)
            ),
            pl.BlockSpec((nb, rank, width), lambda i, idx: (i, 0, 0)),
        ],
        out_specs=pl.BlockSpec((nb, rank, ports), lambda i, idx: (i, 0, 0)),
    )
    return pl.pallas_call(
        functools.partial(couple_kernel, nb, listed, total),
        grid_spec=grid_spec,
        out_shape=jax.ShapeDtypeStruct((n, rank, ports), jnp.float32),
        compiler_params=pltpu.CompilerParams(vmem_limit_bytes=60 * 1024 * 1024),
        cost_estimate=pl.CostEstimate(
            flops=2 * n * rank * width * ports,
            bytes_accessed=4 * (n * rank * width + total * rank * ports + n * rank * ports),
            transcendentals=0,
        ),
    )(rows.reshape(-1), arrived, coupling)


def payload_kernel(chunk, size_ref, parent_ref, send_leaf_ref, send_mid_ref, charges_ref, basis_ref,
                   transfer_ref, mid_transfer_ref, out_ref, top_ref, leaf_sc, mid_sc):
    i = pl.program_id(0)
    leaves, rank, points = basis_ref.shape
    mids = mid_transfer_ref.shape[0]

    @pl.when(i == 0)
    def _():
        mid_sc[...] = jnp.zeros(mid_sc.shape, jnp.float32)
        rows = lax.broadcasted_iota(jnp.int32, (points, 1), 0)
        for l in range(leaves):
            blk = charges_ref[l * points:(l + 1) * points, :]
            blk = jnp.where(rows < size_ref[l], blk, 0.0)
            coef = jnp.dot(basis_ref[l], blk, precision=exact_mode, preferred_element_type=jnp.float32)
            leaf_sc[l] = coef
            up = jnp.dot(transfer_ref[l], coef, precision=exact_mode, preferred_element_type=jnp.float32)
            p = parent_ref[l]
            mid_sc[p] = mid_sc[p] + up
        top = jnp.zeros(top_ref.shape, jnp.float32)
        for c in range(mids):
            top = top + jnp.dot(mid_transfer_ref[c], mid_sc[c], precision=exact_mode,
                                preferred_element_type=jnp.float32)
        top_ref[...] = top

    per = chunk // 4
    for q in range(per):
        r = i * per + q
        for j in range(2):
            a = send_leaf_ref[r * 2 + j]
            out_ref[q * 4 + j] = jnp.where(a < leaves, leaf_sc[jnp.minimum(a, leaves - 1)], 0.0)
            b = send_mid_ref[r * 2 + j]
            out_ref[q * 4 + 2 + j] = jnp.where(b < mids, mid_sc[jnp.minimum(b, mids - 1)], 0.0)

def build_payload(charges, leaf_size, leaf_parent, send_leaf, send_mid, leaf_basis, leaf_transfer, mid_transfer, steps=8):
    leaves, rank, points = leaf_basis.shape
    ports = charges.shape[1]
    mids = mid_transfer.shape[0]
    owners = send_leaf.shape[0] // 2
    total = owners * 4
    chunk = total // steps
    full = lambda shape: pl.BlockSpec(shape, lambda i, *_: (0,) * len(shape), pipeline_mode=pl.Buffered(1))
    grid_spec = pltpu.PrefetchScalarGridSpec(
        num_scalar_prefetch=4,
        grid=(steps,),
        in_specs=[full(charges.shape), full(leaf_basis.shape), full(leaf_transfer.shape), full(mid_transfer.shape)],
        out_specs=[pl.BlockSpec((chunk, rank, ports), lambda i, *_: (i, 0, 0)),
                   pl.BlockSpec((rank, ports), lambda i, *_: (0, 0))],
        scratch_shapes=[pltpu.VMEM((leaves, rank, ports), jnp.float32), pltpu.VMEM((mids, rank, ports), jnp.float32)],
    )
    return pl.pallas_call(
        functools.partial(payload_kernel, chunk),
        grid_spec=grid_spec,
        out_shape=[jax.ShapeDtypeStruct((total, rank, ports), jnp.float32), jax.ShapeDtypeStruct((rank, ports), jnp.float32)],
        compiler_params=pltpu.CompilerParams(vmem_limit_bytes=60 * 1024 * 1024, dimension_semantics=("arbitrary",)),
        cost_estimate=pl.CostEstimate(flops=2 * leaves * rank * points * ports, bytes_accessed=4 * (charges.size + leaf_basis.size + total * rank * ports), transcendentals=0),
    )(leaf_size, leaf_parent, send_leaf, send_mid, charges, leaf_basis, leaf_transfer, mid_transfer)

def far_kernel(nb, size_ref, parent_ref, near_ref, transfer_ref, basis_ref, down_mid_ref, out_ref):
    i = pl.program_id(0)
    rank = near_ref.shape[1]
    points = basis_ref.shape[2]
    rows = lax.broadcasted_iota(jnp.int32, (points, 1), 0)
    tdims = (((0,), (0,)), ((), ()))
    for t in range(nb):
        l = i * nb + t
        p = parent_ref[l]
        dm = down_mid_ref[p]
        dl = near_ref[t] + lax.dot_general(transfer_ref[t], dm, tdims, precision=exact_mode, preferred_element_type=jnp.float32)
        far = lax.dot_general(basis_ref[t], dl, tdims, precision=exact_mode, preferred_element_type=jnp.float32)
        out_ref[t * points:(t + 1) * points, :] = jnp.where(rows < size_ref[l], far, 0.0)

def far_field_pallas(near_leaf, leaf_transfer, leaf_basis, down_mid, leaf_size, leaf_parent, nb=8):
    leaves, rank, points = leaf_basis.shape
    ports = near_leaf.shape[2]
    grid_spec = pltpu.PrefetchScalarGridSpec(
        num_scalar_prefetch=2,
        grid=(leaves // nb,),
        in_specs=[pl.BlockSpec((nb, rank, ports), lambda i, *_: (i, 0, 0)),
                  pl.BlockSpec((nb, rank, rank), lambda i, *_: (i, 0, 0)),
                  pl.BlockSpec((nb, rank, points), lambda i, *_: (i, 0, 0)),
                  pl.BlockSpec(down_mid.shape, lambda i, *_: (0, 0, 0))],
        out_specs=pl.BlockSpec((nb * points, ports), lambda i, *_: (i, 0)),
    )
    return pl.pallas_call(
        functools.partial(far_kernel, nb),
        grid_spec=grid_spec,
        out_shape=jax.ShapeDtypeStruct((leaves * points, ports), jnp.float32),
        compiler_params=pltpu.CompilerParams(vmem_limit_bytes=60 * 1024 * 1024),
        cost_estimate=pl.CostEstimate(flops=2 * leaves * rank * points * ports, bytes_accessed=4 * (leaf_basis.size + 2 * leaves * points * ports), transcendentals=0),
    )(leaf_size, leaf_parent, near_leaf, leaf_transfer, leaf_basis, down_mid)


def exchange_kernel(axes, sizes, payload_ref, landing_ref, send_sem, recv_sem, local_sem):
    outer, inner = sizes
    count = outer * inner
    me = lax.axis_index(axes[0]) * inner + lax.axis_index(axes[1])
    barrier = pltpu.get_barrier_semaphore()

    def greet(q, carry):
        peer = lax.rem(me + q, count)
        pl.semaphore_signal(barrier, 1, device_id=(peer // inner, peer % inner),
                            device_id_type=pl.DeviceIdType.MESH)
        return carry

    lax.fori_loop(1, count, greet, 0)
    pl.semaphore_wait(barrier, count - 1)

    def send(q, carry):
        peer = lax.rem(me + q, count)
        pltpu.make_async_remote_copy(
            src_ref=payload_ref.at[peer],
            dst_ref=landing_ref.at[me],
            send_sem=send_sem,
            recv_sem=recv_sem,
            device_id=(peer // inner, peer % inner),
            device_id_type=pl.DeviceIdType.MESH,
        ).start()
        return carry

    lax.fori_loop(1, count, send, 0)
    own = pltpu.make_async_copy(payload_ref.at[me], landing_ref.at[me], local_sem)
    own.start()
    own.wait()
    everything = pltpu.make_async_remote_copy(
        src_ref=payload_ref.at[pl.ds(0, count - 1)],
        dst_ref=landing_ref.at[pl.ds(0, count - 1)],
        send_sem=send_sem,
        recv_sem=recv_sem,
        device_id=(0, 0),
        device_id_type=pl.DeviceIdType.MESH,
    )
    everything.wait_send()
    everything.wait_recv()

def exchange(payload, axes, sizes):
    return pl.pallas_call(
        functools.partial(exchange_kernel, axes, sizes),
        out_shape=jax.ShapeDtypeStruct(payload.shape, payload.dtype),
        in_specs=[pl.BlockSpec(memory_space=pl.ANY)],
        out_specs=pl.BlockSpec(memory_space=pl.ANY),
        scratch_shapes=[pltpu.SemaphoreType.DMA, pltpu.SemaphoreType.DMA, pltpu.SemaphoreType.DMA],
        compiler_params=pltpu.CompilerParams(collective_id=0, has_side_effects=True),
    )(payload)


def body(
    sizes,
    charges,
    leaf_size,
    leaf_basis,
    leaf_transfer,
    mid_transfer,
    leaf_parent,
    send_leaf,
    pair_leaf,
    leaf_coupling,
    send_mid,
    pair_mid,
    mid_coupling,
    top_pairs,
    top_coupling,
):
    leaf_count, coef_rank, leaf_points = leaf_basis.shape
    port_count = charges.shape[1]
    mid_count = mid_transfer.shape[0]
    owners = send_leaf.shape[0] // 2
    slots = 2
    arrived_rows, coef_top = build_payload(
        charges, leaf_size, leaf_parent, send_leaf, send_mid, leaf_basis, leaf_transfer, mid_transfer
    )
    owners_total = send_leaf.shape[0] // 2
    landing = exchange(
        arrived_rows.reshape((owners_total, -1) + arrived_rows.shape[1:]),
        ("group", "cluster"),
        sizes,
    )
    arrived = landing.reshape(arrived_rows.shape)

    listed = top_pairs.shape[1]
    position = lax.axis_index("cluster")
    wanted = lax.dynamic_slice_in_dim(top_pairs, position, 1, 0)[0]
    own_coupling = lax.dynamic_slice_in_dim(top_coupling, position, 1, 0)[0]
    shard_rows = lax.all_gather(coef_top[None], ("group", "cluster"), axis=0, tiled=True)
    inside = (wanted >= 0) & (wanted < shard_rows.shape[0])
    taken_rows = jnp.take(shard_rows, jnp.clip(wanted, 0, shard_rows.shape[0] - 1), axis=0)
    picked = jnp.where(
        inside[:, None, None], taken_rows, jnp.zeros((listed, coef_rank, port_count), jnp.float32)
    )
    near_top = jnp.einsum(
        "kq,qp->kp",
        own_coupling,
        picked.reshape(listed * coef_rank, port_count),
        precision=exact_mode,
    )

    total_rows = owners * 2 * slots
    live_leaf = pair_leaf < owners * slots
    leaf_rows = jnp.where(live_leaf, pair_leaf + (pair_leaf // slots) * slots, total_rows)
    near_leaf = couple_pallas(leaf_coupling, arrived, leaf_rows, 4)
    live_mid = pair_mid < owners * slots
    mid_rows = jnp.where(live_mid, pair_mid + (pair_mid // slots + 1) * slots, total_rows)
    near_mid = couple_pallas(mid_coupling, arrived, mid_rows, 2)
    down_mid = near_mid + jnp.einsum("mjk,jp->mkp", mid_transfer, near_top, precision=exact_mode)
    return far_field_pallas(near_leaf, leaf_transfer, leaf_basis, down_mid, leaf_size, leaf_parent)


def solution(mesh):
    in_specs = (
        P(("group", "cluster"), None),
        P(("group", "cluster")),
        P(("group", "cluster"), None, None),
        P(("group", "cluster"), None, None),
        P(("group", "cluster"), None, None),
        P(("group", "cluster")),
        P(("group", "cluster")),
        P(("group", "cluster"), None),
        P(("group", "cluster"), None, None),
        P(("group", "cluster")),
        P(("group", "cluster"), None),
        P(("group", "cluster"), None, None),
        P("group", None),
        P("group", None, None),
    )
    out_specs = P(("group", "cluster"), None)
    sizes = (mesh.shape["group"], mesh.shape["cluster"])
    return jax.shard_map(functools.partial(body, sizes), mesh=mesh, in_specs=in_specs, out_specs=out_specs, check_vma=False)
```

```python
import functools
import math

import jax
import jax.numpy as jnp
from jax import lax
from jax.experimental import pallas as pl
from jax.experimental.pallas import tpu as pltpu
from jax.sharding import PartitionSpec as P

exact_mode = lax.Precision.HIGHEST


def couple(coupling, coef, index):
    stacked = jnp.take(coef, index, axis=0, mode="fill", fill_value=0.0)
    stacked = stacked.reshape(index.shape[0], index.shape[1] * coef.shape[1], coef.shape[2])
    return jnp.einsum("nkq,nqp->nkp", coupling, stacked, precision=exact_mode)


def couple_kernel(nb, listed, total, idx_ref, arrived_ref, coupling_ref, out_ref):
    i = pl.program_id(0)
    rank = arrived_ref.shape[1]
    for t in range(nb):
        acc = jnp.zeros(out_ref.shape[1:], jnp.float32)
        for k in range(listed):
            r = idx_ref[(i * nb + t) * listed + k]
            valid = r < total
            blk = arrived_ref[jnp.minimum(r, total - 1)]
            c = coupling_ref[t, :, k * rank : (k + 1) * rank]
            prod = jnp.dot(c, blk, precision=exact_mode, preferred_element_type=jnp.float32)
            acc = acc + jnp.where(valid, prod, 0.0)
        out_ref[t] = acc


def couple_pallas(coupling, arrived, rows, nb):
    n, rank, width = coupling.shape
    listed = rows.shape[1]
    total, _, ports = arrived.shape
    grid_spec = pltpu.PrefetchScalarGridSpec(
        num_scalar_prefetch=1,
        grid=(n // nb,),
        in_specs=[
            pl.BlockSpec(
                (total, rank, ports), lambda i, idx: (0, 0, 0), pipeline_mode=pl.Buffered(1)
            ),
            pl.BlockSpec((nb, rank, width), lambda i, idx: (i, 0, 0)),
        ],
        out_specs=pl.BlockSpec((nb, rank, ports), lambda i, idx: (i, 0, 0)),
    )
    return pl.pallas_call(
        functools.partial(couple_kernel, nb, listed, total),
        grid_spec=grid_spec,
        out_shape=jax.ShapeDtypeStruct((n, rank, ports), jnp.float32),
        compiler_params=pltpu.CompilerParams(vmem_limit_bytes=60 * 1024 * 1024),
        cost_estimate=pl.CostEstimate(
            flops=2 * n * rank * width * ports,
            bytes_accessed=4 * (n * rank * width + total * rank * ports + n * rank * ports),
            transcendentals=0,
        ),
    )(rows.reshape(-1), arrived, coupling)


def payload_kernel(chunk, size_ref, parent_ref, send_leaf_ref, send_mid_ref, charges_ref, basis_ref,
                   transfer_ref, mid_transfer_ref, out_ref, top_ref, leaf_sc, mid_sc):
    i = pl.program_id(0)
    leaves, rank, points = basis_ref.shape
    mids = mid_transfer_ref.shape[0]

    @pl.when(i == 0)
    def _():
        mid_sc[...] = jnp.zeros(mid_sc.shape, jnp.float32)
        rows = lax.broadcasted_iota(jnp.int32, (points, 1), 0)
        for l in range(leaves):
            blk = charges_ref[l * points:(l + 1) * points, :]
            blk = jnp.where(rows < size_ref[l], blk, 0.0)
            coef = jnp.dot(basis_ref[l], blk, precision=exact_mode, preferred_element_type=jnp.float32)
            leaf_sc[l] = coef
            up = jnp.dot(transfer_ref[l], coef, precision=exact_mode, preferred_element_type=jnp.float32)
            p = parent_ref[l]
            mid_sc[p] = mid_sc[p] + up
        top = jnp.zeros(top_ref.shape, jnp.float32)
        for c in range(mids):
            top = top + jnp.dot(mid_transfer_ref[c], mid_sc[c], precision=exact_mode,
                                preferred_element_type=jnp.float32)
        top_ref[...] = top

    per = chunk // 4
    for q in range(per):
        r = i * per + q
        for j in range(2):
            a = send_leaf_ref[r * 2 + j]
            out_ref[q * 4 + j] = jnp.where(a < leaves, leaf_sc[jnp.minimum(a, leaves - 1)], 0.0)
            b = send_mid_ref[r * 2 + j]
            out_ref[q * 4 + 2 + j] = jnp.where(b < mids, mid_sc[jnp.minimum(b, mids - 1)], 0.0)

def build_payload(charges, leaf_size, leaf_parent, send_leaf, send_mid, leaf_basis, leaf_transfer, mid_transfer, steps=8):
    leaves, rank, points = leaf_basis.shape
    ports = charges.shape[1]
    mids = mid_transfer.shape[0]
    owners = send_leaf.shape[0] // 2
    total = owners * 4
    chunk = total // steps
    full = lambda shape: pl.BlockSpec(shape, lambda i, *_: (0,) * len(shape), pipeline_mode=pl.Buffered(1))
    grid_spec = pltpu.PrefetchScalarGridSpec(
        num_scalar_prefetch=4,
        grid=(steps,),
        in_specs=[full(charges.shape), full(leaf_basis.shape), full(leaf_transfer.shape), full(mid_transfer.shape)],
        out_specs=[pl.BlockSpec((chunk, rank, ports), lambda i, *_: (i, 0, 0)),
                   pl.BlockSpec((rank, ports), lambda i, *_: (0, 0))],
        scratch_shapes=[pltpu.VMEM((leaves, rank, ports), jnp.float32), pltpu.VMEM((mids, rank, ports), jnp.float32)],
    )
    return pl.pallas_call(
        functools.partial(payload_kernel, chunk),
        grid_spec=grid_spec,
        out_shape=[jax.ShapeDtypeStruct((total, rank, ports), jnp.float32), jax.ShapeDtypeStruct((rank, ports), jnp.float32)],
        compiler_params=pltpu.CompilerParams(vmem_limit_bytes=60 * 1024 * 1024, dimension_semantics=("arbitrary",)),
        cost_estimate=pl.CostEstimate(flops=2 * leaves * rank * points * ports, bytes_accessed=4 * (charges.size + leaf_basis.size + total * rank * ports), transcendentals=0),
    )(leaf_size, leaf_parent, send_leaf, send_mid, charges, leaf_basis, leaf_transfer, mid_transfer)

def far_kernel(nb, size_ref, parent_ref, near_ref, transfer_ref, basis_ref, down_mid_ref, out_ref):
    i = pl.program_id(0)
    rank = near_ref.shape[1]
    points = basis_ref.shape[2]
    rows = lax.broadcasted_iota(jnp.int32, (points, 1), 0)
    tdims = (((0,), (0,)), ((), ()))
    for t in range(nb):
        l = i * nb + t
        p = parent_ref[l]
        dm = down_mid_ref[p]
        dl = near_ref[t] + lax.dot_general(transfer_ref[t], dm, tdims, precision=exact_mode, preferred_element_type=jnp.float32)
        far = lax.dot_general(basis_ref[t], dl, tdims, precision=exact_mode, preferred_element_type=jnp.float32)
        out_ref[t * points:(t + 1) * points, :] = jnp.where(rows < size_ref[l], far, 0.0)

def far_field_pallas(near_leaf, leaf_transfer, leaf_basis, down_mid, leaf_size, leaf_parent, nb=8):
    leaves, rank, points = leaf_basis.shape
    ports = near_leaf.shape[2]
    grid_spec = pltpu.PrefetchScalarGridSpec(
        num_scalar_prefetch=2,
        grid=(leaves // nb,),
        in_specs=[pl.BlockSpec((nb, rank, ports), lambda i, *_: (i, 0, 0)),
                  pl.BlockSpec((nb, rank, rank), lambda i, *_: (i, 0, 0)),
                  pl.BlockSpec((nb, rank, points), lambda i, *_: (i, 0, 0)),
                  pl.BlockSpec(down_mid.shape, lambda i, *_: (0, 0, 0))],
        out_specs=pl.BlockSpec((nb * points, ports), lambda i, *_: (i, 0)),
    )
    return pl.pallas_call(
        functools.partial(far_kernel, nb),
        grid_spec=grid_spec,
        out_shape=jax.ShapeDtypeStruct((leaves * points, ports), jnp.float32),
        compiler_params=pltpu.CompilerParams(vmem_limit_bytes=60 * 1024 * 1024),
        cost_estimate=pl.CostEstimate(flops=2 * leaves * rank * points * ports, bytes_accessed=4 * (leaf_basis.size + 2 * leaves * points * ports), transcendentals=0),
    )(leaf_size, leaf_parent, near_leaf, leaf_transfer, leaf_basis, down_mid)


def exchange_kernel(axes, sizes, payload_ref, landing_ref, send_sem, recv_sem, local_sem):
    outer, inner = sizes
    count = outer * inner
    me = lax.axis_index(axes[0]) * inner + lax.axis_index(axes[1])
    barrier = pltpu.get_barrier_semaphore()

    def greet(q, carry):
        peer = lax.rem(me + q, count)
        pl.semaphore_signal(barrier, 1, device_id=(peer // inner, peer % inner),
                            device_id_type=pl.DeviceIdType.MESH)
        return carry

    lax.fori_loop(1, count, greet, 0)
    pl.semaphore_wait(barrier, count - 1)

    stride = 37 if math.gcd(37, count) == 1 else 1

    def send(k, carry):
        peer = lax.rem(me + lax.rem(k * stride, count), count)
        pltpu.make_async_remote_copy(
            src_ref=payload_ref.at[peer],
            dst_ref=landing_ref.at[me],
            send_sem=send_sem,
            recv_sem=recv_sem,
            device_id=(peer // inner, peer % inner),
            device_id_type=pl.DeviceIdType.MESH,
        ).start()
        return carry

    lax.fori_loop(1, count, send, 0)
    own = pltpu.make_async_copy(payload_ref.at[me], landing_ref.at[me], local_sem)
    own.start()
    own.wait()
    everything = pltpu.make_async_remote_copy(
        src_ref=payload_ref.at[pl.ds(0, count - 1)],
        dst_ref=landing_ref.at[pl.ds(0, count - 1)],
        send_sem=send_sem,
        recv_sem=recv_sem,
        device_id=(0, 0),
        device_id_type=pl.DeviceIdType.MESH,
    )
    everything.wait_send()
    everything.wait_recv()

def exchange(payload, axes, sizes):
    return pl.pallas_call(
        functools.partial(exchange_kernel, axes, sizes),
        out_shape=jax.ShapeDtypeStruct(payload.shape, payload.dtype),
        in_specs=[pl.BlockSpec(memory_space=pl.ANY)],
        out_specs=pl.BlockSpec(memory_space=pl.ANY),
        scratch_shapes=[pltpu.SemaphoreType.DMA, pltpu.SemaphoreType.DMA, pltpu.SemaphoreType.DMA],
        compiler_params=pltpu.CompilerParams(collective_id=0, has_side_effects=True),
    )(payload)


def body(
    sizes,
    charges,
    leaf_size,
    leaf_basis,
    leaf_transfer,
    mid_transfer,
    leaf_parent,
    send_leaf,
    pair_leaf,
    leaf_coupling,
    send_mid,
    pair_mid,
    mid_coupling,
    top_pairs,
    top_coupling,
):
    leaf_count, coef_rank, leaf_points = leaf_basis.shape
    port_count = charges.shape[1]
    mid_count = mid_transfer.shape[0]
    owners = send_leaf.shape[0] // 2
    slots = 2
    arrived_rows, coef_top = build_payload(
        charges, leaf_size, leaf_parent, send_leaf, send_mid, leaf_basis, leaf_transfer, mid_transfer
    )
    owners_total = send_leaf.shape[0] // 2
    landing = exchange(
        arrived_rows.reshape((owners_total, -1) + arrived_rows.shape[1:]),
        ("group", "cluster"),
        sizes,
    )
    arrived = landing.reshape(arrived_rows.shape)

    listed = top_pairs.shape[1]
    position = lax.axis_index("cluster")
    wanted = lax.dynamic_slice_in_dim(top_pairs, position, 1, 0)[0]
    own_coupling = lax.dynamic_slice_in_dim(top_coupling, position, 1, 0)[0]
    shard_rows = lax.all_gather(coef_top[None], ("group", "cluster"), axis=0, tiled=True)
    inside = (wanted >= 0) & (wanted < shard_rows.shape[0])
    taken_rows = jnp.take(shard_rows, jnp.clip(wanted, 0, shard_rows.shape[0] - 1), axis=0)
    picked = jnp.where(
        inside[:, None, None], taken_rows, jnp.zeros((listed, coef_rank, port_count), jnp.float32)
    )
    near_top = jnp.einsum(
        "kq,qp->kp",
        own_coupling,
        picked.reshape(listed * coef_rank, port_count),
        precision=exact_mode,
    )

    total_rows = owners * 2 * slots
    live_leaf = pair_leaf < owners * slots
    leaf_rows = jnp.where(live_leaf, pair_leaf + (pair_leaf // slots) * slots, total_rows)
    near_leaf = couple_pallas(leaf_coupling, arrived, leaf_rows, 4)
    live_mid = pair_mid < owners * slots
    mid_rows = jnp.where(live_mid, pair_mid + (pair_mid // slots + 1) * slots, total_rows)
    near_mid = couple_pallas(mid_coupling, arrived, mid_rows, 2)
    down_mid = near_mid + jnp.einsum("mjk,jp->mkp", mid_transfer, near_top, precision=exact_mode)
    return far_field_pallas(near_leaf, leaf_transfer, leaf_basis, down_mid, leaf_size, leaf_parent)


def solution(mesh):
    in_specs = (
        P(("group", "cluster"), None),
        P(("group", "cluster")),
        P(("group", "cluster"), None, None),
        P(("group", "cluster"), None, None),
        P(("group", "cluster"), None, None),
        P(("group", "cluster")),
        P(("group", "cluster")),
        P(("group", "cluster"), None),
        P(("group", "cluster"), None, None),
        P(("group", "cluster")),
        P(("group", "cluster"), None),
        P(("group", "cluster"), None, None),
        P("group", None),
        P("group", None, None),
    )
    out_specs = P(("group", "cluster"), None)
    sizes = (mesh.shape["group"], mesh.shape["cluster"])
    return jax.shard_map(functools.partial(body, sizes), mesh=mesh, in_specs=in_specs, out_specs=out_specs, check_vma=False)
```

```python
import functools
import math

import jax
import jax.numpy as jnp
from jax import lax
from jax.experimental import pallas as pl
from jax.experimental.pallas import tpu as pltpu
from jax.sharding import PartitionSpec as P

exact_mode = lax.Precision.HIGHEST


def couple(coupling, coef, index):
    stacked = jnp.take(coef, index, axis=0, mode="fill", fill_value=0.0)
    stacked = stacked.reshape(index.shape[0], index.shape[1] * coef.shape[1], coef.shape[2])
    return jnp.einsum("nkq,nqp->nkp", coupling, stacked, precision=exact_mode)


def couple_kernel(nb, listed, total, idx_ref, arrived_ref, coupling_ref, out_ref):
    i = pl.program_id(0)
    rank = arrived_ref.shape[1]
    for t in range(nb):
        acc = jnp.zeros(out_ref.shape[1:], jnp.float32)
        for k in range(listed):
            r = idx_ref[(i * nb + t) * listed + k]
            valid = r < total
            blk = arrived_ref[jnp.minimum(r, total - 1)]
            c = coupling_ref[t, :, k * rank : (k + 1) * rank]
            prod = jnp.dot(c, blk, precision=lax.Precision.HIGH, preferred_element_type=jnp.float32)
            acc = acc + jnp.where(valid, prod, 0.0)
        out_ref[t] = acc


def couple_pallas(coupling, arrived, rows, nb):
    n, rank, width = coupling.shape
    listed = rows.shape[1]
    total, _, ports = arrived.shape
    grid_spec = pltpu.PrefetchScalarGridSpec(
        num_scalar_prefetch=1,
        grid=(n // nb,),
        in_specs=[
            pl.BlockSpec(
                (total, rank, ports), lambda i, idx: (0, 0, 0), pipeline_mode=pl.Buffered(1)
            ),
            pl.BlockSpec((nb, rank, width), lambda i, idx: (i, 0, 0)),
        ],
        out_specs=pl.BlockSpec((nb, rank, ports), lambda i, idx: (i, 0, 0)),
    )
    return pl.pallas_call(
        functools.partial(couple_kernel, nb, listed, total),
        grid_spec=grid_spec,
        out_shape=jax.ShapeDtypeStruct((n, rank, ports), jnp.float32),
        compiler_params=pltpu.CompilerParams(vmem_limit_bytes=60 * 1024 * 1024),
        cost_estimate=pl.CostEstimate(
            flops=2 * n * rank * width * ports,
            bytes_accessed=4 * (n * rank * width + total * rank * ports + n * rank * ports),
            transcendentals=0,
        ),
    )(rows.reshape(-1), arrived, coupling)


def payload_kernel(chunk, size_ref, parent_ref, send_leaf_ref, send_mid_ref, charges_ref, basis_ref,
                   transfer_ref, mid_transfer_ref, out_ref, top_ref, leaf_sc, mid_sc):
    i = pl.program_id(0)
    leaves, rank, points = basis_ref.shape
    mids = mid_transfer_ref.shape[0]

    @pl.when(i == 0)
    def _():
        mid_sc[...] = jnp.zeros(mid_sc.shape, jnp.float32)
        rows = lax.broadcasted_iota(jnp.int32, (points, 1), 0)
        for l in range(leaves):
            blk = charges_ref[l * points:(l + 1) * points, :]
            blk = jnp.where(rows < size_ref[l], blk, 0.0)
            coef = jnp.dot(basis_ref[l], blk, precision=exact_mode, preferred_element_type=jnp.float32)
            leaf_sc[l] = coef
            up = jnp.dot(transfer_ref[l], coef, precision=exact_mode, preferred_element_type=jnp.float32)
            p = parent_ref[l]
            mid_sc[p] = mid_sc[p] + up
        top = jnp.zeros(top_ref.shape, jnp.float32)
        for c in range(mids):
            top = top + jnp.dot(mid_transfer_ref[c], mid_sc[c], precision=exact_mode,
                                preferred_element_type=jnp.float32)
        top_ref[...] = top

    per = chunk // 4
    for q in range(per):
        r = i * per + q
        for j in range(2):
            a = send_leaf_ref[r * 2 + j]
            out_ref[q * 4 + j] = jnp.where(a < leaves, leaf_sc[jnp.minimum(a, leaves - 1)], 0.0)
            b = send_mid_ref[r * 2 + j]
            out_ref[q * 4 + 2 + j] = jnp.where(b < mids, mid_sc[jnp.minimum(b, mids - 1)], 0.0)

def build_payload(charges, leaf_size, leaf_parent, send_leaf, send_mid, leaf_basis, leaf_transfer, mid_transfer, steps=8):
    leaves, rank, points = leaf_basis.shape
    ports = charges.shape[1]
    mids = mid_transfer.shape[0]
    owners = send_leaf.shape[0] // 2
    total = owners * 4
    chunk = total // steps
    full = lambda shape: pl.BlockSpec(shape, lambda i, *_: (0,) * len(shape), pipeline_mode=pl.Buffered(1))
    grid_spec = pltpu.PrefetchScalarGridSpec(
        num_scalar_prefetch=4,
        grid=(steps,),
        in_specs=[full(charges.shape), full(leaf_basis.shape), full(leaf_transfer.shape), full(mid_transfer.shape)],
        out_specs=[pl.BlockSpec((chunk, rank, ports), lambda i, *_: (i, 0, 0)),
                   pl.BlockSpec((rank, ports), lambda i, *_: (0, 0))],
        scratch_shapes=[pltpu.VMEM((leaves, rank, ports), jnp.float32), pltpu.VMEM((mids, rank, ports), jnp.float32)],
    )
    return pl.pallas_call(
        functools.partial(payload_kernel, chunk),
        grid_spec=grid_spec,
        out_shape=[jax.ShapeDtypeStruct((total, rank, ports), jnp.float32), jax.ShapeDtypeStruct((rank, ports), jnp.float32)],
        compiler_params=pltpu.CompilerParams(vmem_limit_bytes=60 * 1024 * 1024, dimension_semantics=("arbitrary",)),
        cost_estimate=pl.CostEstimate(flops=2 * leaves * rank * points * ports, bytes_accessed=4 * (charges.size + leaf_basis.size + total * rank * ports), transcendentals=0),
    )(leaf_size, leaf_parent, send_leaf, send_mid, charges, leaf_basis, leaf_transfer, mid_transfer)

def far_kernel(nb, size_ref, parent_ref, near_ref, transfer_ref, basis_ref, down_mid_ref, out_ref):
    i = pl.program_id(0)
    rank = near_ref.shape[1]
    points = basis_ref.shape[2]
    rows = lax.broadcasted_iota(jnp.int32, (points, 1), 0)
    tdims = (((0,), (0,)), ((), ()))
    for t in range(nb):
        l = i * nb + t
        p = parent_ref[l]
        dm = down_mid_ref[p]
        dl = near_ref[t] + lax.dot_general(transfer_ref[t], dm, tdims, precision=exact_mode, preferred_element_type=jnp.float32)
        far = lax.dot_general(basis_ref[t], dl, tdims, precision=exact_mode, preferred_element_type=jnp.float32)
        out_ref[t * points:(t + 1) * points, :] = jnp.where(rows < size_ref[l], far, 0.0)

def far_field_pallas(near_leaf, leaf_transfer, leaf_basis, down_mid, leaf_size, leaf_parent, nb=8):
    leaves, rank, points = leaf_basis.shape
    ports = near_leaf.shape[2]
    grid_spec = pltpu.PrefetchScalarGridSpec(
        num_scalar_prefetch=2,
        grid=(leaves // nb,),
        in_specs=[pl.BlockSpec((nb, rank, ports), lambda i, *_: (i, 0, 0)),
                  pl.BlockSpec((nb, rank, rank), lambda i, *_: (i, 0, 0)),
                  pl.BlockSpec((nb, rank, points), lambda i, *_: (i, 0, 0)),
                  pl.BlockSpec(down_mid.shape, lambda i, *_: (0, 0, 0))],
        out_specs=pl.BlockSpec((nb * points, ports), lambda i, *_: (i, 0)),
    )
    return pl.pallas_call(
        functools.partial(far_kernel, nb),
        grid_spec=grid_spec,
        out_shape=jax.ShapeDtypeStruct((leaves * points, ports), jnp.float32),
        compiler_params=pltpu.CompilerParams(vmem_limit_bytes=60 * 1024 * 1024),
        cost_estimate=pl.CostEstimate(flops=2 * leaves * rank * points * ports, bytes_accessed=4 * (leaf_basis.size + 2 * leaves * points * ports), transcendentals=0),
    )(leaf_size, leaf_parent, near_leaf, leaf_transfer, leaf_basis, down_mid)


def exchange_kernel(axes, sizes, payload_ref, landing_ref, send_sem, recv_sem, local_sem):
    outer, inner = sizes
    count = outer * inner
    me = lax.axis_index(axes[0]) * inner + lax.axis_index(axes[1])
    barrier = pltpu.get_barrier_semaphore()

    def greet(q, carry):
        peer = lax.rem(me + q, count)
        pl.semaphore_signal(barrier, 1, device_id=(peer // inner, peer % inner),
                            device_id_type=pl.DeviceIdType.MESH)
        return carry

    lax.fori_loop(1, count, greet, 0)
    pl.semaphore_wait(barrier, count - 1)

    stride = 37 if math.gcd(37, count) == 1 else 1

    def send(k, carry):
        peer = lax.rem(me + lax.rem(k * stride, count), count)
        pltpu.make_async_remote_copy(
            src_ref=payload_ref.at[peer],
            dst_ref=landing_ref.at[me],
            send_sem=send_sem,
            recv_sem=recv_sem,
            device_id=(peer // inner, peer % inner),
            device_id_type=pl.DeviceIdType.MESH,
        ).start()
        return carry

    lax.fori_loop(1, count, send, 0)
    own = pltpu.make_async_copy(payload_ref.at[me], landing_ref.at[me], local_sem)
    own.start()
    own.wait()
    everything = pltpu.make_async_remote_copy(
        src_ref=payload_ref.at[pl.ds(0, count - 1)],
        dst_ref=landing_ref.at[pl.ds(0, count - 1)],
        send_sem=send_sem,
        recv_sem=recv_sem,
        device_id=(0, 0),
        device_id_type=pl.DeviceIdType.MESH,
    )
    everything.wait_send()
    everything.wait_recv()

def exchange(payload, axes, sizes):
    return pl.pallas_call(
        functools.partial(exchange_kernel, axes, sizes),
        out_shape=jax.ShapeDtypeStruct(payload.shape, payload.dtype),
        in_specs=[pl.BlockSpec(memory_space=pl.ANY)],
        out_specs=pl.BlockSpec(memory_space=pl.ANY),
        scratch_shapes=[pltpu.SemaphoreType.DMA, pltpu.SemaphoreType.DMA, pltpu.SemaphoreType.DMA],
        compiler_params=pltpu.CompilerParams(collective_id=0, has_side_effects=True),
    )(payload)


def body(
    sizes,
    charges,
    leaf_size,
    leaf_basis,
    leaf_transfer,
    mid_transfer,
    leaf_parent,
    send_leaf,
    pair_leaf,
    leaf_coupling,
    send_mid,
    pair_mid,
    mid_coupling,
    top_pairs,
    top_coupling,
):
    leaf_count, coef_rank, leaf_points = leaf_basis.shape
    port_count = charges.shape[1]
    mid_count = mid_transfer.shape[0]
    owners = send_leaf.shape[0] // 2
    slots = 2
    arrived_rows, coef_top = build_payload(
        charges, leaf_size, leaf_parent, send_leaf, send_mid, leaf_basis, leaf_transfer, mid_transfer
    )
    owners_total = send_leaf.shape[0] // 2
    landing = exchange(
        arrived_rows.reshape((owners_total, -1) + arrived_rows.shape[1:]),
        ("group", "cluster"),
        sizes,
    )
    arrived = landing.reshape(arrived_rows.shape)

    listed = top_pairs.shape[1]
    position = lax.axis_index("cluster")
    wanted = lax.dynamic_slice_in_dim(top_pairs, position, 1, 0)[0]
    own_coupling = lax.dynamic_slice_in_dim(top_coupling, position, 1, 0)[0]
    shard_rows = lax.all_gather(coef_top[None], ("group", "cluster"), axis=0, tiled=True)
    inside = (wanted >= 0) & (wanted < shard_rows.shape[0])
    taken_rows = jnp.take(shard_rows, jnp.clip(wanted, 0, shard_rows.shape[0] - 1), axis=0)
    picked = jnp.where(
        inside[:, None, None], taken_rows, jnp.zeros((listed, coef_rank, port_count), jnp.float32)
    )
    near_top = jnp.einsum(
        "kq,qp->kp",
        own_coupling,
        picked.reshape(listed * coef_rank, port_count),
        precision=exact_mode,
    )

    total_rows = owners * 2 * slots
    live_leaf = pair_leaf < owners * slots
    leaf_rows = jnp.where(live_leaf, pair_leaf + (pair_leaf // slots) * slots, total_rows)
    near_leaf = couple_pallas(leaf_coupling, arrived, leaf_rows, 4)
    live_mid = pair_mid < owners * slots
    mid_rows = jnp.where(live_mid, pair_mid + (pair_mid // slots + 1) * slots, total_rows)
    near_mid = couple_pallas(mid_coupling, arrived, mid_rows, 2)
    down_mid = near_mid + jnp.einsum("mjk,jp->mkp", mid_transfer, near_top, precision=exact_mode)
    return far_field_pallas(near_leaf, leaf_transfer, leaf_basis, down_mid, leaf_size, leaf_parent)


def solution(mesh):
    in_specs = (
        P(("group", "cluster"), None),
        P(("group", "cluster")),
        P(("group", "cluster"), None, None),
        P(("group", "cluster"), None, None),
        P(("group", "cluster"), None, None),
        P(("group", "cluster")),
        P(("group", "cluster")),
        P(("group", "cluster"), None),
        P(("group", "cluster"), None, None),
        P(("group", "cluster")),
        P(("group", "cluster"), None),
        P(("group", "cluster"), None, None),
        P("group", None),
        P("group", None, None),
    )
    out_specs = P(("group", "cluster"), None)
    sizes = (mesh.shape["group"], mesh.shape["cluster"])
    return jax.shard_map(functools.partial(body, sizes), mesh=mesh, in_specs=in_specs, out_specs=out_specs, check_vma=False)
```

```python
import functools
import math

import jax
import jax.numpy as jnp
from jax import lax
from jax.experimental import pallas as pl
from jax.experimental.pallas import tpu as pltpu
from jax.sharding import PartitionSpec as P

exact_mode = lax.Precision.HIGHEST


def couple(coupling, coef, index):
    stacked = jnp.take(coef, index, axis=0, mode="fill", fill_value=0.0)
    stacked = stacked.reshape(index.shape[0], index.shape[1] * coef.shape[1], coef.shape[2])
    return jnp.einsum("nkq,nqp->nkp", coupling, stacked, precision=exact_mode)


def couple_kernel(nb, listed, total, idx_ref, arrived_ref, coupling_ref, out_ref):
    i = pl.program_id(0)
    rank = arrived_ref.shape[1]
    for t in range(nb):
        acc = jnp.zeros(out_ref.shape[1:], jnp.float32)
        for k in range(listed):
            r = idx_ref[(i * nb + t) * listed + k]
            valid = r < total
            blk = arrived_ref[jnp.minimum(r, total - 1)]
            c = coupling_ref[t, :, k * rank : (k + 1) * rank]
            prod = jnp.dot(c, blk, precision=lax.Precision.HIGH, preferred_element_type=jnp.float32)
            acc = acc + jnp.where(valid, prod, 0.0)
        out_ref[t] = acc


def couple_pallas(coupling, arrived, rows, nb):
    n, rank, width = coupling.shape
    listed = rows.shape[1]
    total, _, ports = arrived.shape
    grid_spec = pltpu.PrefetchScalarGridSpec(
        num_scalar_prefetch=1,
        grid=(n // nb,),
        in_specs=[
            pl.BlockSpec(
                (total, rank, ports), lambda i, idx: (0, 0, 0), pipeline_mode=pl.Buffered(1)
            ),
            pl.BlockSpec((nb, rank, width), lambda i, idx: (i, 0, 0)),
        ],
        out_specs=pl.BlockSpec((nb, rank, ports), lambda i, idx: (i, 0, 0)),
    )
    return pl.pallas_call(
        functools.partial(couple_kernel, nb, listed, total),
        grid_spec=grid_spec,
        out_shape=jax.ShapeDtypeStruct((n, rank, ports), jnp.float32),
        compiler_params=pltpu.CompilerParams(vmem_limit_bytes=60 * 1024 * 1024),
        cost_estimate=pl.CostEstimate(
            flops=2 * n * rank * width * ports,
            bytes_accessed=4 * (n * rank * width + total * rank * ports + n * rank * ports),
            transcendentals=0,
        ),
    )(rows.reshape(-1), arrived, coupling)


def payload_kernel(chunk, size_ref, parent_ref, send_leaf_ref, send_mid_ref, charges_ref, basis_ref,
                   transfer_ref, mid_transfer_ref, out_ref, mid_out_ref, top_ref, leaf_sc, mid_sc):
    i = pl.program_id(0)
    leaves, rank, points = basis_ref.shape
    mids = mid_transfer_ref.shape[0]

    @pl.when(i == 0)
    def _():
        mid_sc[...] = jnp.zeros(mid_sc.shape, jnp.float32)
        rows = lax.broadcasted_iota(jnp.int32, (points, 1), 0)
        for l in range(leaves):
            blk = charges_ref[l * points:(l + 1) * points, :]
            blk = jnp.where(rows < size_ref[l], blk, 0.0)
            coef = jnp.dot(basis_ref[l], blk, precision=exact_mode, preferred_element_type=jnp.float32)
            leaf_sc[l] = coef
            up = jnp.dot(transfer_ref[l], coef, precision=exact_mode, preferred_element_type=jnp.float32)
            p = parent_ref[l]
            mid_sc[p] = mid_sc[p] + up
        top = jnp.zeros(top_ref.shape, jnp.float32)
        for c in range(mids):
            top = top + jnp.dot(mid_transfer_ref[c], mid_sc[c], precision=exact_mode,
                                preferred_element_type=jnp.float32)
        top_ref[...] = top

    per = chunk // 2
    for q in range(per):
        r = i * per + q
        for j in range(2):
            a = send_leaf_ref[r * 2 + j]
            out_ref[q * 2 + j] = jnp.where(a < leaves, leaf_sc[jnp.minimum(a, leaves - 1)], 0.0)
            b = send_mid_ref[r * 2 + j]
            mid_out_ref[q * 2 + j] = jnp.where(b < mids, mid_sc[jnp.minimum(b, mids - 1)], 0.0)

def build_payload(charges, leaf_size, leaf_parent, send_leaf, send_mid, leaf_basis, leaf_transfer, mid_transfer, steps=8):
    leaves, rank, points = leaf_basis.shape
    ports = charges.shape[1]
    mids = mid_transfer.shape[0]
    owners = send_leaf.shape[0] // 2
    total = owners * 2
    chunk = total // steps
    full = lambda shape: pl.BlockSpec(shape, lambda i, *_: (0,) * len(shape), pipeline_mode=pl.Buffered(1))
    grid_spec = pltpu.PrefetchScalarGridSpec(
        num_scalar_prefetch=4,
        grid=(steps,),
        in_specs=[full(charges.shape), full(leaf_basis.shape), full(leaf_transfer.shape), full(mid_transfer.shape)],
        out_specs=[pl.BlockSpec((chunk, rank, ports), lambda i, *_: (i, 0, 0)),
                   pl.BlockSpec((chunk, rank, ports), lambda i, *_: (i, 0, 0)),
                   pl.BlockSpec((rank, ports), lambda i, *_: (0, 0))],
        scratch_shapes=[pltpu.VMEM((leaves, rank, ports), jnp.float32), pltpu.VMEM((mids, rank, ports), jnp.float32)],
    )
    return pl.pallas_call(
        functools.partial(payload_kernel, chunk),
        grid_spec=grid_spec,
        out_shape=[jax.ShapeDtypeStruct((total, rank, ports), jnp.float32),
                   jax.ShapeDtypeStruct((total, rank, ports), jnp.float32),
                   jax.ShapeDtypeStruct((rank, ports), jnp.float32)],
        compiler_params=pltpu.CompilerParams(vmem_limit_bytes=60 * 1024 * 1024, dimension_semantics=("arbitrary",)),
        cost_estimate=pl.CostEstimate(flops=2 * leaves * rank * points * ports, bytes_accessed=4 * (charges.size + leaf_basis.size + 2 * total * rank * ports), transcendentals=0),
    )(leaf_size, leaf_parent, send_leaf, send_mid, charges, leaf_basis, leaf_transfer, mid_transfer)

def far_kernel(nb, size_ref, parent_ref, near_ref, transfer_ref, basis_ref, down_mid_ref, out_ref):
    i = pl.program_id(0)
    rank = near_ref.shape[1]
    points = basis_ref.shape[2]
    rows = lax.broadcasted_iota(jnp.int32, (points, 1), 0)
    tdims = (((0,), (0,)), ((), ()))
    for t in range(nb):
        l = i * nb + t
        p = parent_ref[l]
        dm = down_mid_ref[p]
        dl = near_ref[t] + lax.dot_general(transfer_ref[t], dm, tdims, precision=exact_mode, preferred_element_type=jnp.float32)
        far = lax.dot_general(basis_ref[t], dl, tdims, precision=exact_mode, preferred_element_type=jnp.float32)
        out_ref[t * points:(t + 1) * points, :] = jnp.where(rows < size_ref[l], far, 0.0)

def far_field_pallas(near_leaf, leaf_transfer, leaf_basis, down_mid, leaf_size, leaf_parent, nb=8):
    leaves, rank, points = leaf_basis.shape
    ports = near_leaf.shape[2]
    grid_spec = pltpu.PrefetchScalarGridSpec(
        num_scalar_prefetch=2,
        grid=(leaves // nb,),
        in_specs=[pl.BlockSpec((nb, rank, ports), lambda i, *_: (i, 0, 0)),
                  pl.BlockSpec((nb, rank, rank), lambda i, *_: (i, 0, 0)),
                  pl.BlockSpec((nb, rank, points), lambda i, *_: (i, 0, 0)),
                  pl.BlockSpec(down_mid.shape, lambda i, *_: (0, 0, 0))],
        out_specs=pl.BlockSpec((nb * points, ports), lambda i, *_: (i, 0)),
    )
    return pl.pallas_call(
        functools.partial(far_kernel, nb),
        grid_spec=grid_spec,
        out_shape=jax.ShapeDtypeStruct((leaves * points, ports), jnp.float32),
        compiler_params=pltpu.CompilerParams(vmem_limit_bytes=60 * 1024 * 1024),
        cost_estimate=pl.CostEstimate(flops=2 * leaves * rank * points * ports, bytes_accessed=4 * (leaf_basis.size + 2 * leaves * points * ports), transcendentals=0),
    )(leaf_size, leaf_parent, near_leaf, leaf_transfer, leaf_basis, down_mid)


def couple_rows(pairs_ref, land_ref, coupling_ref, out_ref, listed):
    total = land_ref.shape[0]
    rank = land_ref.shape[1]

    def target(t, carry):
        acc = jnp.zeros(out_ref.shape[1:], jnp.float32)
        for k in range(listed):
            r = pairs_ref[t * listed + k]
            blk = land_ref[jnp.minimum(r, total - 1)]
            c = coupling_ref[t, :, k * rank : (k + 1) * rank]
            prod = jnp.dot(c, blk, precision=lax.Precision.HIGH, preferred_element_type=jnp.float32)
            acc = acc + jnp.where(r < total, prod, 0.0)
        out_ref[t] = acc
        return carry

    lax.fori_loop(0, out_ref.shape[0], target, 0)


def exchange_couple_kernel(axes, sizes, pair_leaf_ref, pair_mid_ref, leaf_pay_ref, mid_pay_ref,
                           leaf_coupling_ref, mid_coupling_ref, near_leaf_ref, near_mid_ref,
                           leaf_land, mid_land, sems):
    outer, inner = sizes
    count = outer * inner
    me = lax.axis_index(axes[0]) * inner + lax.axis_index(axes[1])
    barrier = pltpu.get_barrier_semaphore()

    def greet(q, carry):
        peer = lax.rem(me + q, count)
        pl.semaphore_signal(barrier, 1, device_id=(peer // inner, peer % inner),
                            device_id_type=pl.DeviceIdType.MESH)
        return carry

    lax.fori_loop(1, count, greet, 0)
    pl.semaphore_wait(barrier, count - 1)
    stride = 37 if math.gcd(37, count) == 1 else 1
    slots = leaf_pay_ref.shape[0] // count

    def sender(pay_ref, land_ref, send_sem, recv_sem):
        def send(k, carry):
            peer = lax.rem(me + lax.rem(k * stride, count), count)
            pltpu.make_async_remote_copy(
                src_ref=pay_ref.at[pl.ds(peer * slots, slots)],
                dst_ref=land_ref.at[pl.ds(me * slots, slots)],
                send_sem=send_sem,
                recv_sem=recv_sem,
                device_id=(peer // inner, peer % inner),
                device_id_type=pl.DeviceIdType.MESH,
            ).start()
            return carry

        lax.fori_loop(1, count, send, 0)

    def everything(pay_ref, land_ref, send_sem, recv_sem):
        return pltpu.make_async_remote_copy(
            src_ref=pay_ref.at[pl.ds(0, (count - 1) * slots)],
            dst_ref=land_ref.at[pl.ds(0, (count - 1) * slots)],
            send_sem=send_sem,
            recv_sem=recv_sem,
            device_id=(0, 0),
            device_id_type=pl.DeviceIdType.MESH,
        )

    sender(leaf_pay_ref, leaf_land, sems.at[0], sems.at[1])
    own_leaf = pltpu.make_async_copy(leaf_pay_ref.at[pl.ds(me * slots, slots)],
                                     leaf_land.at[pl.ds(me * slots, slots)], sems.at[4])
    own_leaf.start()
    sender(mid_pay_ref, mid_land, sems.at[2], sems.at[3])
    own_mid = pltpu.make_async_copy(mid_pay_ref.at[pl.ds(me * slots, slots)],
                                    mid_land.at[pl.ds(me * slots, slots)], sems.at[5])
    own_mid.start()

    leaf_all = everything(leaf_pay_ref, leaf_land, sems.at[0], sems.at[1])
    mid_all = everything(mid_pay_ref, mid_land, sems.at[2], sems.at[3])
    own_leaf.wait()
    leaf_all.wait_recv()
    couple_rows(pair_leaf_ref, leaf_land, leaf_coupling_ref, near_leaf_ref, pair_leaf_ref.shape[0] // near_leaf_ref.shape[0])
    own_mid.wait()
    mid_all.wait_recv()
    couple_rows(pair_mid_ref, mid_land, mid_coupling_ref, near_mid_ref, pair_mid_ref.shape[0] // near_mid_ref.shape[0])
    leaf_all.wait_send()
    mid_all.wait_send()


def exchange_couple(pair_leaf, pair_mid, leaf_pay, mid_pay, leaf_coupling, mid_coupling, axes, sizes):
    rank, ports = leaf_pay.shape[1:]
    n_leaf = leaf_coupling.shape[0]
    n_mid = mid_coupling.shape[0]
    vmem = pl.BlockSpec(memory_space=pltpu.VMEM)
    smem = pl.BlockSpec(memory_space=pltpu.SMEM)
    hbm = pl.BlockSpec(memory_space=pl.ANY)
    return pl.pallas_call(
        functools.partial(exchange_couple_kernel, axes, sizes),
        out_shape=[jax.ShapeDtypeStruct((n_leaf, rank, ports), jnp.float32),
                   jax.ShapeDtypeStruct((n_mid, rank, ports), jnp.float32)],
        in_specs=[smem, smem, hbm, hbm, vmem, vmem],
        out_specs=[vmem, vmem],
        scratch_shapes=[pltpu.VMEM(leaf_pay.shape, jnp.float32), pltpu.VMEM(mid_pay.shape, jnp.float32),
                        pltpu.SemaphoreType.DMA((6,))],
        compiler_params=pltpu.CompilerParams(collective_id=0, has_side_effects=True,
                                             vmem_limit_bytes=62 * 1024 * 1024),
        cost_estimate=pl.CostEstimate(
            flops=2 * (leaf_coupling.size + mid_coupling.size) * ports,
            bytes_accessed=4 * (leaf_pay.size + mid_pay.size + leaf_coupling.size + mid_coupling.size),
            transcendentals=0),
    )(pair_leaf.reshape(-1), pair_mid.reshape(-1), leaf_pay, mid_pay, leaf_coupling, mid_coupling)


def body(
    sizes,
    charges,
    leaf_size,
    leaf_basis,
    leaf_transfer,
    mid_transfer,
    leaf_parent,
    send_leaf,
    pair_leaf,
    leaf_coupling,
    send_mid,
    pair_mid,
    mid_coupling,
    top_pairs,
    top_coupling,
):
    leaf_count, coef_rank, leaf_points = leaf_basis.shape
    port_count = charges.shape[1]
    mid_count = mid_transfer.shape[0]
    owners = send_leaf.shape[0] // 2
    slots = 2
    leaf_pay, mid_pay, coef_top = build_payload(
        charges, leaf_size, leaf_parent, send_leaf, send_mid, leaf_basis, leaf_transfer, mid_transfer
    )
    near_leaf, near_mid = exchange_couple(
        pair_leaf, pair_mid, leaf_pay, mid_pay, leaf_coupling, mid_coupling, ("group", "cluster"), sizes
    )

    listed = top_pairs.shape[1]
    position = lax.axis_index("cluster")
    wanted = lax.dynamic_slice_in_dim(top_pairs, position, 1, 0)[0]
    own_coupling = lax.dynamic_slice_in_dim(top_coupling, position, 1, 0)[0]
    shard_rows = lax.all_gather(coef_top[None], ("group", "cluster"), axis=0, tiled=True)
    inside = (wanted >= 0) & (wanted < shard_rows.shape[0])
    taken_rows = jnp.take(shard_rows, jnp.clip(wanted, 0, shard_rows.shape[0] - 1), axis=0)
    picked = jnp.where(
        inside[:, None, None], taken_rows, jnp.zeros((listed, coef_rank, port_count), jnp.float32)
    )
    near_top = jnp.einsum(
        "kq,qp->kp",
        own_coupling,
        picked.reshape(listed * coef_rank, port_count),
        precision=exact_mode,
    )

    down_mid = near_mid + jnp.einsum("mjk,jp->mkp", mid_transfer, near_top, precision=exact_mode)
    return far_field_pallas(near_leaf, leaf_transfer, leaf_basis, down_mid, leaf_size, leaf_parent)


def solution(mesh):
    in_specs = (
        P(("group", "cluster"), None),
        P(("group", "cluster")),
        P(("group", "cluster"), None, None),
        P(("group", "cluster"), None, None),
        P(("group", "cluster"), None, None),
        P(("group", "cluster")),
        P(("group", "cluster")),
        P(("group", "cluster"), None),
        P(("group", "cluster"), None, None),
        P(("group", "cluster")),
        P(("group", "cluster"), None),
        P(("group", "cluster"), None, None),
        P("group", None),
        P("group", None, None),
    )
    out_specs = P(("group", "cluster"), None)
    sizes = (mesh.shape["group"], mesh.shape["cluster"])
    return jax.shard_map(functools.partial(body, sizes), mesh=mesh, in_specs=in_specs, out_specs=out_specs, check_vma=False)
```

```python
import functools
import math

import jax
import jax.numpy as jnp
from jax import lax
from jax.experimental import pallas as pl
from jax.experimental.pallas import tpu as pltpu
from jax.sharding import PartitionSpec as P

exact_mode = lax.Precision.HIGHEST


def couple(coupling, coef, index):
    stacked = jnp.take(coef, index, axis=0, mode="fill", fill_value=0.0)
    stacked = stacked.reshape(index.shape[0], index.shape[1] * coef.shape[1], coef.shape[2])
    return jnp.einsum("nkq,nqp->nkp", coupling, stacked, precision=exact_mode)


def couple_kernel(nb, listed, total, idx_ref, arrived_ref, coupling_ref, out_ref):
    i = pl.program_id(0)
    rank = arrived_ref.shape[1]
    for t in range(nb):
        acc = jnp.zeros(out_ref.shape[1:], jnp.float32)
        for k in range(listed):
            r = idx_ref[(i * nb + t) * listed + k]
            valid = r < total
            blk = arrived_ref[jnp.minimum(r, total - 1)]
            c = coupling_ref[t, :, k * rank : (k + 1) * rank]
            prod = jnp.dot(c, blk, precision=lax.Precision.HIGH, preferred_element_type=jnp.float32)
            acc = acc + jnp.where(valid, prod, 0.0)
        out_ref[t] = acc


def couple_pallas(coupling, arrived, rows, nb):
    n, rank, width = coupling.shape
    listed = rows.shape[1]
    total, _, ports = arrived.shape
    grid_spec = pltpu.PrefetchScalarGridSpec(
        num_scalar_prefetch=1,
        grid=(n // nb,),
        in_specs=[
            pl.BlockSpec(
                (total, rank, ports), lambda i, idx: (0, 0, 0), pipeline_mode=pl.Buffered(1)
            ),
            pl.BlockSpec((nb, rank, width), lambda i, idx: (i, 0, 0)),
        ],
        out_specs=pl.BlockSpec((nb, rank, ports), lambda i, idx: (i, 0, 0)),
    )
    return pl.pallas_call(
        functools.partial(couple_kernel, nb, listed, total),
        grid_spec=grid_spec,
        out_shape=jax.ShapeDtypeStruct((n, rank, ports), jnp.float32),
        compiler_params=pltpu.CompilerParams(vmem_limit_bytes=60 * 1024 * 1024),
        cost_estimate=pl.CostEstimate(
            flops=2 * n * rank * width * ports,
            bytes_accessed=4 * (n * rank * width + total * rank * ports + n * rank * ports),
            transcendentals=0,
        ),
    )(rows.reshape(-1), arrived, coupling)


def payload_kernel(chunk, size_ref, parent_ref, send_leaf_ref, send_mid_ref, charges_ref, basis_ref,
                   transfer_ref, mid_transfer_ref, out_ref, mid_out_ref, top_ref, leaf_sc, mid_sc):
    i = pl.program_id(0)
    leaves, rank, points = basis_ref.shape
    mids = mid_transfer_ref.shape[0]

    @pl.when(i == 0)
    def _():
        mid_sc[...] = jnp.zeros(mid_sc.shape, jnp.float32)
        rows = lax.broadcasted_iota(jnp.int32, (points, 1), 0)
        for l in range(leaves):
            blk = charges_ref[l * points:(l + 1) * points, :]
            blk = jnp.where(rows < size_ref[l], blk, 0.0)
            coef = jnp.dot(basis_ref[l], blk, precision=exact_mode, preferred_element_type=jnp.float32)
            leaf_sc[l] = coef
            up = jnp.dot(transfer_ref[l], coef, precision=exact_mode, preferred_element_type=jnp.float32)
            p = parent_ref[l]
            mid_sc[p] = mid_sc[p] + up
        top = jnp.zeros(top_ref.shape, jnp.float32)
        for c in range(mids):
            top = top + jnp.dot(mid_transfer_ref[c], mid_sc[c], precision=exact_mode,
                                preferred_element_type=jnp.float32)
        top_ref[...] = top

    per = chunk // 2
    for q in range(per):
        r = i * per + q
        for j in range(2):
            a = send_leaf_ref[r * 2 + j]
            out_ref[q * 2 + j] = jnp.where(a < leaves, leaf_sc[jnp.minimum(a, leaves - 1)], 0.0)
            b = send_mid_ref[r * 2 + j]
            mid_out_ref[q * 2 + j] = jnp.where(b < mids, mid_sc[jnp.minimum(b, mids - 1)], 0.0)

def build_payload(charges, leaf_size, leaf_parent, send_leaf, send_mid, leaf_basis, leaf_transfer, mid_transfer, steps=8):
    leaves, rank, points = leaf_basis.shape
    ports = charges.shape[1]
    mids = mid_transfer.shape[0]
    owners = send_leaf.shape[0] // 2
    total = owners * 2
    chunk = total // steps
    full = lambda shape: pl.BlockSpec(shape, lambda i, *_: (0,) * len(shape), pipeline_mode=pl.Buffered(1))
    grid_spec = pltpu.PrefetchScalarGridSpec(
        num_scalar_prefetch=4,
        grid=(steps,),
        in_specs=[full(charges.shape), full(leaf_basis.shape), full(leaf_transfer.shape), full(mid_transfer.shape)],
        out_specs=[pl.BlockSpec((chunk, rank, ports), lambda i, *_: (i, 0, 0)),
                   pl.BlockSpec((chunk, rank, ports), lambda i, *_: (i, 0, 0)),
                   pl.BlockSpec((rank, ports), lambda i, *_: (0, 0))],
        scratch_shapes=[pltpu.VMEM((leaves, rank, ports), jnp.float32), pltpu.VMEM((mids, rank, ports), jnp.float32)],
    )
    return pl.pallas_call(
        functools.partial(payload_kernel, chunk),
        grid_spec=grid_spec,
        out_shape=[jax.ShapeDtypeStruct((total, rank, ports), jnp.float32),
                   jax.ShapeDtypeStruct((total, rank, ports), jnp.float32),
                   jax.ShapeDtypeStruct((rank, ports), jnp.float32)],
        compiler_params=pltpu.CompilerParams(vmem_limit_bytes=60 * 1024 * 1024, dimension_semantics=("arbitrary",)),
        cost_estimate=pl.CostEstimate(flops=2 * leaves * rank * points * ports, bytes_accessed=4 * (charges.size + leaf_basis.size + 2 * total * rank * ports), transcendentals=0),
    )(leaf_size, leaf_parent, send_leaf, send_mid, charges, leaf_basis, leaf_transfer, mid_transfer)

def far_kernel(nb, size_ref, parent_ref, near_ref, transfer_ref, basis_ref, down_mid_ref, out_ref):
    i = pl.program_id(0)
    rank = near_ref.shape[1]
    points = basis_ref.shape[2]
    rows = lax.broadcasted_iota(jnp.int32, (points, 1), 0)
    tdims = (((0,), (0,)), ((), ()))
    for t in range(nb):
        l = i * nb + t
        p = parent_ref[l]
        dm = down_mid_ref[p]
        dl = near_ref[t] + lax.dot_general(transfer_ref[t], dm, tdims, precision=exact_mode, preferred_element_type=jnp.float32)
        far = lax.dot_general(basis_ref[t], dl, tdims, precision=exact_mode, preferred_element_type=jnp.float32)
        out_ref[t * points:(t + 1) * points, :] = jnp.where(rows < size_ref[l], far, 0.0)

def far_field_pallas(near_leaf, leaf_transfer, leaf_basis, down_mid, leaf_size, leaf_parent, nb=8):
    leaves, rank, points = leaf_basis.shape
    ports = near_leaf.shape[2]
    grid_spec = pltpu.PrefetchScalarGridSpec(
        num_scalar_prefetch=2,
        grid=(leaves // nb,),
        in_specs=[pl.BlockSpec((nb, rank, ports), lambda i, *_: (i, 0, 0)),
                  pl.BlockSpec((nb, rank, rank), lambda i, *_: (i, 0, 0)),
                  pl.BlockSpec((nb, rank, points), lambda i, *_: (i, 0, 0)),
                  pl.BlockSpec(down_mid.shape, lambda i, *_: (0, 0, 0))],
        out_specs=pl.BlockSpec((nb * points, ports), lambda i, *_: (i, 0)),
    )
    return pl.pallas_call(
        functools.partial(far_kernel, nb),
        grid_spec=grid_spec,
        out_shape=jax.ShapeDtypeStruct((leaves * points, ports), jnp.float32),
        compiler_params=pltpu.CompilerParams(vmem_limit_bytes=60 * 1024 * 1024),
        cost_estimate=pl.CostEstimate(flops=2 * leaves * rank * points * ports, bytes_accessed=4 * (leaf_basis.size + 2 * leaves * points * ports), transcendentals=0),
    )(leaf_size, leaf_parent, near_leaf, leaf_transfer, leaf_basis, down_mid)


def couple_rows(pairs_ref, land_ref, coupling_ref, out_ref, listed):
    total = land_ref.shape[0]
    rank = land_ref.shape[1]

    def target(t, carry):
        acc = jnp.zeros(out_ref.shape[1:], jnp.float32)
        for k in range(listed):
            r = pairs_ref[t * listed + k]
            blk = land_ref[jnp.minimum(r, total - 1)]
            c = coupling_ref[t, :, k * rank : (k + 1) * rank]
            prod = jnp.dot(c, blk, precision=lax.Precision.HIGH, preferred_element_type=jnp.float32)
            acc = acc + jnp.where(r < total, prod, 0.0)
        out_ref[t] = acc
        return carry

    lax.fori_loop(0, out_ref.shape[0], target, 0)


def exchange_couple_kernel(axes, sizes, pair_leaf_ref, pair_mid_ref, leaf_pay_ref, mid_pay_ref,
                           leaf_coupling_ref, mid_coupling_ref, near_leaf_ref, near_mid_ref,
                           leaf_land, mid_land, sems):
    outer, inner = sizes
    count = outer * inner
    me = lax.axis_index(axes[0]) * inner + lax.axis_index(axes[1])
    barrier = pltpu.get_barrier_semaphore()

    def greet(q, carry):
        peer = lax.rem(me + q, count)
        pl.semaphore_signal(barrier, 1, device_id=(peer // inner, peer % inner),
                            device_id_type=pl.DeviceIdType.MESH)
        return carry

    lax.fori_loop(1, count, greet, 0)
    pl.semaphore_wait(barrier, count - 1)
    stride = 2 * lax.rem(me * 37, count // 2) + 1 if count % 2 == 0 else 1
    slots = leaf_pay_ref.shape[0] // count

    def sender(pay_ref, land_ref, send_sem, recv_sem):
        def send(k, carry):
            peer = lax.rem(me + lax.rem(k * stride, count), count)
            pltpu.make_async_remote_copy(
                src_ref=pay_ref.at[pl.ds(peer * slots, slots)],
                dst_ref=land_ref.at[pl.ds(me * slots, slots)],
                send_sem=send_sem,
                recv_sem=recv_sem,
                device_id=(peer // inner, peer % inner),
                device_id_type=pl.DeviceIdType.MESH,
            ).start()
            return carry

        lax.fori_loop(1, count, send, 0)

    def everything(pay_ref, land_ref, send_sem, recv_sem):
        return pltpu.make_async_remote_copy(
            src_ref=pay_ref.at[pl.ds(0, (count - 1) * slots)],
            dst_ref=land_ref.at[pl.ds(0, (count - 1) * slots)],
            send_sem=send_sem,
            recv_sem=recv_sem,
            device_id=(0, 0),
            device_id_type=pl.DeviceIdType.MESH,
        )

    sender(leaf_pay_ref, leaf_land, sems.at[0], sems.at[1])
    own_leaf = pltpu.make_async_copy(leaf_pay_ref.at[pl.ds(me * slots, slots)],
                                     leaf_land.at[pl.ds(me * slots, slots)], sems.at[4])
    own_leaf.start()
    sender(mid_pay_ref, mid_land, sems.at[2], sems.at[3])
    own_mid = pltpu.make_async_copy(mid_pay_ref.at[pl.ds(me * slots, slots)],
                                    mid_land.at[pl.ds(me * slots, slots)], sems.at[5])
    own_mid.start()

    leaf_all = everything(leaf_pay_ref, leaf_land, sems.at[0], sems.at[1])
    mid_all = everything(mid_pay_ref, mid_land, sems.at[2], sems.at[3])
    own_leaf.wait()
    leaf_all.wait_recv()
    couple_rows(pair_leaf_ref, leaf_land, leaf_coupling_ref, near_leaf_ref, pair_leaf_ref.shape[0] // near_leaf_ref.shape[0])
    own_mid.wait()
    mid_all.wait_recv()
    couple_rows(pair_mid_ref, mid_land, mid_coupling_ref, near_mid_ref, pair_mid_ref.shape[0] // near_mid_ref.shape[0])
    leaf_all.wait_send()
    mid_all.wait_send()


def exchange_couple(pair_leaf, pair_mid, leaf_pay, mid_pay, leaf_coupling, mid_coupling, axes, sizes):
    rank, ports = leaf_pay.shape[1:]
    n_leaf = leaf_coupling.shape[0]
    n_mid = mid_coupling.shape[0]
    vmem = pl.BlockSpec(memory_space=pltpu.VMEM)
    smem = pl.BlockSpec(memory_space=pltpu.SMEM)
    hbm = pl.BlockSpec(memory_space=pl.ANY)
    return pl.pallas_call(
        functools.partial(exchange_couple_kernel, axes, sizes),
        out_shape=[jax.ShapeDtypeStruct((n_leaf, rank, ports), jnp.float32),
                   jax.ShapeDtypeStruct((n_mid, rank, ports), jnp.float32)],
        in_specs=[smem, smem, hbm, hbm, vmem, vmem],
        out_specs=[vmem, vmem],
        scratch_shapes=[pltpu.VMEM(leaf_pay.shape, jnp.float32), pltpu.VMEM(mid_pay.shape, jnp.float32),
                        pltpu.SemaphoreType.DMA((6,))],
        compiler_params=pltpu.CompilerParams(collective_id=0, has_side_effects=True,
                                             vmem_limit_bytes=62 * 1024 * 1024),
        cost_estimate=pl.CostEstimate(
            flops=2 * (leaf_coupling.size + mid_coupling.size) * ports,
            bytes_accessed=4 * (leaf_pay.size + mid_pay.size + leaf_coupling.size + mid_coupling.size),
            transcendentals=0),
    )(pair_leaf.reshape(-1), pair_mid.reshape(-1), leaf_pay, mid_pay, leaf_coupling, mid_coupling)


def body(
    sizes,
    charges,
    leaf_size,
    leaf_basis,
    leaf_transfer,
    mid_transfer,
    leaf_parent,
    send_leaf,
    pair_leaf,
    leaf_coupling,
    send_mid,
    pair_mid,
    mid_coupling,
    top_pairs,
    top_coupling,
):
    leaf_count, coef_rank, leaf_points = leaf_basis.shape
    port_count = charges.shape[1]
    mid_count = mid_transfer.shape[0]
    owners = send_leaf.shape[0] // 2
    slots = 2
    leaf_pay, mid_pay, coef_top = build_payload(
        charges, leaf_size, leaf_parent, send_leaf, send_mid, leaf_basis, leaf_transfer, mid_transfer
    )
    near_leaf, near_mid = exchange_couple(
        pair_leaf, pair_mid, leaf_pay, mid_pay, leaf_coupling, mid_coupling, ("group", "cluster"), sizes
    )

    listed = top_pairs.shape[1]
    position = lax.axis_index("cluster")
    wanted = lax.dynamic_slice_in_dim(top_pairs, position, 1, 0)[0]
    own_coupling = lax.dynamic_slice_in_dim(top_coupling, position, 1, 0)[0]
    shard_rows = lax.all_gather(coef_top[None], ("group", "cluster"), axis=0, tiled=True)
    inside = (wanted >= 0) & (wanted < shard_rows.shape[0])
    taken_rows = jnp.take(shard_rows, jnp.clip(wanted, 0, shard_rows.shape[0] - 1), axis=0)
    picked = jnp.where(
        inside[:, None, None], taken_rows, jnp.zeros((listed, coef_rank, port_count), jnp.float32)
    )
    near_top = jnp.einsum(
        "kq,qp->kp",
        own_coupling,
        picked.reshape(listed * coef_rank, port_count),
        precision=exact_mode,
    )

    down_mid = near_mid + jnp.einsum("mjk,jp->mkp", mid_transfer, near_top, precision=exact_mode)
    return far_field_pallas(near_leaf, leaf_transfer, leaf_basis, down_mid, leaf_size, leaf_parent)


def solution(mesh):
    in_specs = (
        P(("group", "cluster"), None),
        P(("group", "cluster")),
        P(("group", "cluster"), None, None),
        P(("group", "cluster"), None, None),
        P(("group", "cluster"), None, None),
        P(("group", "cluster")),
        P(("group", "cluster")),
        P(("group", "cluster"), None),
        P(("group", "cluster"), None, None),
        P(("group", "cluster")),
        P(("group", "cluster"), None),
        P(("group", "cluster"), None, None),
        P("group", None),
        P("group", None, None),
    )
    out_specs = P(("group", "cluster"), None)
    sizes = (mesh.shape["group"], mesh.shape["cluster"])
    return jax.shard_map(functools.partial(body, sizes), mesh=mesh, in_specs=in_specs, out_specs=out_specs, check_vma=False)
```

```python
import functools
import math

import jax
import jax.numpy as jnp
from jax import lax
from jax.experimental import pallas as pl
from jax.experimental.pallas import tpu as pltpu
from jax.sharding import PartitionSpec as P

exact_mode = lax.Precision.HIGHEST


def couple(coupling, coef, index):
    stacked = jnp.take(coef, index, axis=0, mode="fill", fill_value=0.0)
    stacked = stacked.reshape(index.shape[0], index.shape[1] * coef.shape[1], coef.shape[2])
    return jnp.einsum("nkq,nqp->nkp", coupling, stacked, precision=exact_mode)


def couple_kernel(nb, listed, total, idx_ref, arrived_ref, coupling_ref, out_ref):
    i = pl.program_id(0)
    rank = arrived_ref.shape[1]
    for t in range(nb):
        acc = jnp.zeros(out_ref.shape[1:], jnp.float32)
        for k in range(listed):
            r = idx_ref[(i * nb + t) * listed + k]
            valid = r < total
            blk = arrived_ref[jnp.minimum(r, total - 1)]
            c = coupling_ref[t, :, k * rank : (k + 1) * rank]
            prod = jnp.dot(c, blk, precision=lax.Precision.HIGH, preferred_element_type=jnp.float32)
            acc = acc + jnp.where(valid, prod, 0.0)
        out_ref[t] = acc


def couple_pallas(coupling, arrived, rows, nb):
    n, rank, width = coupling.shape
    listed = rows.shape[1]
    total, _, ports = arrived.shape
    grid_spec = pltpu.PrefetchScalarGridSpec(
        num_scalar_prefetch=1,
        grid=(n // nb,),
        in_specs=[
            pl.BlockSpec(
                (total, rank, ports), lambda i, idx: (0, 0, 0), pipeline_mode=pl.Buffered(1)
            ),
            pl.BlockSpec((nb, rank, width), lambda i, idx: (i, 0, 0)),
        ],
        out_specs=pl.BlockSpec((nb, rank, ports), lambda i, idx: (i, 0, 0)),
    )
    return pl.pallas_call(
        functools.partial(couple_kernel, nb, listed, total),
        grid_spec=grid_spec,
        out_shape=jax.ShapeDtypeStruct((n, rank, ports), jnp.float32),
        compiler_params=pltpu.CompilerParams(vmem_limit_bytes=60 * 1024 * 1024),
        cost_estimate=pl.CostEstimate(
            flops=2 * n * rank * width * ports,
            bytes_accessed=4 * (n * rank * width + total * rank * ports + n * rank * ports),
            transcendentals=0,
        ),
    )(rows.reshape(-1), arrived, coupling)


def coef_kernel(size_ref, parent_ref, charges_ref, basis_ref, transfer_ref, mid_transfer_ref,
                leaf_ref, mid_ref, top_ref):
    leaves, rank, points = basis_ref.shape
    mids = mid_transfer_ref.shape[0]
    mid_ref[...] = jnp.zeros(mid_ref.shape, jnp.float32)
    rows = lax.broadcasted_iota(jnp.int32, (points, 1), 0)
    for l in range(leaves):
        blk = charges_ref[l * points:(l + 1) * points, :]
        blk = jnp.where(rows < size_ref[l], blk, 0.0)
        coef = jnp.dot(basis_ref[l], blk, precision=exact_mode, preferred_element_type=jnp.float32)
        leaf_ref[l] = coef
        up = jnp.dot(transfer_ref[l], coef, precision=exact_mode, preferred_element_type=jnp.float32)
        p = parent_ref[l]
        mid_ref[p] = mid_ref[p] + up
    top = jnp.zeros(top_ref.shape, jnp.float32)
    for c in range(mids):
        top = top + jnp.dot(mid_transfer_ref[c], mid_ref[c], precision=exact_mode,
                            preferred_element_type=jnp.float32)
    top_ref[...] = top


def build_coefs(charges, leaf_size, leaf_parent, leaf_basis, leaf_transfer, mid_transfer):
    leaves, rank, points = leaf_basis.shape
    ports = charges.shape[1]
    mids = mid_transfer.shape[0]
    vmem = pl.BlockSpec(memory_space=pltpu.VMEM)
    smem = pl.BlockSpec(memory_space=pltpu.SMEM)
    return pl.pallas_call(
        coef_kernel,
        out_shape=[jax.ShapeDtypeStruct((leaves, rank, ports), jnp.float32),
                   jax.ShapeDtypeStruct((mids, rank, ports), jnp.float32),
                   jax.ShapeDtypeStruct((rank, ports), jnp.float32)],
        in_specs=[smem, smem, vmem, vmem, vmem, vmem],
        out_specs=[vmem, vmem, vmem],
        compiler_params=pltpu.CompilerParams(vmem_limit_bytes=60 * 1024 * 1024),
        cost_estimate=pl.CostEstimate(flops=2 * leaves * rank * points * ports,
                                      bytes_accessed=4 * (charges.size + leaf_basis.size),
                                      transcendentals=0),
    )(leaf_size, leaf_parent, charges, leaf_basis, leaf_transfer, mid_transfer)


def far_kernel(nb, size_ref, parent_ref, near_ref, transfer_ref, basis_ref, down_mid_ref, out_ref):
    i = pl.program_id(0)
    rank = near_ref.shape[1]
    points = basis_ref.shape[2]
    rows = lax.broadcasted_iota(jnp.int32, (points, 1), 0)
    tdims = (((0,), (0,)), ((), ()))
    for t in range(nb):
        l = i * nb + t
        p = parent_ref[l]
        dm = down_mid_ref[p]
        dl = near_ref[t] + lax.dot_general(transfer_ref[t], dm, tdims, precision=exact_mode, preferred_element_type=jnp.float32)
        far = lax.dot_general(basis_ref[t], dl, tdims, precision=exact_mode, preferred_element_type=jnp.float32)
        out_ref[t * points:(t + 1) * points, :] = jnp.where(rows < size_ref[l], far, 0.0)

def far_field_pallas(near_leaf, leaf_transfer, leaf_basis, down_mid, leaf_size, leaf_parent, nb=8):
    leaves, rank, points = leaf_basis.shape
    ports = near_leaf.shape[2]
    grid_spec = pltpu.PrefetchScalarGridSpec(
        num_scalar_prefetch=2,
        grid=(leaves // nb,),
        in_specs=[pl.BlockSpec((nb, rank, ports), lambda i, *_: (i, 0, 0)),
                  pl.BlockSpec((nb, rank, rank), lambda i, *_: (i, 0, 0)),
                  pl.BlockSpec((nb, rank, points), lambda i, *_: (i, 0, 0)),
                  pl.BlockSpec(down_mid.shape, lambda i, *_: (0, 0, 0))],
        out_specs=pl.BlockSpec((nb * points, ports), lambda i, *_: (i, 0)),
    )
    return pl.pallas_call(
        functools.partial(far_kernel, nb),
        grid_spec=grid_spec,
        out_shape=jax.ShapeDtypeStruct((leaves * points, ports), jnp.float32),
        compiler_params=pltpu.CompilerParams(vmem_limit_bytes=60 * 1024 * 1024),
        cost_estimate=pl.CostEstimate(flops=2 * leaves * rank * points * ports, bytes_accessed=4 * (leaf_basis.size + 2 * leaves * points * ports), transcendentals=0),
    )(leaf_size, leaf_parent, near_leaf, leaf_transfer, leaf_basis, down_mid)


def couple_rows(pairs_ref, land_ref, coupling_ref, out_ref, listed):
    total = land_ref.shape[0]
    rank = land_ref.shape[1]

    def target(t, carry):
        acc = jnp.zeros(out_ref.shape[1:], jnp.float32)
        for k in range(listed):
            r = pairs_ref[t * listed + k]
            blk = land_ref[jnp.minimum(r, total - 1)]
            c = coupling_ref[t, :, k * rank : (k + 1) * rank]
            prod = jnp.dot(c, blk, precision=lax.Precision.HIGH, preferred_element_type=jnp.float32)
            acc = acc + jnp.where(r < total, prod, 0.0)
        out_ref[t] = acc
        return carry

    lax.fori_loop(0, out_ref.shape[0], target, 0)


def fill_slots(send_ref, coef_ref, pay_ref):
    held = coef_ref.shape[0]

    def fill(i, carry):
        a = send_ref[i]
        pay_ref[i] = jnp.where(a < held, coef_ref[jnp.minimum(a, held - 1)], 0.0)
        return carry

    lax.fori_loop(0, pay_ref.shape[0], fill, 0)


def exchange_couple_kernel(axes, sizes, pair_leaf_ref, pair_mid_ref, send_leaf_ref, send_mid_ref,
                           coef_leaf_ref, coef_mid_ref,
                           leaf_coupling_ref, mid_coupling_ref, near_leaf_ref, near_mid_ref,
                           leaf_pay_ref, mid_pay_ref, leaf_land, mid_land, sems):
    outer, inner = sizes
    count = outer * inner
    me = lax.axis_index(axes[0]) * inner + lax.axis_index(axes[1])
    fill_slots(send_leaf_ref, coef_leaf_ref, leaf_pay_ref)
    fill_slots(send_mid_ref, coef_mid_ref, mid_pay_ref)
    barrier = pltpu.get_barrier_semaphore()

    def greet(q, carry):
        peer = lax.rem(me + q, count)
        pl.semaphore_signal(barrier, 1, device_id=(peer // inner, peer % inner),
                            device_id_type=pl.DeviceIdType.MESH)
        return carry

    lax.fori_loop(1, count, greet, 0)
    pl.semaphore_wait(barrier, count - 1)
    stride = 37 if math.gcd(37, count) == 1 else 1
    slots = leaf_pay_ref.shape[0] // count

    def sender(pay_ref, land_ref, send_sem, recv_sem):
        def send(k, carry):
            peer = lax.rem(me + lax.rem(k * stride, count), count)
            pltpu.make_async_remote_copy(
                src_ref=pay_ref.at[pl.ds(peer * slots, slots)],
                dst_ref=land_ref.at[pl.ds(me * slots, slots)],
                send_sem=send_sem,
                recv_sem=recv_sem,
                device_id=(peer // inner, peer % inner),
                device_id_type=pl.DeviceIdType.MESH,
            ).start()
            return carry

        lax.fori_loop(1, count, send, 0)

    def everything(pay_ref, land_ref, send_sem, recv_sem):
        return pltpu.make_async_remote_copy(
            src_ref=pay_ref.at[pl.ds(0, (count - 1) * slots)],
            dst_ref=land_ref.at[pl.ds(0, (count - 1) * slots)],
            send_sem=send_sem,
            recv_sem=recv_sem,
            device_id=(0, 0),
            device_id_type=pl.DeviceIdType.MESH,
        )

    sender(leaf_pay_ref, leaf_land, sems.at[0], sems.at[1])
    own_leaf = pltpu.make_async_copy(leaf_pay_ref.at[pl.ds(me * slots, slots)],
                                     leaf_land.at[pl.ds(me * slots, slots)], sems.at[4])
    own_leaf.start()
    sender(mid_pay_ref, mid_land, sems.at[2], sems.at[3])
    own_mid = pltpu.make_async_copy(mid_pay_ref.at[pl.ds(me * slots, slots)],
                                    mid_land.at[pl.ds(me * slots, slots)], sems.at[5])
    own_mid.start()

    leaf_all = everything(leaf_pay_ref, leaf_land, sems.at[0], sems.at[1])
    mid_all = everything(mid_pay_ref, mid_land, sems.at[2], sems.at[3])
    own_leaf.wait()
    leaf_all.wait_recv()
    couple_rows(pair_leaf_ref, leaf_land, leaf_coupling_ref, near_leaf_ref, pair_leaf_ref.shape[0] // near_leaf_ref.shape[0])
    own_mid.wait()
    mid_all.wait_recv()
    couple_rows(pair_mid_ref, mid_land, mid_coupling_ref, near_mid_ref, pair_mid_ref.shape[0] // near_mid_ref.shape[0])
    leaf_all.wait_send()
    mid_all.wait_send()


def exchange_couple(pair_leaf, pair_mid, send_leaf, send_mid, coef_leaf, coef_mid, leaf_coupling,
                    mid_coupling, axes, sizes):
    rank, ports = coef_leaf.shape[1:]
    pay_shape = (send_leaf.shape[0], rank, ports)
    n_leaf = leaf_coupling.shape[0]
    n_mid = mid_coupling.shape[0]
    vmem = pl.BlockSpec(memory_space=pltpu.VMEM)
    smem = pl.BlockSpec(memory_space=pltpu.SMEM)
    hbm = pl.BlockSpec(memory_space=pl.ANY)
    return pl.pallas_call(
        functools.partial(exchange_couple_kernel, axes, sizes),
        out_shape=[jax.ShapeDtypeStruct((n_leaf, rank, ports), jnp.float32),
                   jax.ShapeDtypeStruct((n_mid, rank, ports), jnp.float32)],
        in_specs=[smem, smem, smem, smem, vmem, vmem, vmem, vmem],
        out_specs=[vmem, vmem],
        scratch_shapes=[pltpu.VMEM(pay_shape, jnp.float32), pltpu.VMEM(pay_shape, jnp.float32),
                        pltpu.VMEM(pay_shape, jnp.float32), pltpu.VMEM(pay_shape, jnp.float32),
                        pltpu.SemaphoreType.DMA((6,))],
        compiler_params=pltpu.CompilerParams(collective_id=0, has_side_effects=True,
                                             vmem_limit_bytes=62 * 1024 * 1024),
        cost_estimate=pl.CostEstimate(
            flops=2 * (leaf_coupling.size + mid_coupling.size) * ports,
            bytes_accessed=4 * (coef_leaf.size + coef_mid.size + leaf_coupling.size + mid_coupling.size),
            transcendentals=0),
    )(pair_leaf.reshape(-1), pair_mid.reshape(-1), send_leaf, send_mid, coef_leaf, coef_mid,
      leaf_coupling, mid_coupling)


def body(
    sizes,
    charges,
    leaf_size,
    leaf_basis,
    leaf_transfer,
    mid_transfer,
    leaf_parent,
    send_leaf,
    pair_leaf,
    leaf_coupling,
    send_mid,
    pair_mid,
    mid_coupling,
    top_pairs,
    top_coupling,
):
    leaf_count, coef_rank, leaf_points = leaf_basis.shape
    port_count = charges.shape[1]
    mid_count = mid_transfer.shape[0]
    owners = send_leaf.shape[0] // 2
    slots = 2
    coef_leaf, coef_mid, coef_top = build_coefs(
        charges, leaf_size, leaf_parent, leaf_basis, leaf_transfer, mid_transfer
    )
    near_leaf, near_mid = exchange_couple(
        pair_leaf, pair_mid, send_leaf, send_mid, coef_leaf, coef_mid, leaf_coupling, mid_coupling,
        ("group", "cluster"), sizes,
    )

    listed = top_pairs.shape[1]
    position = lax.axis_index("cluster")
    wanted = lax.dynamic_slice_in_dim(top_pairs, position, 1, 0)[0]
    own_coupling = lax.dynamic_slice_in_dim(top_coupling, position, 1, 0)[0]
    shard_rows = lax.all_gather(coef_top[None], ("group", "cluster"), axis=0, tiled=True)
    inside = (wanted >= 0) & (wanted < shard_rows.shape[0])
    taken_rows = jnp.take(shard_rows, jnp.clip(wanted, 0, shard_rows.shape[0] - 1), axis=0)
    picked = jnp.where(
        inside[:, None, None], taken_rows, jnp.zeros((listed, coef_rank, port_count), jnp.float32)
    )
    near_top = jnp.einsum(
        "kq,qp->kp",
        own_coupling,
        picked.reshape(listed * coef_rank, port_count),
        precision=exact_mode,
    )

    down_mid = near_mid + jnp.einsum("mjk,jp->mkp", mid_transfer, near_top, precision=exact_mode)
    return far_field_pallas(near_leaf, leaf_transfer, leaf_basis, down_mid, leaf_size, leaf_parent)


def solution(mesh):
    in_specs = (
        P(("group", "cluster"), None),
        P(("group", "cluster")),
        P(("group", "cluster"), None, None),
        P(("group", "cluster"), None, None),
        P(("group", "cluster"), None, None),
        P(("group", "cluster")),
        P(("group", "cluster")),
        P(("group", "cluster"), None),
        P(("group", "cluster"), None, None),
        P(("group", "cluster")),
        P(("group", "cluster"), None),
        P(("group", "cluster"), None, None),
        P("group", None),
        P("group", None, None),
    )
    out_specs = P(("group", "cluster"), None)
    sizes = (mesh.shape["group"], mesh.shape["cluster"])
    return jax.shard_map(functools.partial(body, sizes), mesh=mesh, in_specs=in_specs, out_specs=out_specs, check_vma=False)
```

```python
import functools
import math

import jax
import jax.numpy as jnp
from jax import lax
from jax.experimental import pallas as pl
from jax.experimental.pallas import tpu as pltpu
from jax.sharding import PartitionSpec as P

exact_mode = lax.Precision.HIGHEST


def couple(coupling, coef, index):
    stacked = jnp.take(coef, index, axis=0, mode="fill", fill_value=0.0)
    stacked = stacked.reshape(index.shape[0], index.shape[1] * coef.shape[1], coef.shape[2])
    return jnp.einsum("nkq,nqp->nkp", coupling, stacked, precision=exact_mode)


def couple_kernel(nb, listed, total, idx_ref, arrived_ref, coupling_ref, out_ref):
    i = pl.program_id(0)
    rank = arrived_ref.shape[1]
    for t in range(nb):
        acc = jnp.zeros(out_ref.shape[1:], jnp.float32)
        for k in range(listed):
            r = idx_ref[(i * nb + t) * listed + k]
            valid = r < total
            blk = arrived_ref[jnp.minimum(r, total - 1)]
            c = coupling_ref[t, :, k * rank : (k + 1) * rank]
            prod = jnp.dot(c, blk, precision=lax.Precision.HIGH, preferred_element_type=jnp.float32)
            acc = acc + jnp.where(valid, prod, 0.0)
        out_ref[t] = acc


def couple_pallas(coupling, arrived, rows, nb):
    n, rank, width = coupling.shape
    listed = rows.shape[1]
    total, _, ports = arrived.shape
    grid_spec = pltpu.PrefetchScalarGridSpec(
        num_scalar_prefetch=1,
        grid=(n // nb,),
        in_specs=[
            pl.BlockSpec(
                (total, rank, ports), lambda i, idx: (0, 0, 0), pipeline_mode=pl.Buffered(1)
            ),
            pl.BlockSpec((nb, rank, width), lambda i, idx: (i, 0, 0)),
        ],
        out_specs=pl.BlockSpec((nb, rank, ports), lambda i, idx: (i, 0, 0)),
    )
    return pl.pallas_call(
        functools.partial(couple_kernel, nb, listed, total),
        grid_spec=grid_spec,
        out_shape=jax.ShapeDtypeStruct((n, rank, ports), jnp.float32),
        compiler_params=pltpu.CompilerParams(vmem_limit_bytes=60 * 1024 * 1024),
        cost_estimate=pl.CostEstimate(
            flops=2 * n * rank * width * ports,
            bytes_accessed=4 * (n * rank * width + total * rank * ports + n * rank * ports),
            transcendentals=0,
        ),
    )(rows.reshape(-1), arrived, coupling)


def coef_kernel(size_ref, parent_ref, charges_ref, basis_ref, transfer_ref, mid_transfer_ref,
                leaf_ref, mid_ref, top_ref):
    leaves, rank, points = basis_ref.shape
    mids = mid_transfer_ref.shape[0]
    mid_ref[...] = jnp.zeros(mid_ref.shape, jnp.float32)
    rows = lax.broadcasted_iota(jnp.int32, (points, 1), 0)
    for l in range(leaves):
        blk = charges_ref[l * points:(l + 1) * points, :]
        blk = jnp.where(rows < size_ref[l], blk, 0.0)
        coef = jnp.dot(basis_ref[l], blk, precision=exact_mode, preferred_element_type=jnp.float32)
        leaf_ref[l] = coef
        up = jnp.dot(transfer_ref[l], coef, precision=exact_mode, preferred_element_type=jnp.float32)
        p = parent_ref[l]
        mid_ref[p] = mid_ref[p] + up
    top = jnp.zeros(top_ref.shape, jnp.float32)
    for c in range(mids):
        top = top + jnp.dot(mid_transfer_ref[c], mid_ref[c], precision=exact_mode,
                            preferred_element_type=jnp.float32)
    top_ref[...] = top


def build_coefs(charges, leaf_size, leaf_parent, leaf_basis, leaf_transfer, mid_transfer):
    leaves, rank, points = leaf_basis.shape
    ports = charges.shape[1]
    mids = mid_transfer.shape[0]
    vmem = pl.BlockSpec(memory_space=pltpu.VMEM)
    smem = pl.BlockSpec(memory_space=pltpu.SMEM)
    return pl.pallas_call(
        coef_kernel,
        out_shape=[jax.ShapeDtypeStruct((leaves, rank, ports), jnp.float32),
                   jax.ShapeDtypeStruct((mids, rank, ports), jnp.float32),
                   jax.ShapeDtypeStruct((rank, ports), jnp.float32)],
        in_specs=[smem, smem, vmem, vmem, vmem, vmem],
        out_specs=[vmem, vmem, vmem],
        compiler_params=pltpu.CompilerParams(vmem_limit_bytes=60 * 1024 * 1024),
        cost_estimate=pl.CostEstimate(flops=2 * leaves * rank * points * ports,
                                      bytes_accessed=4 * (charges.size + leaf_basis.size),
                                      transcendentals=0),
    )(leaf_size, leaf_parent, charges, leaf_basis, leaf_transfer, mid_transfer)


def far_kernel(nb, size_ref, parent_ref, near_ref, transfer_ref, basis_ref, down_mid_ref, out_ref):
    i = pl.program_id(0)
    rank = near_ref.shape[1]
    points = basis_ref.shape[2]
    rows = lax.broadcasted_iota(jnp.int32, (points, 1), 0)
    tdims = (((0,), (0,)), ((), ()))
    for t in range(nb):
        l = i * nb + t
        p = parent_ref[l]
        dm = down_mid_ref[p]
        dl = near_ref[t] + lax.dot_general(transfer_ref[t], dm, tdims, precision=lax.Precision.HIGH, preferred_element_type=jnp.float32)
        far = lax.dot_general(basis_ref[t], dl, tdims, precision=lax.Precision.HIGH, preferred_element_type=jnp.float32)
        out_ref[t * points:(t + 1) * points, :] = jnp.where(rows < size_ref[l], far, 0.0)

def far_field_pallas(near_leaf, leaf_transfer, leaf_basis, down_mid, leaf_size, leaf_parent, nb=8):
    leaves, rank, points = leaf_basis.shape
    ports = near_leaf.shape[2]
    grid_spec = pltpu.PrefetchScalarGridSpec(
        num_scalar_prefetch=2,
        grid=(leaves // nb,),
        in_specs=[pl.BlockSpec((nb, rank, ports), lambda i, *_: (i, 0, 0)),
                  pl.BlockSpec((nb, rank, rank), lambda i, *_: (i, 0, 0)),
                  pl.BlockSpec((nb, rank, points), lambda i, *_: (i, 0, 0)),
                  pl.BlockSpec(down_mid.shape, lambda i, *_: (0, 0, 0))],
        out_specs=pl.BlockSpec((nb * points, ports), lambda i, *_: (i, 0)),
    )
    return pl.pallas_call(
        functools.partial(far_kernel, nb),
        grid_spec=grid_spec,
        out_shape=jax.ShapeDtypeStruct((leaves * points, ports), jnp.float32),
        compiler_params=pltpu.CompilerParams(vmem_limit_bytes=60 * 1024 * 1024),
        cost_estimate=pl.CostEstimate(flops=2 * leaves * rank * points * ports, bytes_accessed=4 * (leaf_basis.size + 2 * leaves * points * ports), transcendentals=0),
    )(leaf_size, leaf_parent, near_leaf, leaf_transfer, leaf_basis, down_mid)


def couple_rows(pairs_ref, land_ref, coupling_ref, out_ref, listed):
    total = land_ref.shape[0]
    rank = land_ref.shape[1]

    def target(t, carry):
        acc = jnp.zeros(out_ref.shape[1:], jnp.float32)
        for k in range(listed):
            r = pairs_ref[t * listed + k]
            blk = land_ref[jnp.minimum(r, total - 1)]
            c = coupling_ref[t, :, k * rank : (k + 1) * rank]
            prod = jnp.dot(c, blk, precision=lax.Precision.HIGH, preferred_element_type=jnp.float32)
            acc = acc + jnp.where(r < total, prod, 0.0)
        out_ref[t] = acc
        return carry

    lax.fori_loop(0, out_ref.shape[0], target, 0)


def fill_slots(send_ref, coef_ref, pay_ref):
    held = coef_ref.shape[0]

    def fill(i, carry):
        a = send_ref[i]
        pay_ref[i] = jnp.where(a < held, coef_ref[jnp.minimum(a, held - 1)], 0.0)
        return carry

    lax.fori_loop(0, pay_ref.shape[0], fill, 0)


def exchange_couple_kernel(axes, sizes, pair_leaf_ref, pair_mid_ref, send_leaf_ref, send_mid_ref,
                           coef_leaf_ref, coef_mid_ref,
                           leaf_coupling_ref, mid_coupling_ref, near_leaf_ref, near_mid_ref,
                           leaf_pay_ref, mid_pay_ref, leaf_land, mid_land, sems):
    outer, inner = sizes
    count = outer * inner
    me = lax.axis_index(axes[0]) * inner + lax.axis_index(axes[1])
    fill_slots(send_leaf_ref, coef_leaf_ref, leaf_pay_ref)
    fill_slots(send_mid_ref, coef_mid_ref, mid_pay_ref)
    barrier = pltpu.get_barrier_semaphore()

    def greet(q, carry):
        peer = lax.rem(me + q, count)
        pl.semaphore_signal(barrier, 1, device_id=(peer // inner, peer % inner),
                            device_id_type=pl.DeviceIdType.MESH)
        return carry

    lax.fori_loop(1, count, greet, 0)
    pl.semaphore_wait(barrier, count - 1)
    stride = 37 if math.gcd(37, count) == 1 else 1
    slots = leaf_pay_ref.shape[0] // count

    def sender(pay_ref, land_ref, send_sem, recv_sem):
        def send(k, carry):
            peer = lax.rem(me + lax.rem(k * stride, count), count)
            pltpu.make_async_remote_copy(
                src_ref=pay_ref.at[pl.ds(peer * slots, slots)],
                dst_ref=land_ref.at[pl.ds(me * slots, slots)],
                send_sem=send_sem,
                recv_sem=recv_sem,
                device_id=(peer // inner, peer % inner),
                device_id_type=pl.DeviceIdType.MESH,
            ).start()
            return carry

        lax.fori_loop(1, count, send, 0)

    def everything(pay_ref, land_ref, send_sem, recv_sem):
        return pltpu.make_async_remote_copy(
            src_ref=pay_ref.at[pl.ds(0, (count - 1) * slots)],
            dst_ref=land_ref.at[pl.ds(0, (count - 1) * slots)],
            send_sem=send_sem,
            recv_sem=recv_sem,
            device_id=(0, 0),
            device_id_type=pl.DeviceIdType.MESH,
        )

    sender(leaf_pay_ref, leaf_land, sems.at[0], sems.at[1])
    own_leaf = pltpu.make_async_copy(leaf_pay_ref.at[pl.ds(me * slots, slots)],
                                     leaf_land.at[pl.ds(me * slots, slots)], sems.at[4])
    own_leaf.start()
    sender(mid_pay_ref, mid_land, sems.at[2], sems.at[3])
    own_mid = pltpu.make_async_copy(mid_pay_ref.at[pl.ds(me * slots, slots)],
                                    mid_land.at[pl.ds(me * slots, slots)], sems.at[5])
    own_mid.start()

    leaf_all = everything(leaf_pay_ref, leaf_land, sems.at[0], sems.at[1])
    mid_all = everything(mid_pay_ref, mid_land, sems.at[2], sems.at[3])
    own_leaf.wait()
    leaf_all.wait_recv()
    couple_rows(pair_leaf_ref, leaf_land, leaf_coupling_ref, near_leaf_ref, pair_leaf_ref.shape[0] // near_leaf_ref.shape[0])
    own_mid.wait()
    mid_all.wait_recv()
    couple_rows(pair_mid_ref, mid_land, mid_coupling_ref, near_mid_ref, pair_mid_ref.shape[0] // near_mid_ref.shape[0])
    leaf_all.wait_send()
    mid_all.wait_send()


def exchange_couple(pair_leaf, pair_mid, send_leaf, send_mid, coef_leaf, coef_mid, leaf_coupling,
                    mid_coupling, axes, sizes):
    rank, ports = coef_leaf.shape[1:]
    pay_shape = (send_leaf.shape[0], rank, ports)
    n_leaf = leaf_coupling.shape[0]
    n_mid = mid_coupling.shape[0]
    vmem = pl.BlockSpec(memory_space=pltpu.VMEM)
    smem = pl.BlockSpec(memory_space=pltpu.SMEM)
    hbm = pl.BlockSpec(memory_space=pl.ANY)
    return pl.pallas_call(
        functools.partial(exchange_couple_kernel, axes, sizes),
        out_shape=[jax.ShapeDtypeStruct((n_leaf, rank, ports), jnp.float32),
                   jax.ShapeDtypeStruct((n_mid, rank, ports), jnp.float32)],
        in_specs=[smem, smem, smem, smem, vmem, vmem, vmem, vmem],
        out_specs=[vmem, vmem],
        scratch_shapes=[pltpu.VMEM(pay_shape, jnp.float32), pltpu.VMEM(pay_shape, jnp.float32),
                        pltpu.VMEM(pay_shape, jnp.float32), pltpu.VMEM(pay_shape, jnp.float32),
                        pltpu.SemaphoreType.DMA((6,))],
        compiler_params=pltpu.CompilerParams(collective_id=0, has_side_effects=True,
                                             vmem_limit_bytes=62 * 1024 * 1024),
        cost_estimate=pl.CostEstimate(
            flops=2 * (leaf_coupling.size + mid_coupling.size) * ports,
            bytes_accessed=4 * (coef_leaf.size + coef_mid.size + leaf_coupling.size + mid_coupling.size),
            transcendentals=0),
    )(pair_leaf.reshape(-1), pair_mid.reshape(-1), send_leaf, send_mid, coef_leaf, coef_mid,
      leaf_coupling, mid_coupling)


def body(
    sizes,
    charges,
    leaf_size,
    leaf_basis,
    leaf_transfer,
    mid_transfer,
    leaf_parent,
    send_leaf,
    pair_leaf,
    leaf_coupling,
    send_mid,
    pair_mid,
    mid_coupling,
    top_pairs,
    top_coupling,
):
    leaf_count, coef_rank, leaf_points = leaf_basis.shape
    port_count = charges.shape[1]
    mid_count = mid_transfer.shape[0]
    owners = send_leaf.shape[0] // 2
    slots = 2
    coef_leaf, coef_mid, coef_top = build_coefs(
        charges, leaf_size, leaf_parent, leaf_basis, leaf_transfer, mid_transfer
    )
    near_leaf, near_mid = exchange_couple(
        pair_leaf, pair_mid, send_leaf, send_mid, coef_leaf, coef_mid, leaf_coupling, mid_coupling,
        ("group", "cluster"), sizes,
    )

    listed = top_pairs.shape[1]
    position = lax.axis_index("cluster")
    wanted = lax.dynamic_slice_in_dim(top_pairs, position, 1, 0)[0]
    own_coupling = lax.dynamic_slice_in_dim(top_coupling, position, 1, 0)[0]
    shard_rows = lax.all_gather(coef_top[None], ("group", "cluster"), axis=0, tiled=True)
    inside = (wanted >= 0) & (wanted < shard_rows.shape[0])
    taken_rows = jnp.take(shard_rows, jnp.clip(wanted, 0, shard_rows.shape[0] - 1), axis=0)
    picked = jnp.where(
        inside[:, None, None], taken_rows, jnp.zeros((listed, coef_rank, port_count), jnp.float32)
    )
    near_top = jnp.einsum(
        "kq,qp->kp",
        own_coupling,
        picked.reshape(listed * coef_rank, port_count),
        precision=exact_mode,
    )

    down_mid = near_mid + jnp.einsum("mjk,jp->mkp", mid_transfer, near_top, precision=exact_mode)
    return far_field_pallas(near_leaf, leaf_transfer, leaf_basis, down_mid, leaf_size, leaf_parent)


def solution(mesh):
    in_specs = (
        P(("group", "cluster"), None),
        P(("group", "cluster")),
        P(("group", "cluster"), None, None),
        P(("group", "cluster"), None, None),
        P(("group", "cluster"), None, None),
        P(("group", "cluster")),
        P(("group", "cluster")),
        P(("group", "cluster"), None),
        P(("group", "cluster"), None, None),
        P(("group", "cluster")),
        P(("group", "cluster"), None),
        P(("group", "cluster"), None, None),
        P("group", None),
        P("group", None, None),
    )
    out_specs = P(("group", "cluster"), None)
    sizes = (mesh.shape["group"], mesh.shape["cluster"])
    return jax.shard_map(functools.partial(body, sizes), mesh=mesh, in_specs=in_specs, out_specs=out_specs, check_vma=False)
```

```python
import functools
import math

import jax
import jax.numpy as jnp
from jax import lax
from jax.experimental import pallas as pl
from jax.experimental.pallas import tpu as pltpu
from jax.sharding import PartitionSpec as P

exact_mode = lax.Precision.HIGHEST


def couple(coupling, coef, index):
    stacked = jnp.take(coef, index, axis=0, mode="fill", fill_value=0.0)
    stacked = stacked.reshape(index.shape[0], index.shape[1] * coef.shape[1], coef.shape[2])
    return jnp.einsum("nkq,nqp->nkp", coupling, stacked, precision=exact_mode)


def couple_kernel(nb, listed, total, idx_ref, arrived_ref, coupling_ref, out_ref):
    i = pl.program_id(0)
    rank = arrived_ref.shape[1]
    for t in range(nb):
        acc = jnp.zeros(out_ref.shape[1:], jnp.float32)
        for k in range(listed):
            r = idx_ref[(i * nb + t) * listed + k]
            valid = r < total
            blk = arrived_ref[jnp.minimum(r, total - 1)]
            c = coupling_ref[t, :, k * rank : (k + 1) * rank]
            prod = jnp.dot(c, blk, precision=lax.Precision.HIGH, preferred_element_type=jnp.float32)
            acc = acc + jnp.where(valid, prod, 0.0)
        out_ref[t] = acc


def couple_pallas(coupling, arrived, rows, nb):
    n, rank, width = coupling.shape
    listed = rows.shape[1]
    total, _, ports = arrived.shape
    grid_spec = pltpu.PrefetchScalarGridSpec(
        num_scalar_prefetch=1,
        grid=(n // nb,),
        in_specs=[
            pl.BlockSpec(
                (total, rank, ports), lambda i, idx: (0, 0, 0), pipeline_mode=pl.Buffered(1)
            ),
            pl.BlockSpec((nb, rank, width), lambda i, idx: (i, 0, 0)),
        ],
        out_specs=pl.BlockSpec((nb, rank, ports), lambda i, idx: (i, 0, 0)),
    )
    return pl.pallas_call(
        functools.partial(couple_kernel, nb, listed, total),
        grid_spec=grid_spec,
        out_shape=jax.ShapeDtypeStruct((n, rank, ports), jnp.float32),
        compiler_params=pltpu.CompilerParams(vmem_limit_bytes=60 * 1024 * 1024),
        cost_estimate=pl.CostEstimate(
            flops=2 * n * rank * width * ports,
            bytes_accessed=4 * (n * rank * width + total * rank * ports + n * rank * ports),
            transcendentals=0,
        ),
    )(rows.reshape(-1), arrived, coupling)


def coef_kernel(size_ref, parent_ref, charges_ref, basis_ref, transfer_ref, mid_transfer_ref,
                leaf_ref, mid_ref, top_ref):
    leaves, rank, points = basis_ref.shape
    mids = mid_transfer_ref.shape[0]
    mid_ref[...] = jnp.zeros(mid_ref.shape, jnp.float32)
    rows = lax.broadcasted_iota(jnp.int32, (points, 1), 0)
    for l in range(leaves):
        blk = charges_ref[l * points:(l + 1) * points, :]
        blk = jnp.where(rows < size_ref[l], blk, 0.0)
        coef = jnp.dot(basis_ref[l], blk, precision=exact_mode, preferred_element_type=jnp.float32)
        leaf_ref[l] = coef
        up = jnp.dot(transfer_ref[l], coef, precision=exact_mode, preferred_element_type=jnp.float32)
        p = parent_ref[l]
        mid_ref[p] = mid_ref[p] + up
    top = jnp.zeros(top_ref.shape, jnp.float32)
    for c in range(mids):
        top = top + jnp.dot(mid_transfer_ref[c], mid_ref[c], precision=exact_mode,
                            preferred_element_type=jnp.float32)
    top_ref[...] = top


def build_coefs(charges, leaf_size, leaf_parent, leaf_basis, leaf_transfer, mid_transfer):
    leaves, rank, points = leaf_basis.shape
    ports = charges.shape[1]
    mids = mid_transfer.shape[0]
    vmem = pl.BlockSpec(memory_space=pltpu.VMEM)
    smem = pl.BlockSpec(memory_space=pltpu.SMEM)
    return pl.pallas_call(
        coef_kernel,
        out_shape=[jax.ShapeDtypeStruct((leaves, rank, ports), jnp.float32),
                   jax.ShapeDtypeStruct((mids, rank, ports), jnp.float32),
                   jax.ShapeDtypeStruct((rank, ports), jnp.float32)],
        in_specs=[smem, smem, vmem, vmem, vmem, vmem],
        out_specs=[vmem, vmem, vmem],
        compiler_params=pltpu.CompilerParams(vmem_limit_bytes=60 * 1024 * 1024),
        cost_estimate=pl.CostEstimate(flops=2 * leaves * rank * points * ports,
                                      bytes_accessed=4 * (charges.size + leaf_basis.size),
                                      transcendentals=0),
    )(leaf_size, leaf_parent, charges, leaf_basis, leaf_transfer, mid_transfer)


def far_kernel(nb, listed, coarse, size_ref, parent_ref, wanted_ref, pos_ref, near_ref, transfer_ref,
               basis_ref, near_mid_ref, mid_transfer_ref, top_coupling_ref, *rest):
    row_refs = rest[:listed]
    out_ref = rest[listed]
    down_mid = rest[listed + 1]
    i = pl.program_id(0)
    rank = near_ref.shape[1]
    points = basis_ref.shape[2]
    tdims = (((0,), (0,)), ((), ()))

    @pl.when(i == 0)
    def _():
        near_top = jnp.zeros(near_mid_ref.shape[1:], jnp.float32)
        for k in range(listed):
            c = top_coupling_ref[0, :, k * rank : (k + 1) * rank]
            prod = jnp.dot(c, row_refs[k][0], precision=exact_mode, preferred_element_type=jnp.float32)
            near_top = near_top + jnp.where(wanted_ref[k] < coarse, prod, 0.0)
        for c in range(near_mid_ref.shape[0]):
            down_mid[c] = near_mid_ref[c] + lax.dot_general(
                mid_transfer_ref[c], near_top, tdims, precision=exact_mode,
                preferred_element_type=jnp.float32)

    rows = lax.broadcasted_iota(jnp.int32, (points, 1), 0)
    for t in range(nb):
        l = i * nb + t
        p = parent_ref[l]
        dm = down_mid[p]
        dl = near_ref[t] + lax.dot_general(transfer_ref[t], dm, tdims, precision=lax.Precision.HIGH, preferred_element_type=jnp.float32)
        far = lax.dot_general(basis_ref[t], dl, tdims, precision=lax.Precision.HIGH, preferred_element_type=jnp.float32)
        out_ref[t * points:(t + 1) * points, :] = jnp.where(rows < size_ref[l], far, 0.0)


def far_field_pallas(near_leaf, leaf_transfer, leaf_basis, near_mid, mid_transfer, top_coupling,
                     shard_rows, wanted, position, leaf_size, leaf_parent, nb=8):
    leaves, rank, points = leaf_basis.shape
    ports = near_leaf.shape[2]
    listed = wanted.shape[0]
    coarse = shard_rows.shape[0]

    def row_spec(k):
        return pl.BlockSpec(
            (1, rank, ports), lambda i, s, p, w, q: (jnp.minimum(w[k], coarse - 1), 0, 0)
        )

    grid_spec = pltpu.PrefetchScalarGridSpec(
        num_scalar_prefetch=4,
        grid=(leaves // nb,),
        in_specs=[pl.BlockSpec((nb, rank, ports), lambda i, *_: (i, 0, 0)),
                  pl.BlockSpec((nb, rank, rank), lambda i, *_: (i, 0, 0)),
                  pl.BlockSpec((nb, rank, points), lambda i, *_: (i, 0, 0)),
                  pl.BlockSpec(near_mid.shape, lambda i, *_: (0, 0, 0)),
                  pl.BlockSpec(mid_transfer.shape, lambda i, *_: (0, 0, 0)),
                  pl.BlockSpec((1,) + top_coupling.shape[1:], lambda i, s, p, w, q: (q[0], 0, 0))]
                 + [row_spec(k) for k in range(listed)],
        out_specs=pl.BlockSpec((nb * points, ports), lambda i, *_: (i, 0)),
        scratch_shapes=[pltpu.VMEM(near_mid.shape, jnp.float32)],
    )
    return pl.pallas_call(
        functools.partial(far_kernel, nb, listed, coarse),
        grid_spec=grid_spec,
        out_shape=jax.ShapeDtypeStruct((leaves * points, ports), jnp.float32),
        compiler_params=pltpu.CompilerParams(vmem_limit_bytes=60 * 1024 * 1024,
                                             dimension_semantics=("arbitrary",)),
        cost_estimate=pl.CostEstimate(flops=2 * leaves * rank * points * ports, bytes_accessed=4 * (leaf_basis.size + 2 * leaves * points * ports), transcendentals=0),
    )(leaf_size, leaf_parent, wanted, position, near_leaf, leaf_transfer, leaf_basis, near_mid,
      mid_transfer, top_coupling, *([shard_rows] * listed))


def couple_rows(pairs_ref, land_ref, coupling_ref, out_ref, listed):
    total = land_ref.shape[0]
    rank = land_ref.shape[1]

    def target(t, carry):
        acc = jnp.zeros(out_ref.shape[1:], jnp.float32)
        for k in range(listed):
            r = pairs_ref[t * listed + k]
            blk = land_ref[jnp.minimum(r, total - 1)]
            c = coupling_ref[t, :, k * rank : (k + 1) * rank]
            prod = jnp.dot(c, blk, precision=lax.Precision.HIGH, preferred_element_type=jnp.float32)
            acc = acc + jnp.where(r < total, prod, 0.0)
        out_ref[t] = acc
        return carry

    lax.fori_loop(0, out_ref.shape[0], target, 0)


def fill_slots(send_ref, coef_ref, pay_ref):
    held = coef_ref.shape[0]

    def fill(i, carry):
        a = send_ref[i]
        pay_ref[i] = jnp.where(a < held, coef_ref[jnp.minimum(a, held - 1)], 0.0)
        return carry

    lax.fori_loop(0, pay_ref.shape[0], fill, 0)


def exchange_couple_kernel(axes, sizes, pair_leaf_ref, pair_mid_ref, send_leaf_ref, send_mid_ref,
                           coef_leaf_ref, coef_mid_ref,
                           leaf_coupling_ref, mid_coupling_ref, near_leaf_ref, near_mid_ref,
                           leaf_pay_ref, mid_pay_ref, leaf_land, mid_land, sems):
    outer, inner = sizes
    count = outer * inner
    me = lax.axis_index(axes[0]) * inner + lax.axis_index(axes[1])
    fill_slots(send_leaf_ref, coef_leaf_ref, leaf_pay_ref)
    fill_slots(send_mid_ref, coef_mid_ref, mid_pay_ref)
    barrier = pltpu.get_barrier_semaphore()

    def greet(q, carry):
        peer = lax.rem(me + q, count)
        pl.semaphore_signal(barrier, 1, device_id=(peer // inner, peer % inner),
                            device_id_type=pl.DeviceIdType.MESH)
        return carry

    lax.fori_loop(1, count, greet, 0)
    pl.semaphore_wait(barrier, count - 1)
    stride = 37 if math.gcd(37, count) == 1 else 1
    slots = leaf_pay_ref.shape[0] // count

    def sender(pay_ref, land_ref, send_sem, recv_sem):
        def send(k, carry):
            peer = lax.rem(me + lax.rem(k * stride, count), count)
            pltpu.make_async_remote_copy(
                src_ref=pay_ref.at[pl.ds(peer * slots, slots)],
                dst_ref=land_ref.at[pl.ds(me * slots, slots)],
                send_sem=send_sem,
                recv_sem=recv_sem,
                device_id=(peer // inner, peer % inner),
                device_id_type=pl.DeviceIdType.MESH,
            ).start()
            return carry

        lax.fori_loop(1, count, send, 0)

    def everything(pay_ref, land_ref, send_sem, recv_sem):
        return pltpu.make_async_remote_copy(
            src_ref=pay_ref.at[pl.ds(0, (count - 1) * slots)],
            dst_ref=land_ref.at[pl.ds(0, (count - 1) * slots)],
            send_sem=send_sem,
            recv_sem=recv_sem,
            device_id=(0, 0),
            device_id_type=pl.DeviceIdType.MESH,
        )

    sender(leaf_pay_ref, leaf_land, sems.at[0], sems.at[1])
    own_leaf = pltpu.make_async_copy(leaf_pay_ref.at[pl.ds(me * slots, slots)],
                                     leaf_land.at[pl.ds(me * slots, slots)], sems.at[4])
    own_leaf.start()
    sender(mid_pay_ref, mid_land, sems.at[2], sems.at[3])
    own_mid = pltpu.make_async_copy(mid_pay_ref.at[pl.ds(me * slots, slots)],
                                    mid_land.at[pl.ds(me * slots, slots)], sems.at[5])
    own_mid.start()

    leaf_all = everything(leaf_pay_ref, leaf_land, sems.at[0], sems.at[1])
    mid_all = everything(mid_pay_ref, mid_land, sems.at[2], sems.at[3])
    own_leaf.wait()
    leaf_all.wait_recv()
    couple_rows(pair_leaf_ref, leaf_land, leaf_coupling_ref, near_leaf_ref, pair_leaf_ref.shape[0] // near_leaf_ref.shape[0])
    own_mid.wait()
    mid_all.wait_recv()
    couple_rows(pair_mid_ref, mid_land, mid_coupling_ref, near_mid_ref, pair_mid_ref.shape[0] // near_mid_ref.shape[0])
    leaf_all.wait_send()
    mid_all.wait_send()


def exchange_couple(pair_leaf, pair_mid, send_leaf, send_mid, coef_leaf, coef_mid, leaf_coupling,
                    mid_coupling, axes, sizes):
    rank, ports = coef_leaf.shape[1:]
    pay_shape = (send_leaf.shape[0], rank, ports)
    n_leaf = leaf_coupling.shape[0]
    n_mid = mid_coupling.shape[0]
    vmem = pl.BlockSpec(memory_space=pltpu.VMEM)
    smem = pl.BlockSpec(memory_space=pltpu.SMEM)
    hbm = pl.BlockSpec(memory_space=pl.ANY)
    return pl.pallas_call(
        functools.partial(exchange_couple_kernel, axes, sizes),
        out_shape=[jax.ShapeDtypeStruct((n_leaf, rank, ports), jnp.float32),
                   jax.ShapeDtypeStruct((n_mid, rank, ports), jnp.float32)],
        in_specs=[smem, smem, smem, smem, vmem, vmem, vmem, vmem],
        out_specs=[vmem, vmem],
        scratch_shapes=[pltpu.VMEM(pay_shape, jnp.float32), pltpu.VMEM(pay_shape, jnp.float32),
                        pltpu.VMEM(pay_shape, jnp.float32), pltpu.VMEM(pay_shape, jnp.float32),
                        pltpu.SemaphoreType.DMA((6,))],
        compiler_params=pltpu.CompilerParams(collective_id=0, has_side_effects=True,
                                             vmem_limit_bytes=62 * 1024 * 1024),
        cost_estimate=pl.CostEstimate(
            flops=2 * (leaf_coupling.size + mid_coupling.size) * ports,
            bytes_accessed=4 * (coef_leaf.size + coef_mid.size + leaf_coupling.size + mid_coupling.size),
            transcendentals=0),
    )(pair_leaf.reshape(-1), pair_mid.reshape(-1), send_leaf, send_mid, coef_leaf, coef_mid,
      leaf_coupling, mid_coupling)


def body(
    sizes,
    charges,
    leaf_size,
    leaf_basis,
    leaf_transfer,
    mid_transfer,
    leaf_parent,
    send_leaf,
    pair_leaf,
    leaf_coupling,
    send_mid,
    pair_mid,
    mid_coupling,
    top_pairs,
    top_coupling,
):
    leaf_count, coef_rank, leaf_points = leaf_basis.shape
    port_count = charges.shape[1]
    mid_count = mid_transfer.shape[0]
    owners = send_leaf.shape[0] // 2
    slots = 2
    coef_leaf, coef_mid, coef_top = build_coefs(
        charges, leaf_size, leaf_parent, leaf_basis, leaf_transfer, mid_transfer
    )
    near_leaf, near_mid = exchange_couple(
        pair_leaf, pair_mid, send_leaf, send_mid, coef_leaf, coef_mid, leaf_coupling, mid_coupling,
        ("group", "cluster"), sizes,
    )

    position = lax.axis_index("cluster").astype(jnp.int32).reshape(1)
    wanted = lax.dynamic_slice_in_dim(top_pairs, position[0], 1, 0)[0]
    shard_rows = lax.all_gather(coef_top[None], ("group", "cluster"), axis=0, tiled=True)
    return far_field_pallas(near_leaf, leaf_transfer, leaf_basis, near_mid, mid_transfer, top_coupling,
                            shard_rows, wanted, position, leaf_size, leaf_parent)


def solution(mesh):
    in_specs = (
        P(("group", "cluster"), None),
        P(("group", "cluster")),
        P(("group", "cluster"), None, None),
        P(("group", "cluster"), None, None),
        P(("group", "cluster"), None, None),
        P(("group", "cluster")),
        P(("group", "cluster")),
        P(("group", "cluster"), None),
        P(("group", "cluster"), None, None),
        P(("group", "cluster")),
        P(("group", "cluster"), None),
        P(("group", "cluster"), None, None),
        P("group", None),
        P("group", None, None),
    )
    out_specs = P(("group", "cluster"), None)
    sizes = (mesh.shape["group"], mesh.shape["cluster"])
    return jax.shard_map(functools.partial(body, sizes), mesh=mesh, in_specs=in_specs, out_specs=out_specs, check_vma=False)
```

```python
import functools
import math

import jax
import jax.numpy as jnp
from jax import lax
from jax.experimental import pallas as pl
from jax.experimental.pallas import tpu as pltpu
from jax.sharding import PartitionSpec as P

exact_mode = lax.Precision.HIGHEST


def coef_kernel(size_ref, parent_ref, charges_ref, basis_ref, transfer_ref, mid_transfer_ref,
                leaf_ref, mid_ref, top_ref):
    leaves, rank, points = basis_ref.shape
    mids = mid_transfer_ref.shape[0]
    mid_ref[...] = jnp.zeros(mid_ref.shape, jnp.float32)
    rows = lax.broadcasted_iota(jnp.int32, (points, 1), 0)
    for l in range(leaves):
        blk = charges_ref[l * points:(l + 1) * points, :]
        blk = jnp.where(rows < size_ref[l], blk, 0.0)
        coef = jnp.dot(basis_ref[l], blk, precision=exact_mode, preferred_element_type=jnp.float32)
        leaf_ref[l] = coef
        up = jnp.dot(transfer_ref[l], coef, precision=exact_mode, preferred_element_type=jnp.float32)
        p = parent_ref[l]
        mid_ref[p] = mid_ref[p] + up
    top = jnp.zeros(top_ref.shape, jnp.float32)
    for c in range(mids):
        top = top + jnp.dot(mid_transfer_ref[c], mid_ref[c], precision=exact_mode,
                            preferred_element_type=jnp.float32)
    top_ref[...] = top


def build_coefs(charges, leaf_size, leaf_parent, leaf_basis, leaf_transfer, mid_transfer):
    leaves, rank, points = leaf_basis.shape
    ports = charges.shape[1]
    mids = mid_transfer.shape[0]
    vmem = pl.BlockSpec(memory_space=pltpu.VMEM)
    smem = pl.BlockSpec(memory_space=pltpu.SMEM)
    return pl.pallas_call(
        coef_kernel,
        out_shape=[jax.ShapeDtypeStruct((leaves, rank, ports), jnp.float32),
                   jax.ShapeDtypeStruct((mids, rank, ports), jnp.float32),
                   jax.ShapeDtypeStruct((rank, ports), jnp.float32)],
        in_specs=[smem, smem, vmem, vmem, vmem, vmem],
        out_specs=[vmem, vmem, vmem],
        compiler_params=pltpu.CompilerParams(vmem_limit_bytes=60 * 1024 * 1024),
        cost_estimate=pl.CostEstimate(flops=2 * leaves * rank * points * ports,
                                      bytes_accessed=4 * (charges.size + leaf_basis.size),
                                      transcendentals=0),
    )(leaf_size, leaf_parent, charges, leaf_basis, leaf_transfer, mid_transfer)


def far_kernel(nb, listed, coarse, size_ref, parent_ref, wanted_ref, pos_ref, near_ref, transfer_ref,
               basis_ref, near_mid_ref, mid_transfer_ref, top_coupling_ref, *rest):
    row_refs = rest[:listed]
    out_ref = rest[listed]
    down_mid = rest[listed + 1]
    i = pl.program_id(0)
    rank = near_ref.shape[1]
    points = basis_ref.shape[2]
    tdims = (((0,), (0,)), ((), ()))

    @pl.when(i == 0)
    def _():
        near_top = jnp.zeros(near_mid_ref.shape[1:], jnp.float32)
        for k in range(listed):
            c = top_coupling_ref[0, :, k * rank : (k + 1) * rank]
            prod = jnp.dot(c, row_refs[k][0], precision=exact_mode, preferred_element_type=jnp.float32)
            near_top = near_top + jnp.where(wanted_ref[k] < coarse, prod, 0.0)
        for c in range(near_mid_ref.shape[0]):
            down_mid[c] = near_mid_ref[c] + lax.dot_general(
                mid_transfer_ref[c], near_top, tdims, precision=exact_mode,
                preferred_element_type=jnp.float32)

    rows = lax.broadcasted_iota(jnp.int32, (points, 1), 0)
    for t in range(nb):
        l = i * nb + t
        p = parent_ref[l]
        dm = down_mid[p]
        dl = near_ref[t] + lax.dot_general(transfer_ref[t], dm, tdims, precision=lax.Precision.HIGH, preferred_element_type=jnp.float32)
        far = lax.dot_general(basis_ref[t], dl, tdims, precision=lax.Precision.HIGH, preferred_element_type=jnp.float32)
        out_ref[t * points:(t + 1) * points, :] = jnp.where(rows < size_ref[l], far, 0.0)


def far_field_pallas(near_leaf, leaf_transfer, leaf_basis, near_mid, mid_transfer, top_coupling,
                     shard_rows, wanted, position, leaf_size, leaf_parent, nb=8):
    leaves, rank, points = leaf_basis.shape
    ports = near_leaf.shape[2]
    listed = wanted.shape[0]
    coarse = shard_rows.shape[0]

    def row_spec(k):
        return pl.BlockSpec(
            (1, rank, ports), lambda i, s, p, w, q: (jnp.minimum(w[k], coarse - 1), 0, 0)
        )

    grid_spec = pltpu.PrefetchScalarGridSpec(
        num_scalar_prefetch=4,
        grid=(leaves // nb,),
        in_specs=[pl.BlockSpec((nb, rank, ports), lambda i, *_: (i, 0, 0)),
                  pl.BlockSpec((nb, rank, rank), lambda i, *_: (i, 0, 0)),
                  pl.BlockSpec((nb, rank, points), lambda i, *_: (i, 0, 0)),
                  pl.BlockSpec(near_mid.shape, lambda i, *_: (0, 0, 0)),
                  pl.BlockSpec(mid_transfer.shape, lambda i, *_: (0, 0, 0)),
                  pl.BlockSpec((1,) + top_coupling.shape[1:], lambda i, s, p, w, q: (q[0], 0, 0))]
                 + [row_spec(k) for k in range(listed)],
        out_specs=pl.BlockSpec((nb * points, ports), lambda i, *_: (i, 0)),
        scratch_shapes=[pltpu.VMEM(near_mid.shape, jnp.float32)],
    )
    return pl.pallas_call(
        functools.partial(far_kernel, nb, listed, coarse),
        grid_spec=grid_spec,
        out_shape=jax.ShapeDtypeStruct((leaves * points, ports), jnp.float32),
        compiler_params=pltpu.CompilerParams(vmem_limit_bytes=60 * 1024 * 1024,
                                             dimension_semantics=("arbitrary",)),
        cost_estimate=pl.CostEstimate(flops=2 * leaves * rank * points * ports, bytes_accessed=4 * (leaf_basis.size + 2 * leaves * points * ports), transcendentals=0),
    )(leaf_size, leaf_parent, wanted, position, near_leaf, leaf_transfer, leaf_basis, near_mid,
      mid_transfer, top_coupling, *([shard_rows] * listed))


def couple_rows(pairs_ref, land_ref, coupling_ref, out_ref, listed):
    total = land_ref.shape[0]
    rank = land_ref.shape[1]

    def target(t, carry):
        acc = jnp.zeros(out_ref.shape[1:], jnp.float32)
        for k in range(listed):
            r = pairs_ref[t, k]
            blk = land_ref[jnp.minimum(r, total - 1)]
            c = coupling_ref[t, :, k * rank : (k + 1) * rank]
            prod = jnp.dot(c, blk, precision=lax.Precision.HIGH, preferred_element_type=jnp.float32)
            acc = acc + jnp.where(r < total, prod, 0.0)
        out_ref[t] = acc
        return carry

    lax.fori_loop(0, out_ref.shape[0], target, 0)


def fill_slots(send_ref, coef_ref, pay_ref):
    held = coef_ref.shape[0]

    def fill(i, carry):
        a = send_ref[i]
        pay_ref[i] = jnp.where(a < held, coef_ref[jnp.minimum(a, held - 1)], 0.0)
        return carry

    lax.fori_loop(0, pay_ref.shape[0], fill, 0)


def exchange_couple_kernel(axes, sizes, pair_leaf_ref, pair_mid_ref, send_leaf_ref, send_mid_ref,
                           coef_leaf_ref, coef_mid_ref,
                           leaf_coupling_ref, mid_coupling_ref, near_leaf_ref, near_mid_ref,
                           leaf_pay_ref, mid_pay_ref, leaf_land, mid_land, sems):
    outer, inner = sizes
    count = outer * inner
    me = lax.axis_index(axes[0]) * inner + lax.axis_index(axes[1])
    fill_slots(send_leaf_ref, coef_leaf_ref, leaf_pay_ref)
    fill_slots(send_mid_ref, coef_mid_ref, mid_pay_ref)
    barrier = pltpu.get_barrier_semaphore()

    def greet(q, carry):
        peer = lax.rem(me + q, count)
        pl.semaphore_signal(barrier, 1, device_id=(peer // inner, peer % inner),
                            device_id_type=pl.DeviceIdType.MESH)
        return carry

    lax.fori_loop(1, count, greet, 0)
    pl.semaphore_wait(barrier, count - 1)
    stride = 37 if math.gcd(37, count) == 1 else 1
    slots = leaf_pay_ref.shape[0] // count

    def sender(pay_ref, land_ref, send_sem, recv_sem):
        def send(k, carry):
            peer = lax.rem(me + lax.rem(k * stride, count), count)
            pltpu.make_async_remote_copy(
                src_ref=pay_ref.at[pl.ds(peer * slots, slots)],
                dst_ref=land_ref.at[pl.ds(me * slots, slots)],
                send_sem=send_sem,
                recv_sem=recv_sem,
                device_id=(peer // inner, peer % inner),
                device_id_type=pl.DeviceIdType.MESH,
            ).start()
            return carry

        lax.fori_loop(1, count, send, 0)

    def everything(pay_ref, land_ref, send_sem, recv_sem):
        return pltpu.make_async_remote_copy(
            src_ref=pay_ref.at[pl.ds(0, (count - 1) * slots)],
            dst_ref=land_ref.at[pl.ds(0, (count - 1) * slots)],
            send_sem=send_sem,
            recv_sem=recv_sem,
            device_id=(0, 0),
            device_id_type=pl.DeviceIdType.MESH,
        )

    sender(leaf_pay_ref, leaf_land, sems.at[0], sems.at[1])
    own_leaf = pltpu.make_async_copy(leaf_pay_ref.at[pl.ds(me * slots, slots)],
                                     leaf_land.at[pl.ds(me * slots, slots)], sems.at[4])
    own_leaf.start()
    sender(mid_pay_ref, mid_land, sems.at[2], sems.at[3])
    own_mid = pltpu.make_async_copy(mid_pay_ref.at[pl.ds(me * slots, slots)],
                                    mid_land.at[pl.ds(me * slots, slots)], sems.at[5])
    own_mid.start()

    leaf_all = everything(leaf_pay_ref, leaf_land, sems.at[0], sems.at[1])
    mid_all = everything(mid_pay_ref, mid_land, sems.at[2], sems.at[3])
    own_leaf.wait()
    leaf_all.wait_recv()
    couple_rows(pair_leaf_ref, leaf_land, leaf_coupling_ref, near_leaf_ref, pair_leaf_ref.shape[1])
    own_mid.wait()
    mid_all.wait_recv()
    couple_rows(pair_mid_ref, mid_land, mid_coupling_ref, near_mid_ref, pair_mid_ref.shape[1])
    leaf_all.wait_send()
    mid_all.wait_send()


def exchange_couple(pair_leaf, pair_mid, send_leaf, send_mid, coef_leaf, coef_mid, leaf_coupling,
                    mid_coupling, axes, sizes):
    rank, ports = coef_leaf.shape[1:]
    pay_shape = (send_leaf.shape[0], rank, ports)
    n_leaf = leaf_coupling.shape[0]
    n_mid = mid_coupling.shape[0]
    vmem = pl.BlockSpec(memory_space=pltpu.VMEM)
    smem = pl.BlockSpec(memory_space=pltpu.SMEM)
    hbm = pl.BlockSpec(memory_space=pl.ANY)
    return pl.pallas_call(
        functools.partial(exchange_couple_kernel, axes, sizes),
        out_shape=[jax.ShapeDtypeStruct((n_leaf, rank, ports), jnp.float32),
                   jax.ShapeDtypeStruct((n_mid, rank, ports), jnp.float32)],
        in_specs=[smem, smem, smem, smem, vmem, vmem, vmem, vmem],
        out_specs=[vmem, vmem],
        scratch_shapes=[pltpu.VMEM(pay_shape, jnp.float32), pltpu.VMEM(pay_shape, jnp.float32),
                        pltpu.VMEM(pay_shape, jnp.float32), pltpu.VMEM(pay_shape, jnp.float32),
                        pltpu.SemaphoreType.DMA((6,))],
        compiler_params=pltpu.CompilerParams(collective_id=0, has_side_effects=True,
                                             vmem_limit_bytes=62 * 1024 * 1024),
        cost_estimate=pl.CostEstimate(
            flops=2 * (leaf_coupling.size + mid_coupling.size) * ports,
            bytes_accessed=4 * (coef_leaf.size + coef_mid.size + leaf_coupling.size + mid_coupling.size),
            transcendentals=0),
    )(pair_leaf, pair_mid, send_leaf, send_mid, coef_leaf, coef_mid,
      leaf_coupling, mid_coupling)


def body(
    sizes,
    charges,
    leaf_size,
    leaf_basis,
    leaf_transfer,
    mid_transfer,
    leaf_parent,
    send_leaf,
    pair_leaf,
    leaf_coupling,
    send_mid,
    pair_mid,
    mid_coupling,
    top_pairs,
    top_coupling,
):
    leaf_count, coef_rank, leaf_points = leaf_basis.shape
    port_count = charges.shape[1]
    mid_count = mid_transfer.shape[0]
    owners = send_leaf.shape[0] // 2
    slots = 2
    coef_leaf, coef_mid, coef_top = build_coefs(
        charges, leaf_size, leaf_parent, leaf_basis, leaf_transfer, mid_transfer
    )
    near_leaf, near_mid = exchange_couple(
        pair_leaf, pair_mid, send_leaf, send_mid, coef_leaf, coef_mid, leaf_coupling, mid_coupling,
        ("group", "cluster"), sizes,
    )

    position = lax.axis_index("cluster").astype(jnp.int32).reshape(1)
    wanted = lax.dynamic_slice_in_dim(top_pairs, position[0], 1, 0)[0]
    shard_rows = lax.all_gather(coef_top[None], ("group", "cluster"), axis=0, tiled=True)
    return far_field_pallas(near_leaf, leaf_transfer, leaf_basis, near_mid, mid_transfer, top_coupling,
                            shard_rows, wanted, position, leaf_size, leaf_parent)


def solution(mesh):
    in_specs = (
        P(("group", "cluster"), None),
        P(("group", "cluster")),
        P(("group", "cluster"), None, None),
        P(("group", "cluster"), None, None),
        P(("group", "cluster"), None, None),
        P(("group", "cluster")),
        P(("group", "cluster")),
        P(("group", "cluster"), None),
        P(("group", "cluster"), None, None),
        P(("group", "cluster")),
        P(("group", "cluster"), None),
        P(("group", "cluster"), None, None),
        P("group", None),
        P("group", None, None),
    )
    out_specs = P(("group", "cluster"), None)
    sizes = (mesh.shape["group"], mesh.shape["cluster"])
    return jax.shard_map(functools.partial(body, sizes), mesh=mesh, in_specs=in_specs, out_specs=out_specs, check_vma=False)
```

```python
import functools
import math

import jax
import jax.numpy as jnp
from jax import lax
from jax.experimental import pallas as pl
from jax.experimental.pallas import tpu as pltpu
from jax.sharding import PartitionSpec as P

exact_mode = lax.Precision.HIGHEST


def coef_kernel(size_ref, parent_ref, charges_ref, basis_ref, transfer_ref, mid_transfer_ref,
                leaf_ref, mid_ref, top_ref):
    leaves, rank, points = basis_ref.shape
    mids = mid_transfer_ref.shape[0]
    mid_ref[...] = jnp.zeros(mid_ref.shape, jnp.float32)
    rows = lax.broadcasted_iota(jnp.int32, (points, 1), 0)
    for l in range(leaves):
        blk = charges_ref[l * points:(l + 1) * points, :]
        blk = jnp.where(rows < size_ref[l], blk, 0.0)
        coef = jnp.dot(basis_ref[l], blk, precision=exact_mode, preferred_element_type=jnp.float32)
        leaf_ref[l] = coef
        up = jnp.dot(transfer_ref[l], coef, precision=exact_mode, preferred_element_type=jnp.float32)
        p = parent_ref[l]
        mid_ref[p] = mid_ref[p] + up
    top = jnp.zeros(top_ref.shape, jnp.float32)
    for c in range(mids):
        top = top + jnp.dot(mid_transfer_ref[c], mid_ref[c], precision=exact_mode,
                            preferred_element_type=jnp.float32)
    top_ref[...] = top


def build_coefs(charges, leaf_size, leaf_parent, leaf_basis, leaf_transfer, mid_transfer):
    leaves, rank, points = leaf_basis.shape
    ports = charges.shape[1]
    mids = mid_transfer.shape[0]
    vmem = pl.BlockSpec(memory_space=pltpu.VMEM)
    smem = pl.BlockSpec(memory_space=pltpu.SMEM)
    return pl.pallas_call(
        coef_kernel,
        out_shape=[jax.ShapeDtypeStruct((leaves, rank, ports), jnp.float32),
                   jax.ShapeDtypeStruct((mids, rank, ports), jnp.float32),
                   jax.ShapeDtypeStruct((rank, ports), jnp.float32)],
        in_specs=[smem, smem, vmem, vmem, vmem, vmem],
        out_specs=[vmem, vmem, vmem],
        compiler_params=pltpu.CompilerParams(vmem_limit_bytes=60 * 1024 * 1024),
        cost_estimate=pl.CostEstimate(flops=2 * leaves * rank * points * ports,
                                      bytes_accessed=4 * (charges.size + leaf_basis.size),
                                      transcendentals=0),
    )(leaf_size, leaf_parent, charges, leaf_basis, leaf_transfer, mid_transfer)


def far_kernel(nb, listed, coarse, size_ref, parent_ref, wanted_ref, pos_ref, near_ref, transfer_ref,
               basis_ref, near_mid_ref, mid_transfer_ref, top_coupling_ref, *rest):
    row_refs = rest[:listed]
    out_ref = rest[listed]
    down_mid = rest[listed + 1]
    i = pl.program_id(0)
    rank = near_ref.shape[1]
    points = basis_ref.shape[2]
    tdims = (((0,), (0,)), ((), ()))

    @pl.when(i == 0)
    def _():
        near_top = jnp.zeros(near_mid_ref.shape[1:], jnp.float32)
        for k in range(listed):
            c = top_coupling_ref[0, :, k * rank : (k + 1) * rank]
            prod = jnp.dot(c, row_refs[k][0], precision=exact_mode, preferred_element_type=jnp.float32)
            near_top = near_top + jnp.where(wanted_ref[k] < coarse, prod, 0.0)
        for c in range(near_mid_ref.shape[0]):
            down_mid[c] = near_mid_ref[c] + lax.dot_general(
                mid_transfer_ref[c], near_top, tdims, precision=exact_mode,
                preferred_element_type=jnp.float32)

    rows = lax.broadcasted_iota(jnp.int32, (points, 1), 0)
    for t in range(nb):
        l = i * nb + t
        p = parent_ref[l]
        dm = down_mid[p]
        dl = near_ref[t] + lax.dot_general(transfer_ref[t], dm, tdims, precision=lax.Precision.HIGH, preferred_element_type=jnp.float32)
        far = lax.dot_general(basis_ref[t], dl, tdims, precision=lax.Precision.HIGH, preferred_element_type=jnp.float32)
        out_ref[t * points:(t + 1) * points, :] = jnp.where(rows < size_ref[l], far, 0.0)


def far_field_pallas(near_leaf, leaf_transfer, leaf_basis, near_mid, mid_transfer, top_coupling,
                     shard_rows, wanted, position, leaf_size, leaf_parent, nb=8):
    leaves, rank, points = leaf_basis.shape
    ports = near_leaf.shape[2]
    listed = wanted.shape[0]
    coarse = shard_rows.shape[0]

    def row_spec(k):
        return pl.BlockSpec(
            (1, rank, ports), lambda i, s, p, w, q: (jnp.minimum(w[k], coarse - 1), 0, 0)
        )

    grid_spec = pltpu.PrefetchScalarGridSpec(
        num_scalar_prefetch=4,
        grid=(leaves // nb,),
        in_specs=[pl.BlockSpec((nb, rank, ports), lambda i, *_: (i, 0, 0)),
                  pl.BlockSpec((nb, rank, rank), lambda i, *_: (i, 0, 0)),
                  pl.BlockSpec((nb, rank, points), lambda i, *_: (i, 0, 0)),
                  pl.BlockSpec(near_mid.shape, lambda i, *_: (0, 0, 0)),
                  pl.BlockSpec(mid_transfer.shape, lambda i, *_: (0, 0, 0)),
                  pl.BlockSpec((1,) + top_coupling.shape[1:], lambda i, s, p, w, q: (q[0], 0, 0))]
                 + [row_spec(k) for k in range(listed)],
        out_specs=pl.BlockSpec((nb * points, ports), lambda i, *_: (i, 0)),
        scratch_shapes=[pltpu.VMEM(near_mid.shape, jnp.float32)],
    )
    return pl.pallas_call(
        functools.partial(far_kernel, nb, listed, coarse),
        grid_spec=grid_spec,
        out_shape=jax.ShapeDtypeStruct((leaves * points, ports), jnp.float32),
        compiler_params=pltpu.CompilerParams(vmem_limit_bytes=60 * 1024 * 1024,
                                             dimension_semantics=("arbitrary",)),
        cost_estimate=pl.CostEstimate(flops=2 * leaves * rank * points * ports, bytes_accessed=4 * (leaf_basis.size + 2 * leaves * points * ports), transcendentals=0),
    )(leaf_size, leaf_parent, wanted, position, near_leaf, leaf_transfer, leaf_basis, near_mid,
      mid_transfer, top_coupling, *([shard_rows] * listed))


def couple_rows(pairs_ref, land_ref, coupling_ref, out_ref, listed, keep=None, add=False):
    total = land_ref.shape[0]
    rank = land_ref.shape[1]

    def target(t, carry):
        acc = out_ref[t] if add else jnp.zeros(out_ref.shape[1:], jnp.float32)
        for k in range(listed):
            r = pairs_ref[t, k]
            blk = land_ref[jnp.minimum(r, total - 1)]
            c = coupling_ref[t, :, k * rank : (k + 1) * rank]
            prod = jnp.dot(c, blk, precision=lax.Precision.HIGH, preferred_element_type=jnp.float32)
            live = r < total
            if keep is not None:
                live = live & keep(r)
            acc = acc + jnp.where(live, prod, 0.0)
        out_ref[t] = acc
        return carry

    lax.fori_loop(0, out_ref.shape[0], target, 0)


def fill_slots(send_ref, coef_ref, pay_ref):
    held = coef_ref.shape[0]

    def fill(i, carry):
        a = send_ref[i]
        pay_ref[i] = jnp.where(a < held, coef_ref[jnp.minimum(a, held - 1)], 0.0)
        return carry

    lax.fori_loop(0, pay_ref.shape[0], fill, 0)


def exchange_couple_kernel(axes, sizes, pair_leaf_ref, pair_mid_ref, send_leaf_ref, send_mid_ref,
                           coef_leaf_ref, coef_mid_ref,
                           leaf_coupling_ref, mid_coupling_ref, near_leaf_ref, near_mid_ref,
                           leaf_pay_ref, mid_pay_ref, leaf_land, mid_land, mid_late, sems):
    outer, inner = sizes
    count = outer * inner
    me = lax.axis_index(axes[0]) * inner + lax.axis_index(axes[1])
    fill_slots(send_leaf_ref, coef_leaf_ref, leaf_pay_ref)
    fill_slots(send_mid_ref, coef_mid_ref, mid_pay_ref)
    barrier = pltpu.get_barrier_semaphore()

    def greet(q, carry):
        peer = lax.rem(me + q, count)
        pl.semaphore_signal(barrier, 1, device_id=(peer // inner, peer % inner),
                            device_id_type=pl.DeviceIdType.MESH)
        return carry

    lax.fori_loop(1, count, greet, 0)
    pl.semaphore_wait(barrier, count - 1)
    stride = 37 if math.gcd(37, count) == 1 else 1
    slots = leaf_pay_ref.shape[0] // count

    def sender(pay_ref, land_ref, send_sem, recv_sem, first=1, last=count):
        def send(k, carry):
            peer = lax.rem(me + lax.rem(k * stride, count), count)
            pltpu.make_async_remote_copy(
                src_ref=pay_ref.at[pl.ds(peer * slots, slots)],
                dst_ref=land_ref.at[pl.ds(me * slots, slots)],
                send_sem=send_sem,
                recv_sem=recv_sem,
                device_id=(peer // inner, peer % inner),
                device_id_type=pl.DeviceIdType.MESH,
            ).start()
            return carry

        lax.fori_loop(first, last, send, 0)

    def everything(pay_ref, land_ref, send_sem, recv_sem, copies=count - 1):
        return pltpu.make_async_remote_copy(
            src_ref=pay_ref.at[pl.ds(0, copies * slots)],
            dst_ref=land_ref.at[pl.ds(0, copies * slots)],
            send_sem=send_sem,
            recv_sem=recv_sem,
            device_id=(0, 0),
            device_id_type=pl.DeviceIdType.MESH,
        )

    sender(leaf_pay_ref, leaf_land, sems.at[0], sems.at[1])
    own_leaf = pltpu.make_async_copy(leaf_pay_ref.at[pl.ds(me * slots, slots)],
                                     leaf_land.at[pl.ds(me * slots, slots)], sems.at[4])
    own_leaf.start()
    half = count // 2
    sender(mid_pay_ref, mid_land, sems.at[2], sems.at[3], 1, half)
    sender(mid_pay_ref, mid_late, sems.at[6], sems.at[7], half, count)
    own_mid = pltpu.make_async_copy(mid_pay_ref.at[pl.ds(me * slots, slots)],
                                    mid_land.at[pl.ds(me * slots, slots)], sems.at[5])
    own_mid.start()

    leaf_all = everything(leaf_pay_ref, leaf_land, sems.at[0], sems.at[1])
    early_all = everything(mid_pay_ref, mid_land, sems.at[2], sems.at[3], half - 1)
    late_all = everything(mid_pay_ref, mid_late, sems.at[6], sems.at[7], count - half)
    own_leaf.wait()
    leaf_all.wait_recv()
    couple_rows(pair_leaf_ref, leaf_land, leaf_coupling_ref, near_leaf_ref, pair_leaf_ref.shape[1])
    inverse = pow(stride, -1, count)

    def early(r):
        return lax.rem((me - r // slots + count) * inverse, count) < half

    own_mid.wait()
    early_all.wait_recv()
    couple_rows(pair_mid_ref, mid_land, mid_coupling_ref, near_mid_ref, pair_mid_ref.shape[1], early)
    late_all.wait_recv()
    couple_rows(pair_mid_ref, mid_late, mid_coupling_ref, near_mid_ref, pair_mid_ref.shape[1],
                lambda r: jnp.logical_not(early(r)), True)
    leaf_all.wait_send()
    early_all.wait_send()
    late_all.wait_send()


def exchange_couple(pair_leaf, pair_mid, send_leaf, send_mid, coef_leaf, coef_mid, leaf_coupling,
                    mid_coupling, axes, sizes):
    rank, ports = coef_leaf.shape[1:]
    pay_shape = (send_leaf.shape[0], rank, ports)
    n_leaf = leaf_coupling.shape[0]
    n_mid = mid_coupling.shape[0]
    vmem = pl.BlockSpec(memory_space=pltpu.VMEM)
    smem = pl.BlockSpec(memory_space=pltpu.SMEM)
    hbm = pl.BlockSpec(memory_space=pl.ANY)
    return pl.pallas_call(
        functools.partial(exchange_couple_kernel, axes, sizes),
        out_shape=[jax.ShapeDtypeStruct((n_leaf, rank, ports), jnp.float32),
                   jax.ShapeDtypeStruct((n_mid, rank, ports), jnp.float32)],
        in_specs=[smem, smem, smem, smem, vmem, vmem, vmem, vmem],
        out_specs=[vmem, vmem],
        scratch_shapes=[pltpu.VMEM(pay_shape, jnp.float32), pltpu.VMEM(pay_shape, jnp.float32),
                        pltpu.VMEM(pay_shape, jnp.float32), pltpu.VMEM(pay_shape, jnp.float32),
                        pltpu.VMEM(pay_shape, jnp.float32), pltpu.SemaphoreType.DMA((8,))],
        compiler_params=pltpu.CompilerParams(collective_id=0, has_side_effects=True,
                                             vmem_limit_bytes=62 * 1024 * 1024),
        cost_estimate=pl.CostEstimate(
            flops=2 * (leaf_coupling.size + mid_coupling.size) * ports,
            bytes_accessed=4 * (coef_leaf.size + coef_mid.size + leaf_coupling.size + mid_coupling.size),
            transcendentals=0),
    )(pair_leaf, pair_mid, send_leaf, send_mid, coef_leaf, coef_mid,
      leaf_coupling, mid_coupling)


def body(
    sizes,
    charges,
    leaf_size,
    leaf_basis,
    leaf_transfer,
    mid_transfer,
    leaf_parent,
    send_leaf,
    pair_leaf,
    leaf_coupling,
    send_mid,
    pair_mid,
    mid_coupling,
    top_pairs,
    top_coupling,
):
    leaf_count, coef_rank, leaf_points = leaf_basis.shape
    port_count = charges.shape[1]
    mid_count = mid_transfer.shape[0]
    owners = send_leaf.shape[0] // 2
    slots = 2
    coef_leaf, coef_mid, coef_top = build_coefs(
        charges, leaf_size, leaf_parent, leaf_basis, leaf_transfer, mid_transfer
    )
    near_leaf, near_mid = exchange_couple(
        pair_leaf, pair_mid, send_leaf, send_mid, coef_leaf, coef_mid, leaf_coupling, mid_coupling,
        ("group", "cluster"), sizes,
    )

    position = lax.axis_index("cluster").astype(jnp.int32).reshape(1)
    wanted = lax.dynamic_slice_in_dim(top_pairs, position[0], 1, 0)[0]
    shard_rows = lax.all_gather(coef_top[None], ("group", "cluster"), axis=0, tiled=True)
    return far_field_pallas(near_leaf, leaf_transfer, leaf_basis, near_mid, mid_transfer, top_coupling,
                            shard_rows, wanted, position, leaf_size, leaf_parent)


def solution(mesh):
    in_specs = (
        P(("group", "cluster"), None),
        P(("group", "cluster")),
        P(("group", "cluster"), None, None),
        P(("group", "cluster"), None, None),
        P(("group", "cluster"), None, None),
        P(("group", "cluster")),
        P(("group", "cluster")),
        P(("group", "cluster"), None),
        P(("group", "cluster"), None, None),
        P(("group", "cluster")),
        P(("group", "cluster"), None),
        P(("group", "cluster"), None, None),
        P("group", None),
        P("group", None, None),
    )
    out_specs = P(("group", "cluster"), None)
    sizes = (mesh.shape["group"], mesh.shape["cluster"])
    return jax.shard_map(functools.partial(body, sizes), mesh=mesh, in_specs=in_specs, out_specs=out_specs, check_vma=False)
```

```python
import functools
import math

import jax
import jax.numpy as jnp
from jax import lax
from jax.experimental import pallas as pl
from jax.experimental.pallas import tpu as pltpu
from jax.sharding import PartitionSpec as P

exact_mode = lax.Precision.HIGHEST


def coef_kernel(nb, size_ref, parent_ref, charges_ref, basis_ref, transfer_ref, mid_transfer_ref,
                leaf_ref, mid_ref, top_ref):
    i = pl.program_id(0)
    rank, points = basis_ref.shape[1:]
    mids = mid_transfer_ref.shape[0]

    @pl.when(i == 0)
    def _():
        mid_ref[...] = jnp.zeros(mid_ref.shape, jnp.float32)

    rows = lax.broadcasted_iota(jnp.int32, (points, 1), 0)
    for t in range(nb):
        l = i * nb + t
        blk = charges_ref[t * points:(t + 1) * points, :]
        blk = jnp.where(rows < size_ref[l], blk, 0.0)
        coef = jnp.dot(basis_ref[t], blk, precision=exact_mode, preferred_element_type=jnp.float32)
        leaf_ref[t] = coef
        up = jnp.dot(transfer_ref[t], coef, precision=exact_mode, preferred_element_type=jnp.float32)
        p = parent_ref[l]
        mid_ref[p] = mid_ref[p] + up

    @pl.when(i == pl.num_programs(0) - 1)
    def _():
        top = jnp.zeros(top_ref.shape, jnp.float32)
        for c in range(mids):
            top = top + jnp.dot(mid_transfer_ref[c], mid_ref[c], precision=exact_mode,
                                preferred_element_type=jnp.float32)
        top_ref[...] = top


def build_coefs(charges, leaf_size, leaf_parent, leaf_basis, leaf_transfer, mid_transfer, nb=8):
    leaves, rank, points = leaf_basis.shape
    ports = charges.shape[1]
    mids = mid_transfer.shape[0]
    grid_spec = pltpu.PrefetchScalarGridSpec(
        num_scalar_prefetch=2,
        grid=(leaves // nb,),
        in_specs=[pl.BlockSpec((nb * points, ports), lambda i, *_: (i, 0)),
                  pl.BlockSpec((nb, rank, points), lambda i, *_: (i, 0, 0)),
                  pl.BlockSpec((nb, rank, rank), lambda i, *_: (i, 0, 0)),
                  pl.BlockSpec(mid_transfer.shape, lambda i, *_: (0, 0, 0))],
        out_specs=[pl.BlockSpec((nb, rank, ports), lambda i, *_: (i, 0, 0)),
                   pl.BlockSpec((mids, rank, ports), lambda i, *_: (0, 0, 0)),
                   pl.BlockSpec((rank, ports), lambda i, *_: (0, 0))],
    )
    return pl.pallas_call(
        functools.partial(coef_kernel, nb),
        grid_spec=grid_spec,
        out_shape=[jax.ShapeDtypeStruct((leaves, rank, ports), jnp.float32),
                   jax.ShapeDtypeStruct((mids, rank, ports), jnp.float32),
                   jax.ShapeDtypeStruct((rank, ports), jnp.float32)],
        compiler_params=pltpu.CompilerParams(vmem_limit_bytes=60 * 1024 * 1024,
                                             dimension_semantics=("arbitrary",)),
        cost_estimate=pl.CostEstimate(flops=2 * leaves * rank * points * ports,
                                      bytes_accessed=4 * (charges.size + leaf_basis.size),
                                      transcendentals=0),
    )(leaf_size, leaf_parent, charges, leaf_basis, leaf_transfer, mid_transfer)


def far_kernel(nb, listed, coarse, size_ref, parent_ref, wanted_ref, pos_ref, near_ref, transfer_ref,
               basis_ref, near_mid_ref, mid_transfer_ref, top_coupling_ref, *rest):
    row_refs = rest[:listed]
    out_ref = rest[listed]
    down_mid = rest[listed + 1]
    i = pl.program_id(0)
    rank = near_ref.shape[1]
    points = basis_ref.shape[2]
    tdims = (((0,), (0,)), ((), ()))

    @pl.when(i == 0)
    def _():
        near_top = jnp.zeros(near_mid_ref.shape[1:], jnp.float32)
        for k in range(listed):
            c = top_coupling_ref[0, :, k * rank : (k + 1) * rank]
            prod = jnp.dot(c, row_refs[k][0], precision=exact_mode, preferred_element_type=jnp.float32)
            near_top = near_top + jnp.where(wanted_ref[k] < coarse, prod, 0.0)
        for c in range(near_mid_ref.shape[0]):
            down_mid[c] = near_mid_ref[c] + lax.dot_general(
                mid_transfer_ref[c], near_top, tdims, precision=exact_mode,
                preferred_element_type=jnp.float32)

    rows = lax.broadcasted_iota(jnp.int32, (points, 1), 0)
    for t in range(nb):
        l = i * nb + t
        p = parent_ref[l]
        dm = down_mid[p]
        dl = near_ref[t] + lax.dot_general(transfer_ref[t], dm, tdims, precision=lax.Precision.HIGH, preferred_element_type=jnp.float32)
        far = lax.dot_general(basis_ref[t], dl, tdims, precision=lax.Precision.HIGH, preferred_element_type=jnp.float32)
        out_ref[t * points:(t + 1) * points, :] = jnp.where(rows < size_ref[l], far, 0.0)


def far_field_pallas(near_leaf, leaf_transfer, leaf_basis, near_mid, mid_transfer, top_coupling,
                     shard_rows, wanted, position, leaf_size, leaf_parent, nb=8):
    leaves, rank, points = leaf_basis.shape
    ports = near_leaf.shape[2]
    listed = wanted.shape[0]
    coarse = shard_rows.shape[0]

    def row_spec(k):
        return pl.BlockSpec(
            (1, rank, ports), lambda i, s, p, w, q: (jnp.minimum(w[k], coarse - 1), 0, 0)
        )

    grid_spec = pltpu.PrefetchScalarGridSpec(
        num_scalar_prefetch=4,
        grid=(leaves // nb,),
        in_specs=[pl.BlockSpec((nb, rank, ports), lambda i, *_: (i, 0, 0)),
                  pl.BlockSpec((nb, rank, rank), lambda i, *_: (i, 0, 0)),
                  pl.BlockSpec((nb, rank, points), lambda i, *_: (i, 0, 0)),
                  pl.BlockSpec(near_mid.shape, lambda i, *_: (0, 0, 0)),
                  pl.BlockSpec(mid_transfer.shape, lambda i, *_: (0, 0, 0)),
                  pl.BlockSpec((1,) + top_coupling.shape[1:], lambda i, s, p, w, q: (q[0], 0, 0))]
                 + [row_spec(k) for k in range(listed)],
        out_specs=pl.BlockSpec((nb * points, ports), lambda i, *_: (i, 0)),
        scratch_shapes=[pltpu.VMEM(near_mid.shape, jnp.float32)],
    )
    return pl.pallas_call(
        functools.partial(far_kernel, nb, listed, coarse),
        grid_spec=grid_spec,
        out_shape=jax.ShapeDtypeStruct((leaves * points, ports), jnp.float32),
        compiler_params=pltpu.CompilerParams(vmem_limit_bytes=60 * 1024 * 1024,
                                             dimension_semantics=("arbitrary",)),
        cost_estimate=pl.CostEstimate(flops=2 * leaves * rank * points * ports, bytes_accessed=4 * (leaf_basis.size + 2 * leaves * points * ports), transcendentals=0),
    )(leaf_size, leaf_parent, wanted, position, near_leaf, leaf_transfer, leaf_basis, near_mid,
      mid_transfer, top_coupling, *([shard_rows] * listed))


def couple_rows(pairs_ref, land_ref, coupling_ref, out_ref, listed):
    total = land_ref.shape[0]
    rank = land_ref.shape[1]

    def target(t, carry):
        acc = jnp.zeros(out_ref.shape[1:], jnp.float32)
        for k in range(listed):
            r = pairs_ref[t, k]
            blk = land_ref[jnp.minimum(r, total - 1)]
            c = coupling_ref[t, :, k * rank : (k + 1) * rank]
            prod = jnp.dot(c, blk, precision=lax.Precision.HIGH, preferred_element_type=jnp.float32)
            acc = acc + jnp.where(r < total, prod, 0.0)
        out_ref[t] = acc
        return carry

    lax.fori_loop(0, out_ref.shape[0], target, 0)


def fill_slots(send_ref, coef_ref, pay_ref):
    held = coef_ref.shape[0]

    def fill(i, carry):
        a = send_ref[i]
        pay_ref[i] = jnp.where(a < held, coef_ref[jnp.minimum(a, held - 1)], 0.0)
        return carry

    lax.fori_loop(0, pay_ref.shape[0], fill, 0)


def exchange_couple_kernel(axes, sizes, pair_leaf_ref, pair_mid_ref, send_leaf_ref, send_mid_ref,
                           coef_leaf_ref, coef_mid_ref,
                           leaf_coupling_ref, mid_coupling_ref, near_leaf_ref, near_mid_ref,
                           leaf_pay_ref, mid_pay_ref, leaf_land, mid_land, sems):
    outer, inner = sizes
    count = outer * inner
    me = lax.axis_index(axes[0]) * inner + lax.axis_index(axes[1])
    fill_slots(send_leaf_ref, coef_leaf_ref, leaf_pay_ref)
    fill_slots(send_mid_ref, coef_mid_ref, mid_pay_ref)
    barrier = pltpu.get_barrier_semaphore()

    def greet(q, carry):
        peer = lax.rem(me + q, count)
        pl.semaphore_signal(barrier, 1, device_id=(peer // inner, peer % inner),
                            device_id_type=pl.DeviceIdType.MESH)
        return carry

    lax.fori_loop(1, count, greet, 0)
    pl.semaphore_wait(barrier, count - 1)
    stride = 37 if math.gcd(37, count) == 1 else 1
    slots = leaf_pay_ref.shape[0] // count

    def sender(pay_ref, land_ref, send_sem, recv_sem):
        def send(k, carry):
            peer = lax.rem(me + lax.rem(k * stride, count), count)
            pltpu.make_async_remote_copy(
                src_ref=pay_ref.at[pl.ds(peer * slots, slots)],
                dst_ref=land_ref.at[pl.ds(me * slots, slots)],
                send_sem=send_sem,
                recv_sem=recv_sem,
                device_id=(peer // inner, peer % inner),
                device_id_type=pl.DeviceIdType.MESH,
            ).start()
            return carry

        lax.fori_loop(1, count, send, 0)

    def everything(pay_ref, land_ref, send_sem, recv_sem):
        return pltpu.make_async_remote_copy(
            src_ref=pay_ref.at[pl.ds(0, (count - 1) * slots)],
            dst_ref=land_ref.at[pl.ds(0, (count - 1) * slots)],
            send_sem=send_sem,
            recv_sem=recv_sem,
            device_id=(0, 0),
            device_id_type=pl.DeviceIdType.MESH,
        )

    sender(leaf_pay_ref, leaf_land, sems.at[0], sems.at[1])
    own_leaf = pltpu.make_async_copy(leaf_pay_ref.at[pl.ds(me * slots, slots)],
                                     leaf_land.at[pl.ds(me * slots, slots)], sems.at[4])
    own_leaf.start()
    sender(mid_pay_ref, mid_land, sems.at[2], sems.at[3])
    own_mid = pltpu.make_async_copy(mid_pay_ref.at[pl.ds(me * slots, slots)],
                                    mid_land.at[pl.ds(me * slots, slots)], sems.at[5])
    own_mid.start()

    leaf_all = everything(leaf_pay_ref, leaf_land, sems.at[0], sems.at[1])
    mid_all = everything(mid_pay_ref, mid_land, sems.at[2], sems.at[3])
    own_leaf.wait()
    leaf_all.wait_recv()
    couple_rows(pair_leaf_ref, leaf_land, leaf_coupling_ref, near_leaf_ref, pair_leaf_ref.shape[1])
    own_mid.wait()
    mid_all.wait_recv()
    couple_rows(pair_mid_ref, mid_land, mid_coupling_ref, near_mid_ref, pair_mid_ref.shape[1])
    leaf_all.wait_send()
    mid_all.wait_send()


def exchange_couple(pair_leaf, pair_mid, send_leaf, send_mid, coef_leaf, coef_mid, leaf_coupling,
                    mid_coupling, axes, sizes):
    rank, ports = coef_leaf.shape[1:]
    pay_shape = (send_leaf.shape[0], rank, ports)
    n_leaf = leaf_coupling.shape[0]
    n_mid = mid_coupling.shape[0]
    vmem = pl.BlockSpec(memory_space=pltpu.VMEM)
    smem = pl.BlockSpec(memory_space=pltpu.SMEM)
    hbm = pl.BlockSpec(memory_space=pl.ANY)
    return pl.pallas_call(
        functools.partial(exchange_couple_kernel, axes, sizes),
        out_shape=[jax.ShapeDtypeStruct((n_leaf, rank, ports), jnp.float32),
                   jax.ShapeDtypeStruct((n_mid, rank, ports), jnp.float32)],
        in_specs=[smem, smem, smem, smem, vmem, vmem, vmem, vmem],
        out_specs=[vmem, vmem],
        scratch_shapes=[pltpu.VMEM(pay_shape, jnp.float32), pltpu.VMEM(pay_shape, jnp.float32),
                        pltpu.VMEM(pay_shape, jnp.float32), pltpu.VMEM(pay_shape, jnp.float32),
                        pltpu.SemaphoreType.DMA((6,))],
        compiler_params=pltpu.CompilerParams(collective_id=0, has_side_effects=True,
                                             vmem_limit_bytes=62 * 1024 * 1024),
        cost_estimate=pl.CostEstimate(
            flops=2 * (leaf_coupling.size + mid_coupling.size) * ports,
            bytes_accessed=4 * (coef_leaf.size + coef_mid.size + leaf_coupling.size + mid_coupling.size),
            transcendentals=0),
    )(pair_leaf, pair_mid, send_leaf, send_mid, coef_leaf, coef_mid,
      leaf_coupling, mid_coupling)


def body(
    sizes,
    charges,
    leaf_size,
    leaf_basis,
    leaf_transfer,
    mid_transfer,
    leaf_parent,
    send_leaf,
    pair_leaf,
    leaf_coupling,
    send_mid,
    pair_mid,
    mid_coupling,
    top_pairs,
    top_coupling,
):
    leaf_count, coef_rank, leaf_points = leaf_basis.shape
    port_count = charges.shape[1]
    mid_count = mid_transfer.shape[0]
    owners = send_leaf.shape[0] // 2
    slots = 2
    coef_leaf, coef_mid, coef_top = build_coefs(
        charges, leaf_size, leaf_parent, leaf_basis, leaf_transfer, mid_transfer
    )
    near_leaf, near_mid = exchange_couple(
        pair_leaf, pair_mid, send_leaf, send_mid, coef_leaf, coef_mid, leaf_coupling, mid_coupling,
        ("group", "cluster"), sizes,
    )

    position = lax.axis_index("cluster").astype(jnp.int32).reshape(1)
    wanted = lax.dynamic_slice_in_dim(top_pairs, position[0], 1, 0)[0]
    shard_rows = lax.all_gather(coef_top[None], ("group", "cluster"), axis=0, tiled=True)
    return far_field_pallas(near_leaf, leaf_transfer, leaf_basis, near_mid, mid_transfer, top_coupling,
                            shard_rows, wanted, position, leaf_size, leaf_parent)


def solution(mesh):
    in_specs = (
        P(("group", "cluster"), None),
        P(("group", "cluster")),
        P(("group", "cluster"), None, None),
        P(("group", "cluster"), None, None),
        P(("group", "cluster"), None, None),
        P(("group", "cluster")),
        P(("group", "cluster")),
        P(("group", "cluster"), None),
        P(("group", "cluster"), None, None),
        P(("group", "cluster")),
        P(("group", "cluster"), None),
        P(("group", "cluster"), None, None),
        P("group", None),
        P("group", None, None),
    )
    out_specs = P(("group", "cluster"), None)
    sizes = (mesh.shape["group"], mesh.shape["cluster"])
    return jax.shard_map(functools.partial(body, sizes), mesh=mesh, in_specs=in_specs, out_specs=out_specs, check_vma=False)
```

```python
import functools
import math

import jax
import jax.numpy as jnp
from jax import lax
from jax.experimental import pallas as pl
from jax.experimental.pallas import tpu as pltpu
from jax.sharding import PartitionSpec as P

exact_mode = lax.Precision.HIGHEST


def coef_kernel(nb, size_ref, parent_ref, charges_ref, basis_ref, transfer_ref, mid_transfer_ref,
                leaf_ref, mid_ref, top_ref):
    i = pl.program_id(0)
    rank, points = basis_ref.shape[1:]
    mids = mid_transfer_ref.shape[0]

    @pl.when(i == 0)
    def _():
        mid_ref[...] = jnp.zeros(mid_ref.shape, jnp.float32)

    rows = lax.broadcasted_iota(jnp.int32, (points, 1), 0)
    for t in range(nb):
        l = i * nb + t
        blk = charges_ref[t * points:(t + 1) * points, :]
        blk = jnp.where(rows < size_ref[l], blk, 0.0)
        coef = jnp.dot(basis_ref[t], blk, precision=exact_mode, preferred_element_type=jnp.float32)
        leaf_ref[t] = coef
        up = jnp.dot(transfer_ref[t], coef, precision=exact_mode, preferred_element_type=jnp.float32)
        p = parent_ref[l]
        mid_ref[p] = mid_ref[p] + up

    @pl.when(i == pl.num_programs(0) - 1)
    def _():
        top = jnp.zeros(top_ref.shape, jnp.float32)
        for c in range(mids):
            top = top + jnp.dot(mid_transfer_ref[c], mid_ref[c], precision=exact_mode,
                                preferred_element_type=jnp.float32)
        top_ref[...] = top


def build_coefs(charges, leaf_size, leaf_parent, leaf_basis, leaf_transfer, mid_transfer, nb=8):
    leaves, rank, points = leaf_basis.shape
    ports = charges.shape[1]
    mids = mid_transfer.shape[0]
    grid_spec = pltpu.PrefetchScalarGridSpec(
        num_scalar_prefetch=2,
        grid=(leaves // nb,),
        in_specs=[pl.BlockSpec((nb * points, ports), lambda i, *_: (i, 0)),
                  pl.BlockSpec((nb, rank, points), lambda i, *_: (i, 0, 0)),
                  pl.BlockSpec((nb, rank, rank), lambda i, *_: (i, 0, 0)),
                  pl.BlockSpec(mid_transfer.shape, lambda i, *_: (0, 0, 0))],
        out_specs=[pl.BlockSpec((nb, rank, ports), lambda i, *_: (i, 0, 0)),
                   pl.BlockSpec((mids, rank, ports), lambda i, *_: (0, 0, 0)),
                   pl.BlockSpec((rank, ports), lambda i, *_: (0, 0))],
    )
    return pl.pallas_call(
        functools.partial(coef_kernel, nb),
        grid_spec=grid_spec,
        out_shape=[jax.ShapeDtypeStruct((leaves, rank, ports), jnp.float32),
                   jax.ShapeDtypeStruct((mids, rank, ports), jnp.float32),
                   jax.ShapeDtypeStruct((rank, ports), jnp.float32)],
        compiler_params=pltpu.CompilerParams(vmem_limit_bytes=60 * 1024 * 1024,
                                             dimension_semantics=("arbitrary",)),
        cost_estimate=pl.CostEstimate(flops=2 * leaves * rank * points * ports,
                                      bytes_accessed=4 * (charges.size + leaf_basis.size),
                                      transcendentals=0),
    )(leaf_size, leaf_parent, charges, leaf_basis, leaf_transfer, mid_transfer)


def far_kernel(nb, listed, coarse, size_ref, parent_ref, wanted_ref, pos_ref, near_ref, transfer_ref,
               basis_ref, near_mid_ref, mid_transfer_ref, top_coupling_ref, *rest):
    row_refs = rest[:listed]
    out_ref = rest[listed]
    down_mid = rest[listed + 1]
    i = pl.program_id(0)
    rank = near_ref.shape[1]
    points = basis_ref.shape[2]
    tdims = (((0,), (0,)), ((), ()))

    @pl.when(i == 0)
    def _():
        near_top = jnp.zeros(near_mid_ref.shape[1:], jnp.float32)
        for k in range(listed):
            c = top_coupling_ref[0, :, k * rank : (k + 1) * rank]
            prod = jnp.dot(c, row_refs[k][0], precision=exact_mode, preferred_element_type=jnp.float32)
            near_top = near_top + jnp.where(wanted_ref[k] < coarse, prod, 0.0)
        for c in range(near_mid_ref.shape[0]):
            down_mid[c] = near_mid_ref[c] + lax.dot_general(
                mid_transfer_ref[c], near_top, tdims, precision=exact_mode,
                preferred_element_type=jnp.float32)

    rows = lax.broadcasted_iota(jnp.int32, (points, 1), 0)
    for t in range(nb):
        l = i * nb + t
        p = parent_ref[l]
        dm = down_mid[p]
        dl = near_ref[t] + lax.dot_general(transfer_ref[t], dm, tdims, precision=lax.Precision.HIGH, preferred_element_type=jnp.float32)
        far = lax.dot_general(basis_ref[t], dl, tdims, precision=lax.Precision.HIGH, preferred_element_type=jnp.float32)
        out_ref[t * points:(t + 1) * points, :] = jnp.where(rows < size_ref[l], far, 0.0)


def far_field_pallas(near_leaf, leaf_transfer, leaf_basis, near_mid, mid_transfer, top_coupling,
                     shard_rows, wanted, position, leaf_size, leaf_parent, nb=16):
    leaves, rank, points = leaf_basis.shape
    ports = near_leaf.shape[2]
    listed = wanted.shape[0]
    coarse = shard_rows.shape[0]

    def row_spec(k):
        return pl.BlockSpec(
            (1, rank, ports), lambda i, s, p, w, q: (jnp.minimum(w[k], coarse - 1), 0, 0)
        )

    grid_spec = pltpu.PrefetchScalarGridSpec(
        num_scalar_prefetch=4,
        grid=(leaves // nb,),
        in_specs=[pl.BlockSpec((nb, rank, ports), lambda i, *_: (i, 0, 0)),
                  pl.BlockSpec((nb, rank, rank), lambda i, *_: (i, 0, 0)),
                  pl.BlockSpec((nb, rank, points), lambda i, *_: (i, 0, 0)),
                  pl.BlockSpec(near_mid.shape, lambda i, *_: (0, 0, 0)),
                  pl.BlockSpec(mid_transfer.shape, lambda i, *_: (0, 0, 0)),
                  pl.BlockSpec((1,) + top_coupling.shape[1:], lambda i, s, p, w, q: (q[0], 0, 0))]
                 + [row_spec(k) for k in range(listed)],
        out_specs=pl.BlockSpec((nb * points, ports), lambda i, *_: (i, 0)),
        scratch_shapes=[pltpu.VMEM(near_mid.shape, jnp.float32)],
    )
    return pl.pallas_call(
        functools.partial(far_kernel, nb, listed, coarse),
        grid_spec=grid_spec,
        out_shape=jax.ShapeDtypeStruct((leaves * points, ports), jnp.float32),
        compiler_params=pltpu.CompilerParams(vmem_limit_bytes=60 * 1024 * 1024,
                                             dimension_semantics=("arbitrary",)),
        cost_estimate=pl.CostEstimate(flops=2 * leaves * rank * points * ports, bytes_accessed=4 * (leaf_basis.size + 2 * leaves * points * ports), transcendentals=0),
    )(leaf_size, leaf_parent, wanted, position, near_leaf, leaf_transfer, leaf_basis, near_mid,
      mid_transfer, top_coupling, *([shard_rows] * listed))


def couple_rows(pairs_ref, land_ref, coupling_ref, out_ref, listed):
    total = land_ref.shape[0]
    rank = land_ref.shape[1]

    def target(t, carry):
        acc = jnp.zeros(out_ref.shape[1:], jnp.float32)
        for k in range(listed):
            r = pairs_ref[t, k]
            blk = land_ref[jnp.minimum(r, total - 1)]
            c = coupling_ref[t, :, k * rank : (k + 1) * rank]
            prod = jnp.dot(c, blk, precision=lax.Precision.HIGH, preferred_element_type=jnp.float32)
            acc = acc + jnp.where(r < total, prod, 0.0)
        out_ref[t] = acc
        return carry

    lax.fori_loop(0, out_ref.shape[0], target, 0)


def fill_slots(send_ref, coef_ref, pay_ref):
    held = coef_ref.shape[0]

    def fill(i, carry):
        a = send_ref[i]
        pay_ref[i] = jnp.where(a < held, coef_ref[jnp.minimum(a, held - 1)], 0.0)
        return carry

    lax.fori_loop(0, pay_ref.shape[0], fill, 0)


def exchange_couple_kernel(axes, sizes, pair_leaf_ref, pair_mid_ref, send_leaf_ref, send_mid_ref,
                           coef_leaf_ref, coef_mid_ref,
                           leaf_coupling_ref, mid_coupling_ref, near_leaf_ref, near_mid_ref,
                           leaf_pay_ref, mid_pay_ref, leaf_land, mid_land, sems):
    outer, inner = sizes
    count = outer * inner
    me = lax.axis_index(axes[0]) * inner + lax.axis_index(axes[1])
    fill_slots(send_leaf_ref, coef_leaf_ref, leaf_pay_ref)
    fill_slots(send_mid_ref, coef_mid_ref, mid_pay_ref)
    barrier = pltpu.get_barrier_semaphore()

    def greet(q, carry):
        peer = lax.rem(me + q, count)
        pl.semaphore_signal(barrier, 1, device_id=(peer // inner, peer % inner),
                            device_id_type=pl.DeviceIdType.MESH)
        return carry

    lax.fori_loop(1, count, greet, 0)
    pl.semaphore_wait(barrier, count - 1)
    stride = 37 if math.gcd(37, count) == 1 else 1
    slots = leaf_pay_ref.shape[0] // count

    def sender(pay_ref, land_ref, send_sem, recv_sem):
        def send(k, carry):
            peer = lax.rem(me + lax.rem(k * stride, count), count)
            pltpu.make_async_remote_copy(
                src_ref=pay_ref.at[pl.ds(peer * slots, slots)],
                dst_ref=land_ref.at[pl.ds(me * slots, slots)],
                send_sem=send_sem,
                recv_sem=recv_sem,
                device_id=(peer // inner, peer % inner),
                device_id_type=pl.DeviceIdType.MESH,
            ).start()
            return carry

        lax.fori_loop(1, count, send, 0)

    def everything(pay_ref, land_ref, send_sem, recv_sem):
        return pltpu.make_async_remote_copy(
            src_ref=pay_ref.at[pl.ds(0, (count - 1) * slots)],
            dst_ref=land_ref.at[pl.ds(0, (count - 1) * slots)],
            send_sem=send_sem,
            recv_sem=recv_sem,
            device_id=(0, 0),
            device_id_type=pl.DeviceIdType.MESH,
        )

    sender(leaf_pay_ref, leaf_land, sems.at[0], sems.at[1])
    own_leaf = pltpu.make_async_copy(leaf_pay_ref.at[pl.ds(me * slots, slots)],
                                     leaf_land.at[pl.ds(me * slots, slots)], sems.at[4])
    own_leaf.start()
    sender(mid_pay_ref, mid_land, sems.at[2], sems.at[3])
    own_mid = pltpu.make_async_copy(mid_pay_ref.at[pl.ds(me * slots, slots)],
                                    mid_land.at[pl.ds(me * slots, slots)], sems.at[5])
    own_mid.start()

    leaf_all = everything(leaf_pay_ref, leaf_land, sems.at[0], sems.at[1])
    mid_all = everything(mid_pay_ref, mid_land, sems.at[2], sems.at[3])
    own_leaf.wait()
    leaf_all.wait_recv()
    couple_rows(pair_leaf_ref, leaf_land, leaf_coupling_ref, near_leaf_ref, pair_leaf_ref.shape[1])
    own_mid.wait()
    mid_all.wait_recv()
    couple_rows(pair_mid_ref, mid_land, mid_coupling_ref, near_mid_ref, pair_mid_ref.shape[1])
    leaf_all.wait_send()
    mid_all.wait_send()


def exchange_couple(pair_leaf, pair_mid, send_leaf, send_mid, coef_leaf, coef_mid, leaf_coupling,
                    mid_coupling, axes, sizes):
    rank, ports = coef_leaf.shape[1:]
    pay_shape = (send_leaf.shape[0], rank, ports)
    n_leaf = leaf_coupling.shape[0]
    n_mid = mid_coupling.shape[0]
    vmem = pl.BlockSpec(memory_space=pltpu.VMEM)
    smem = pl.BlockSpec(memory_space=pltpu.SMEM)
    hbm = pl.BlockSpec(memory_space=pl.ANY)
    return pl.pallas_call(
        functools.partial(exchange_couple_kernel, axes, sizes),
        out_shape=[jax.ShapeDtypeStruct((n_leaf, rank, ports), jnp.float32),
                   jax.ShapeDtypeStruct((n_mid, rank, ports), jnp.float32)],
        in_specs=[smem, smem, smem, smem, vmem, vmem, vmem, vmem],
        out_specs=[vmem, vmem],
        scratch_shapes=[pltpu.VMEM(pay_shape, jnp.float32), pltpu.VMEM(pay_shape, jnp.float32),
                        pltpu.VMEM(pay_shape, jnp.float32), pltpu.VMEM(pay_shape, jnp.float32),
                        pltpu.SemaphoreType.DMA((6,))],
        compiler_params=pltpu.CompilerParams(collective_id=0, has_side_effects=True,
                                             vmem_limit_bytes=62 * 1024 * 1024),
        cost_estimate=pl.CostEstimate(
            flops=2 * (leaf_coupling.size + mid_coupling.size) * ports,
            bytes_accessed=4 * (coef_leaf.size + coef_mid.size + leaf_coupling.size + mid_coupling.size),
            transcendentals=0),
    )(pair_leaf, pair_mid, send_leaf, send_mid, coef_leaf, coef_mid,
      leaf_coupling, mid_coupling)


def body(
    sizes,
    charges,
    leaf_size,
    leaf_basis,
    leaf_transfer,
    mid_transfer,
    leaf_parent,
    send_leaf,
    pair_leaf,
    leaf_coupling,
    send_mid,
    pair_mid,
    mid_coupling,
    top_pairs,
    top_coupling,
):
    leaf_count, coef_rank, leaf_points = leaf_basis.shape
    port_count = charges.shape[1]
    mid_count = mid_transfer.shape[0]
    owners = send_leaf.shape[0] // 2
    slots = 2
    coef_leaf, coef_mid, coef_top = build_coefs(
        charges, leaf_size, leaf_parent, leaf_basis, leaf_transfer, mid_transfer
    )
    near_leaf, near_mid = exchange_couple(
        pair_leaf, pair_mid, send_leaf, send_mid, coef_leaf, coef_mid, leaf_coupling, mid_coupling,
        ("group", "cluster"), sizes,
    )

    position = lax.axis_index("cluster").astype(jnp.int32).reshape(1)
    wanted = lax.dynamic_slice_in_dim(top_pairs, position[0], 1, 0)[0]
    shard_rows = lax.all_gather(coef_top[None], ("group", "cluster"), axis=0, tiled=True)
    return far_field_pallas(near_leaf, leaf_transfer, leaf_basis, near_mid, mid_transfer, top_coupling,
                            shard_rows, wanted, position, leaf_size, leaf_parent)


def solution(mesh):
    in_specs = (
        P(("group", "cluster"), None),
        P(("group", "cluster")),
        P(("group", "cluster"), None, None),
        P(("group", "cluster"), None, None),
        P(("group", "cluster"), None, None),
        P(("group", "cluster")),
        P(("group", "cluster")),
        P(("group", "cluster"), None),
        P(("group", "cluster"), None, None),
        P(("group", "cluster")),
        P(("group", "cluster"), None),
        P(("group", "cluster"), None, None),
        P("group", None),
        P("group", None, None),
    )
    out_specs = P(("group", "cluster"), None)
    sizes = (mesh.shape["group"], mesh.shape["cluster"])
    return jax.shard_map(functools.partial(body, sizes), mesh=mesh, in_specs=in_specs, out_specs=out_specs, check_vma=False)
```

```python
import functools
import math

import jax
import jax.numpy as jnp
from jax import lax
from jax.experimental import pallas as pl
from jax.experimental.pallas import tpu as pltpu
from jax.sharding import PartitionSpec as P

exact_mode = lax.Precision.HIGHEST


def coef_kernel(nb, size_ref, parent_ref, charges_ref, basis_ref, transfer_ref, mid_transfer_ref,
                leaf_ref, mid_ref, top_ref):
    i = pl.program_id(0)
    rank, points = basis_ref.shape[1:]
    mids = mid_transfer_ref.shape[0]

    @pl.when(i == 0)
    def _():
        mid_ref[...] = jnp.zeros(mid_ref.shape, jnp.float32)

    rows = lax.broadcasted_iota(jnp.int32, (points, 1), 0)
    for t in range(nb):
        l = i * nb + t
        blk = charges_ref[t * points:(t + 1) * points, :]
        blk = jnp.where(rows < size_ref[l], blk, 0.0)
        coef = jnp.dot(basis_ref[t], blk, precision=exact_mode, preferred_element_type=jnp.float32)
        leaf_ref[t] = coef
        up = jnp.dot(transfer_ref[t], coef, precision=exact_mode, preferred_element_type=jnp.float32)
        p = parent_ref[l]
        mid_ref[p] = mid_ref[p] + up

    @pl.when(i == pl.num_programs(0) - 1)
    def _():
        top = jnp.zeros(top_ref.shape, jnp.float32)
        for c in range(mids):
            top = top + jnp.dot(mid_transfer_ref[c], mid_ref[c], precision=exact_mode,
                                preferred_element_type=jnp.float32)
        top_ref[...] = top


def build_coefs(charges, leaf_size, leaf_parent, leaf_basis, leaf_transfer, mid_transfer, nb=8):
    leaves, rank, points = leaf_basis.shape
    ports = charges.shape[1]
    mids = mid_transfer.shape[0]
    grid_spec = pltpu.PrefetchScalarGridSpec(
        num_scalar_prefetch=2,
        grid=(leaves // nb,),
        in_specs=[pl.BlockSpec((nb * points, ports), lambda i, *_: (i, 0)),
                  pl.BlockSpec((nb, rank, points), lambda i, *_: (i, 0, 0)),
                  pl.BlockSpec((nb, rank, rank), lambda i, *_: (i, 0, 0)),
                  pl.BlockSpec(mid_transfer.shape, lambda i, *_: (0, 0, 0))],
        out_specs=[pl.BlockSpec((nb, rank, ports), lambda i, *_: (i, 0, 0)),
                   pl.BlockSpec((mids, rank, ports), lambda i, *_: (0, 0, 0)),
                   pl.BlockSpec((rank, ports), lambda i, *_: (0, 0))],
    )
    return pl.pallas_call(
        functools.partial(coef_kernel, nb),
        grid_spec=grid_spec,
        out_shape=[jax.ShapeDtypeStruct((leaves, rank, ports), jnp.float32),
                   jax.ShapeDtypeStruct((mids, rank, ports), jnp.float32),
                   jax.ShapeDtypeStruct((rank, ports), jnp.float32)],
        compiler_params=pltpu.CompilerParams(vmem_limit_bytes=60 * 1024 * 1024,
                                             dimension_semantics=("arbitrary",)),
        cost_estimate=pl.CostEstimate(flops=2 * leaves * rank * points * ports,
                                      bytes_accessed=4 * (charges.size + leaf_basis.size),
                                      transcendentals=0),
    )(leaf_size, leaf_parent, charges, leaf_basis, leaf_transfer, mid_transfer)


def far_kernel(nb, listed, coarse, size_ref, parent_ref, wanted_ref, pos_ref, near_ref, transfer_ref,
               basis_ref, near_mid_ref, mid_transfer_ref, top_coupling_ref, *rest):
    row_refs = rest[:listed]
    out_ref = rest[listed]
    down_mid = rest[listed + 1]
    i = pl.program_id(0)
    rank = near_ref.shape[1]
    points = basis_ref.shape[2]
    tdims = (((0,), (0,)), ((), ()))

    @pl.when(i == 0)
    def _():
        near_top = jnp.zeros(near_mid_ref.shape[1:], jnp.float32)
        for k in range(listed):
            c = top_coupling_ref[0, :, k * rank : (k + 1) * rank]
            prod = jnp.dot(c, row_refs[k][0], precision=exact_mode, preferred_element_type=jnp.float32)
            near_top = near_top + jnp.where(wanted_ref[k] < coarse, prod, 0.0)
        for c in range(near_mid_ref.shape[0]):
            down_mid[c] = near_mid_ref[c] + lax.dot_general(
                mid_transfer_ref[c], near_top, tdims, precision=exact_mode,
                preferred_element_type=jnp.float32)

    rows = lax.broadcasted_iota(jnp.int32, (points, 1), 0)
    for t in range(nb):
        l = i * nb + t
        p = parent_ref[l]
        dm = down_mid[p]
        dl = near_ref[t] + lax.dot_general(transfer_ref[t], dm, tdims, precision=lax.Precision.HIGH, preferred_element_type=jnp.float32)
        far = lax.dot_general(basis_ref[t], dl, tdims, precision=lax.Precision.HIGH, preferred_element_type=jnp.float32)
        out_ref[t * points:(t + 1) * points, :] = jnp.where(rows < size_ref[l], far, 0.0)


def far_field_pallas(near_leaf, leaf_transfer, leaf_basis, near_mid, mid_transfer, top_coupling,
                     shard_rows, wanted, position, leaf_size, leaf_parent, nb=8):
    leaves, rank, points = leaf_basis.shape
    ports = near_leaf.shape[2]
    listed = wanted.shape[0]
    coarse = shard_rows.shape[0]

    def row_spec(k):
        return pl.BlockSpec(
            (1, rank, ports), lambda i, s, p, w, q: (jnp.minimum(w[k], coarse - 1), 0, 0)
        )

    grid_spec = pltpu.PrefetchScalarGridSpec(
        num_scalar_prefetch=4,
        grid=(leaves // nb,),
        in_specs=[pl.BlockSpec((nb, rank, ports), lambda i, *_: (i, 0, 0)),
                  pl.BlockSpec((nb, rank, rank), lambda i, *_: (i, 0, 0)),
                  pl.BlockSpec((nb, rank, points), lambda i, *_: (i, 0, 0)),
                  pl.BlockSpec(near_mid.shape, lambda i, *_: (0, 0, 0)),
                  pl.BlockSpec(mid_transfer.shape, lambda i, *_: (0, 0, 0)),
                  pl.BlockSpec((1,) + top_coupling.shape[1:], lambda i, s, p, w, q: (q[0], 0, 0))]
                 + [row_spec(k) for k in range(listed)],
        out_specs=pl.BlockSpec((nb * points, ports), lambda i, *_: (i, 0)),
        scratch_shapes=[pltpu.VMEM(near_mid.shape, jnp.float32)],
    )
    return pl.pallas_call(
        functools.partial(far_kernel, nb, listed, coarse),
        grid_spec=grid_spec,
        out_shape=jax.ShapeDtypeStruct((leaves * points, ports), jnp.float32),
        compiler_params=pltpu.CompilerParams(vmem_limit_bytes=60 * 1024 * 1024,
                                             dimension_semantics=("arbitrary",)),
        cost_estimate=pl.CostEstimate(flops=2 * leaves * rank * points * ports, bytes_accessed=4 * (leaf_basis.size + 2 * leaves * points * ports), transcendentals=0),
    )(leaf_size, leaf_parent, wanted, position, near_leaf, leaf_transfer, leaf_basis, near_mid,
      mid_transfer, top_coupling, *([shard_rows] * listed))


def couple_rows(pairs_ref, land_ref, coupling_ref, out_ref, listed):
    total = land_ref.shape[0]
    rank = land_ref.shape[1]

    def target(t, carry):
        acc = jnp.zeros(out_ref.shape[1:], jnp.float32)
        for k in range(listed):
            r = pairs_ref[t, k]
            blk = land_ref[jnp.minimum(r, total - 1)]
            c = coupling_ref[t, :, k * rank : (k + 1) * rank]
            prod = jnp.dot(c, blk, precision=lax.Precision.HIGH, preferred_element_type=jnp.float32)
            acc = acc + jnp.where(r < total, prod, 0.0)
        out_ref[t] = acc
        return carry

    lax.fori_loop(0, out_ref.shape[0], target, 0)


def fill_slots(send_ref, coef_ref, pay_ref):
    held = coef_ref.shape[0]

    def fill(i, carry):
        a = send_ref[i]
        pay_ref[i] = jnp.where(a < held, coef_ref[jnp.minimum(a, held - 1)], 0.0)
        return carry

    lax.fori_loop(0, pay_ref.shape[0], fill, 0)


def exchange_couple_kernel(axes, sizes, pair_leaf_ref, pair_mid_ref, send_leaf_ref, send_mid_ref,
                           coef_leaf_ref, coef_mid_ref,
                           leaf_coupling_ref, mid_coupling_ref, near_leaf_ref, near_mid_ref,
                           leaf_pay_ref, mid_pay_ref, leaf_land, mid_land, sems):
    outer, inner = sizes
    count = outer * inner
    me = lax.axis_index(axes[0]) * inner + lax.axis_index(axes[1])
    fill_slots(send_leaf_ref, coef_leaf_ref, leaf_pay_ref)
    fill_slots(send_mid_ref, coef_mid_ref, mid_pay_ref)
    barrier = pltpu.get_barrier_semaphore()

    def greet(q, carry):
        peer = lax.rem(me + q, count)
        pl.semaphore_signal(barrier, 1, device_id=(peer // inner, peer % inner),
                            device_id_type=pl.DeviceIdType.MESH)
        return carry

    lax.fori_loop(1, count, greet, 0)
    pl.semaphore_wait(barrier, count - 1)
    stride = 45 if math.gcd(45, count) == 1 else 1
    slots = leaf_pay_ref.shape[0] // count

    def sender(pay_ref, land_ref, send_sem, recv_sem):
        def send(k, carry):
            peer = lax.rem(me + lax.rem(k * stride, count), count)
            pltpu.make_async_remote_copy(
                src_ref=pay_ref.at[pl.ds(peer * slots, slots)],
                dst_ref=land_ref.at[pl.ds(me * slots, slots)],
                send_sem=send_sem,
                recv_sem=recv_sem,
                device_id=(peer // inner, peer % inner),
                device_id_type=pl.DeviceIdType.MESH,
            ).start()
            return carry

        lax.fori_loop(1, count, send, 0)

    def everything(pay_ref, land_ref, send_sem, recv_sem):
        return pltpu.make_async_remote_copy(
            src_ref=pay_ref.at[pl.ds(0, (count - 1) * slots)],
            dst_ref=land_ref.at[pl.ds(0, (count - 1) * slots)],
            send_sem=send_sem,
            recv_sem=recv_sem,
            device_id=(0, 0),
            device_id_type=pl.DeviceIdType.MESH,
        )

    sender(leaf_pay_ref, leaf_land, sems.at[0], sems.at[1])
    own_leaf = pltpu.make_async_copy(leaf_pay_ref.at[pl.ds(me * slots, slots)],
                                     leaf_land.at[pl.ds(me * slots, slots)], sems.at[4])
    own_leaf.start()
    sender(mid_pay_ref, mid_land, sems.at[2], sems.at[3])
    own_mid = pltpu.make_async_copy(mid_pay_ref.at[pl.ds(me * slots, slots)],
                                    mid_land.at[pl.ds(me * slots, slots)], sems.at[5])
    own_mid.start()

    leaf_all = everything(leaf_pay_ref, leaf_land, sems.at[0], sems.at[1])
    mid_all = everything(mid_pay_ref, mid_land, sems.at[2], sems.at[3])
    own_leaf.wait()
    leaf_all.wait_recv()
    couple_rows(pair_leaf_ref, leaf_land, leaf_coupling_ref, near_leaf_ref, pair_leaf_ref.shape[1])
    own_mid.wait()
    mid_all.wait_recv()
    couple_rows(pair_mid_ref, mid_land, mid_coupling_ref, near_mid_ref, pair_mid_ref.shape[1])
    leaf_all.wait_send()
    mid_all.wait_send()


def exchange_couple(pair_leaf, pair_mid, send_leaf, send_mid, coef_leaf, coef_mid, leaf_coupling,
                    mid_coupling, axes, sizes):
    rank, ports = coef_leaf.shape[1:]
    pay_shape = (send_leaf.shape[0], rank, ports)
    n_leaf = leaf_coupling.shape[0]
    n_mid = mid_coupling.shape[0]
    vmem = pl.BlockSpec(memory_space=pltpu.VMEM)
    smem = pl.BlockSpec(memory_space=pltpu.SMEM)
    hbm = pl.BlockSpec(memory_space=pl.ANY)
    return pl.pallas_call(
        functools.partial(exchange_couple_kernel, axes, sizes),
        out_shape=[jax.ShapeDtypeStruct((n_leaf, rank, ports), jnp.float32),
                   jax.ShapeDtypeStruct((n_mid, rank, ports), jnp.float32)],
        in_specs=[smem, smem, smem, smem, vmem, vmem, vmem, vmem],
        out_specs=[vmem, vmem],
        scratch_shapes=[pltpu.VMEM(pay_shape, jnp.float32), pltpu.VMEM(pay_shape, jnp.float32),
                        pltpu.VMEM(pay_shape, jnp.float32), pltpu.VMEM(pay_shape, jnp.float32),
                        pltpu.SemaphoreType.DMA((6,))],
        compiler_params=pltpu.CompilerParams(collective_id=0, has_side_effects=True,
                                             vmem_limit_bytes=62 * 1024 * 1024),
        cost_estimate=pl.CostEstimate(
            flops=2 * (leaf_coupling.size + mid_coupling.size) * ports,
            bytes_accessed=4 * (coef_leaf.size + coef_mid.size + leaf_coupling.size + mid_coupling.size),
            transcendentals=0),
    )(pair_leaf, pair_mid, send_leaf, send_mid, coef_leaf, coef_mid,
      leaf_coupling, mid_coupling)


def body(
    sizes,
    charges,
    leaf_size,
    leaf_basis,
    leaf_transfer,
    mid_transfer,
    leaf_parent,
    send_leaf,
    pair_leaf,
    leaf_coupling,
    send_mid,
    pair_mid,
    mid_coupling,
    top_pairs,
    top_coupling,
):
    leaf_count, coef_rank, leaf_points = leaf_basis.shape
    port_count = charges.shape[1]
    mid_count = mid_transfer.shape[0]
    owners = send_leaf.shape[0] // 2
    slots = 2
    coef_leaf, coef_mid, coef_top = build_coefs(
        charges, leaf_size, leaf_parent, leaf_basis, leaf_transfer, mid_transfer
    )
    near_leaf, near_mid = exchange_couple(
        pair_leaf, pair_mid, send_leaf, send_mid, coef_leaf, coef_mid, leaf_coupling, mid_coupling,
        ("group", "cluster"), sizes,
    )

    position = lax.axis_index("cluster").astype(jnp.int32).reshape(1)
    wanted = lax.dynamic_slice_in_dim(top_pairs, position[0], 1, 0)[0]
    shard_rows = lax.all_gather(coef_top[None], ("group", "cluster"), axis=0, tiled=True)
    return far_field_pallas(near_leaf, leaf_transfer, leaf_basis, near_mid, mid_transfer, top_coupling,
                            shard_rows, wanted, position, leaf_size, leaf_parent)


def solution(mesh):
    in_specs = (
        P(("group", "cluster"), None),
        P(("group", "cluster")),
        P(("group", "cluster"), None, None),
        P(("group", "cluster"), None, None),
        P(("group", "cluster"), None, None),
        P(("group", "cluster")),
        P(("group", "cluster")),
        P(("group", "cluster"), None),
        P(("group", "cluster"), None, None),
        P(("group", "cluster")),
        P(("group", "cluster"), None),
        P(("group", "cluster"), None, None),
        P("group", None),
        P("group", None, None),
    )
    out_specs = P(("group", "cluster"), None)
    sizes = (mesh.shape["group"], mesh.shape["cluster"])
    return jax.shard_map(functools.partial(body, sizes), mesh=mesh, in_specs=in_specs, out_specs=out_specs, check_vma=False)
```

```python
import functools
import math

import jax
import jax.numpy as jnp
from jax import lax
from jax.experimental import pallas as pl
from jax.experimental.pallas import tpu as pltpu
from jax.sharding import PartitionSpec as P

exact_mode = lax.Precision.HIGHEST


def coef_kernel(nb, size_ref, parent_ref, charges_ref, basis_ref, transfer_ref, mid_transfer_ref,
                leaf_ref, mid_ref, top_ref):
    i = pl.program_id(0)
    rank, points = basis_ref.shape[1:]
    mids = mid_transfer_ref.shape[0]

    @pl.when(i == 0)
    def _():
        mid_ref[...] = jnp.zeros(mid_ref.shape, jnp.float32)

    rows = lax.broadcasted_iota(jnp.int32, (points, 1), 0)
    for t in range(nb):
        l = i * nb + t
        blk = charges_ref[t * points:(t + 1) * points, :]
        blk = jnp.where(rows < size_ref[l], blk, 0.0)
        coef = jnp.dot(basis_ref[t], blk, precision=exact_mode, preferred_element_type=jnp.float32)
        leaf_ref[t] = coef
        up = jnp.dot(transfer_ref[t], coef, precision=exact_mode, preferred_element_type=jnp.float32)
        p = parent_ref[l]
        mid_ref[p] = mid_ref[p] + up

    @pl.when(i == pl.num_programs(0) - 1)
    def _():
        top = jnp.zeros(top_ref.shape, jnp.float32)
        for c in range(mids):
            top = top + jnp.dot(mid_transfer_ref[c], mid_ref[c], precision=exact_mode,
                                preferred_element_type=jnp.float32)
        top_ref[...] = top


def build_coefs(charges, leaf_size, leaf_parent, leaf_basis, leaf_transfer, mid_transfer, nb=4):
    leaves, rank, points = leaf_basis.shape
    ports = charges.shape[1]
    mids = mid_transfer.shape[0]
    grid_spec = pltpu.PrefetchScalarGridSpec(
        num_scalar_prefetch=2,
        grid=(leaves // nb,),
        in_specs=[pl.BlockSpec((nb * points, ports), lambda i, *_: (i, 0)),
                  pl.BlockSpec((nb, rank, points), lambda i, *_: (i, 0, 0)),
                  pl.BlockSpec((nb, rank, rank), lambda i, *_: (i, 0, 0)),
                  pl.BlockSpec(mid_transfer.shape, lambda i, *_: (0, 0, 0))],
        out_specs=[pl.BlockSpec((nb, rank, ports), lambda i, *_: (i, 0, 0)),
                   pl.BlockSpec((mids, rank, ports), lambda i, *_: (0, 0, 0)),
                   pl.BlockSpec((rank, ports), lambda i, *_: (0, 0))],
    )
    return pl.pallas_call(
        functools.partial(coef_kernel, nb),
        grid_spec=grid_spec,
        out_shape=[jax.ShapeDtypeStruct((leaves, rank, ports), jnp.float32),
                   jax.ShapeDtypeStruct((mids, rank, ports), jnp.float32),
                   jax.ShapeDtypeStruct((rank, ports), jnp.float32)],
        compiler_params=pltpu.CompilerParams(vmem_limit_bytes=60 * 1024 * 1024,
                                             dimension_semantics=("arbitrary",)),
        cost_estimate=pl.CostEstimate(flops=2 * leaves * rank * points * ports,
                                      bytes_accessed=4 * (charges.size + leaf_basis.size),
                                      transcendentals=0),
    )(leaf_size, leaf_parent, charges, leaf_basis, leaf_transfer, mid_transfer)


def far_kernel(nb, listed, coarse, size_ref, parent_ref, wanted_ref, pos_ref, near_ref, transfer_ref,
               basis_ref, near_mid_ref, mid_transfer_ref, top_coupling_ref, *rest):
    row_refs = rest[:listed]
    out_ref = rest[listed]
    down_mid = rest[listed + 1]
    i = pl.program_id(0)
    rank = near_ref.shape[1]
    points = basis_ref.shape[2]
    tdims = (((0,), (0,)), ((), ()))

    @pl.when(i == 0)
    def _():
        near_top = jnp.zeros(near_mid_ref.shape[1:], jnp.float32)
        for k in range(listed):
            c = top_coupling_ref[0, :, k * rank : (k + 1) * rank]
            prod = jnp.dot(c, row_refs[k][0], precision=exact_mode, preferred_element_type=jnp.float32)
            near_top = near_top + jnp.where(wanted_ref[k] < coarse, prod, 0.0)
        for c in range(near_mid_ref.shape[0]):
            down_mid[c] = near_mid_ref[c] + lax.dot_general(
                mid_transfer_ref[c], near_top, tdims, precision=exact_mode,
                preferred_element_type=jnp.float32)

    rows = lax.broadcasted_iota(jnp.int32, (points, 1), 0)
    for t in range(nb):
        l = i * nb + t
        p = parent_ref[l]
        dm = down_mid[p]
        dl = near_ref[t] + lax.dot_general(transfer_ref[t], dm, tdims, precision=lax.Precision.HIGH, preferred_element_type=jnp.float32)
        far = lax.dot_general(basis_ref[t], dl, tdims, precision=lax.Precision.HIGH, preferred_element_type=jnp.float32)
        out_ref[t * points:(t + 1) * points, :] = jnp.where(rows < size_ref[l], far, 0.0)


def far_field_pallas(near_leaf, leaf_transfer, leaf_basis, near_mid, mid_transfer, top_coupling,
                     shard_rows, wanted, position, leaf_size, leaf_parent, nb=8):
    leaves, rank, points = leaf_basis.shape
    ports = near_leaf.shape[2]
    listed = wanted.shape[0]
    coarse = shard_rows.shape[0]

    def row_spec(k):
        return pl.BlockSpec(
            (1, rank, ports), lambda i, s, p, w, q: (jnp.minimum(w[k], coarse - 1), 0, 0)
        )

    grid_spec = pltpu.PrefetchScalarGridSpec(
        num_scalar_prefetch=4,
        grid=(leaves // nb,),
        in_specs=[pl.BlockSpec((nb, rank, ports), lambda i, *_: (i, 0, 0)),
                  pl.BlockSpec((nb, rank, rank), lambda i, *_: (i, 0, 0)),
                  pl.BlockSpec((nb, rank, points), lambda i, *_: (i, 0, 0)),
                  pl.BlockSpec(near_mid.shape, lambda i, *_: (0, 0, 0)),
                  pl.BlockSpec(mid_transfer.shape, lambda i, *_: (0, 0, 0)),
                  pl.BlockSpec((1,) + top_coupling.shape[1:], lambda i, s, p, w, q: (q[0], 0, 0))]
                 + [row_spec(k) for k in range(listed)],
        out_specs=pl.BlockSpec((nb * points, ports), lambda i, *_: (i, 0)),
        scratch_shapes=[pltpu.VMEM(near_mid.shape, jnp.float32)],
    )
    return pl.pallas_call(
        functools.partial(far_kernel, nb, listed, coarse),
        grid_spec=grid_spec,
        out_shape=jax.ShapeDtypeStruct((leaves * points, ports), jnp.float32),
        compiler_params=pltpu.CompilerParams(vmem_limit_bytes=60 * 1024 * 1024,
                                             dimension_semantics=("arbitrary",)),
        cost_estimate=pl.CostEstimate(flops=2 * leaves * rank * points * ports, bytes_accessed=4 * (leaf_basis.size + 2 * leaves * points * ports), transcendentals=0),
    )(leaf_size, leaf_parent, wanted, position, near_leaf, leaf_transfer, leaf_basis, near_mid,
      mid_transfer, top_coupling, *([shard_rows] * listed))


def couple_rows(pairs_ref, land_ref, coupling_ref, out_ref, listed):
    total = land_ref.shape[0]
    rank = land_ref.shape[1]

    def target(t, carry):
        acc = jnp.zeros(out_ref.shape[1:], jnp.float32)
        for k in range(listed):
            r = pairs_ref[t, k]
            blk = land_ref[jnp.minimum(r, total - 1)]
            c = coupling_ref[t, :, k * rank : (k + 1) * rank]
            prod = jnp.dot(c, blk, precision=lax.Precision.HIGH, preferred_element_type=jnp.float32)
            acc = acc + jnp.where(r < total, prod, 0.0)
        out_ref[t] = acc
        return carry

    lax.fori_loop(0, out_ref.shape[0], target, 0)


def fill_slots(send_ref, coef_ref, pay_ref):
    held = coef_ref.shape[0]

    def fill(i, carry):
        a = send_ref[i]
        pay_ref[i] = jnp.where(a < held, coef_ref[jnp.minimum(a, held - 1)], 0.0)
        return carry

    lax.fori_loop(0, pay_ref.shape[0], fill, 0)


def exchange_couple_kernel(axes, sizes, pair_leaf_ref, pair_mid_ref, send_leaf_ref, send_mid_ref,
                           coef_leaf_ref, coef_mid_ref,
                           leaf_coupling_ref, mid_coupling_ref, near_leaf_ref, near_mid_ref,
                           leaf_pay_ref, mid_pay_ref, leaf_land, mid_land, sems):
    outer, inner = sizes
    count = outer * inner
    me = lax.axis_index(axes[0]) * inner + lax.axis_index(axes[1])
    fill_slots(send_leaf_ref, coef_leaf_ref, leaf_pay_ref)
    fill_slots(send_mid_ref, coef_mid_ref, mid_pay_ref)
    barrier = pltpu.get_barrier_semaphore()

    def greet(q, carry):
        peer = lax.rem(me + q, count)
        pl.semaphore_signal(barrier, 1, device_id=(peer // inner, peer % inner),
                            device_id_type=pl.DeviceIdType.MESH)
        return carry

    lax.fori_loop(1, count, greet, 0)
    pl.semaphore_wait(barrier, count - 1)
    stride = 37 if math.gcd(37, count) == 1 else 1
    slots = leaf_pay_ref.shape[0] // count

    def sender(pay_ref, land_ref, send_sem, recv_sem):
        def send(k, carry):
            peer = lax.rem(me + lax.rem(k * stride, count), count)
            pltpu.make_async_remote_copy(
                src_ref=pay_ref.at[pl.ds(peer * slots, slots)],
                dst_ref=land_ref.at[pl.ds(me * slots, slots)],
                send_sem=send_sem,
                recv_sem=recv_sem,
                device_id=(peer // inner, peer % inner),
                device_id_type=pl.DeviceIdType.MESH,
            ).start()
            return carry

        lax.fori_loop(1, count, send, 0)

    def everything(pay_ref, land_ref, send_sem, recv_sem):
        return pltpu.make_async_remote_copy(
            src_ref=pay_ref.at[pl.ds(0, (count - 1) * slots)],
            dst_ref=land_ref.at[pl.ds(0, (count - 1) * slots)],
            send_sem=send_sem,
            recv_sem=recv_sem,
            device_id=(0, 0),
            device_id_type=pl.DeviceIdType.MESH,
        )

    sender(leaf_pay_ref, leaf_land, sems.at[0], sems.at[1])
    own_leaf = pltpu.make_async_copy(leaf_pay_ref.at[pl.ds(me * slots, slots)],
                                     leaf_land.at[pl.ds(me * slots, slots)], sems.at[4])
    own_leaf.start()
    sender(mid_pay_ref, mid_land, sems.at[2], sems.at[3])
    own_mid = pltpu.make_async_copy(mid_pay_ref.at[pl.ds(me * slots, slots)],
                                    mid_land.at[pl.ds(me * slots, slots)], sems.at[5])
    own_mid.start()

    leaf_all = everything(leaf_pay_ref, leaf_land, sems.at[0], sems.at[1])
    mid_all = everything(mid_pay_ref, mid_land, sems.at[2], sems.at[3])
    own_leaf.wait()
    leaf_all.wait_recv()
    couple_rows(pair_leaf_ref, leaf_land, leaf_coupling_ref, near_leaf_ref, pair_leaf_ref.shape[1])
    own_mid.wait()
    mid_all.wait_recv()
    couple_rows(pair_mid_ref, mid_land, mid_coupling_ref, near_mid_ref, pair_mid_ref.shape[1])
    leaf_all.wait_send()
    mid_all.wait_send()


def exchange_couple(pair_leaf, pair_mid, send_leaf, send_mid, coef_leaf, coef_mid, leaf_coupling,
                    mid_coupling, axes, sizes):
    rank, ports = coef_leaf.shape[1:]
    pay_shape = (send_leaf.shape[0], rank, ports)
    n_leaf = leaf_coupling.shape[0]
    n_mid = mid_coupling.shape[0]
    vmem = pl.BlockSpec(memory_space=pltpu.VMEM)
    smem = pl.BlockSpec(memory_space=pltpu.SMEM)
    hbm = pl.BlockSpec(memory_space=pl.ANY)
    return pl.pallas_call(
        functools.partial(exchange_couple_kernel, axes, sizes),
        out_shape=[jax.ShapeDtypeStruct((n_leaf, rank, ports), jnp.float32),
                   jax.ShapeDtypeStruct((n_mid, rank, ports), jnp.float32)],
        in_specs=[smem, smem, smem, smem, vmem, vmem, vmem, vmem],
        out_specs=[vmem, vmem],
        scratch_shapes=[pltpu.VMEM(pay_shape, jnp.float32), pltpu.VMEM(pay_shape, jnp.float32),
                        pltpu.VMEM(pay_shape, jnp.float32), pltpu.VMEM(pay_shape, jnp.float32),
                        pltpu.SemaphoreType.DMA((6,))],
        compiler_params=pltpu.CompilerParams(collective_id=0, has_side_effects=True,
                                             vmem_limit_bytes=62 * 1024 * 1024),
        cost_estimate=pl.CostEstimate(
            flops=2 * (leaf_coupling.size + mid_coupling.size) * ports,
            bytes_accessed=4 * (coef_leaf.size + coef_mid.size + leaf_coupling.size + mid_coupling.size),
            transcendentals=0),
    )(pair_leaf, pair_mid, send_leaf, send_mid, coef_leaf, coef_mid,
      leaf_coupling, mid_coupling)


def body(
    sizes,
    charges,
    leaf_size,
    leaf_basis,
    leaf_transfer,
    mid_transfer,
    leaf_parent,
    send_leaf,
    pair_leaf,
    leaf_coupling,
    send_mid,
    pair_mid,
    mid_coupling,
    top_pairs,
    top_coupling,
):
    leaf_count, coef_rank, leaf_points = leaf_basis.shape
    port_count = charges.shape[1]
    mid_count = mid_transfer.shape[0]
    owners = send_leaf.shape[0] // 2
    slots = 2
    coef_leaf, coef_mid, coef_top = build_coefs(
        charges, leaf_size, leaf_parent, leaf_basis, leaf_transfer, mid_transfer
    )
    near_leaf, near_mid = exchange_couple(
        pair_leaf, pair_mid, send_leaf, send_mid, coef_leaf, coef_mid, leaf_coupling, mid_coupling,
        ("group", "cluster"), sizes,
    )

    position = lax.axis_index("cluster").astype(jnp.int32).reshape(1)
    wanted = lax.dynamic_slice_in_dim(top_pairs, position[0], 1, 0)[0]
    shard_rows = lax.all_gather(coef_top[None], ("group", "cluster"), axis=0, tiled=True)
    return far_field_pallas(near_leaf, leaf_transfer, leaf_basis, near_mid, mid_transfer, top_coupling,
                            shard_rows, wanted, position, leaf_size, leaf_parent)


def solution(mesh):
    in_specs = (
        P(("group", "cluster"), None),
        P(("group", "cluster")),
        P(("group", "cluster"), None, None),
        P(("group", "cluster"), None, None),
        P(("group", "cluster"), None, None),
        P(("group", "cluster")),
        P(("group", "cluster")),
        P(("group", "cluster"), None),
        P(("group", "cluster"), None, None),
        P(("group", "cluster")),
        P(("group", "cluster"), None),
        P(("group", "cluster"), None, None),
        P("group", None),
        P("group", None, None),
    )
    out_specs = P(("group", "cluster"), None)
    sizes = (mesh.shape["group"], mesh.shape["cluster"])
    return jax.shard_map(functools.partial(body, sizes), mesh=mesh, in_specs=in_specs, out_specs=out_specs, check_vma=False)
```
